128 devices in a mesh: lat: 4 (over z_hi, core), lon: 32 (over y, z_lo, x).
Axes of the slice: x: 4, y: 4, z: 4 (z_hi: 2, z_lo: 2; z = z_hi * 2 + z_lo), core: 2. Of those that a mesh axis runs over, the one named last changes fastest.
Arguments:
- features: bfloat16 [8, 128, 1024, 256], P(None, 'lat', 'lon'), may hold values from -16 to 16
- band_points: int32 [128], replicated, may hold values from 256 to 1024, as said below
- survival_flags: int32 [8, 2], replicated, may hold values 0 or 1
- first_kernel_weight: bfloat16 [3, 3, 256, 256], replicated, may hold values from -0.125 to 0.125
- second_kernel_weight: bfloat16 [3, 3, 256, 256], replicated, may hold values from -0.125 to 0.125
Outputs:
- section_result: bfloat16 [8, 128, 1024, 256], P(None, 'lat', 'lon')
The draws below stay inside these ranges and needn't reach their ends.
Inputs may be any that keep to these rules, and one draw needn't show every extreme that they name: `band_points`: the live points of a row are its first ones.
All inputs are finite; a program needn't handle non-finite values.
Results may differ from the reference program's by a relative error of at most 0.0006.
The reference program's roundings to bfloat16 on the way count: a program that leaves them out, or rounds other values in their place, can miss the bound.
Values may be sent and summed in bfloat16 or wider, within the bound.
No kernel may reach another device: no remote copies, remote signals or barrier semaphores. Data moves between devices by JAX's collectives and lax.ppermute only.
A program may use at most 320 MiB of HBM per device.

```python
import math
import jax
import jax.numpy as jnp
from jax import lax

C = 256
GROUPS = 32
FIRST_DILATION = 2
SECOND_DILATION = 4
B = 8
NLAT = 128
NLON = 1024


def draw_band_points(key, part):
    counts = jax.random.randint(key, (NLAT,), NLON // 4, NLON + 1)
    counts = counts.at[NLAT // 2].set(NLON)
    return counts.at[0].set(NLON // 4).astype(jnp.int32)


def draw_features(key, part):
    keys = jax.random.split(key, 4)
    col_ramp = 0.6 + 1.2 * jnp.arange(NLON, dtype=jnp.float32) / (NLON - 1)
    chan_scale = jnp.exp(jax.random.uniform(keys[1], (C,), minval=math.log(0.3), maxval=math.log(3.0)))
    cell_scale = jnp.exp(jax.random.uniform(keys[2], (B, NLAT, NLON, 1), minval=-0.4, maxval=0.4))
    offset = jax.random.normal(keys[3], (C,)) * 0.5
    noise = jax.random.normal(keys[0], (B, NLAT, NLON, C))
    values = (noise * cell_scale * chan_scale + offset) * col_ramp[:, None]
    return jnp.clip(values, -16.0, 16.0).astype(jnp.bfloat16)


def touch_ends(array, key, low, top_value):
    dims = array.shape
    index_at = [jax.random.randint(jax.random.fold_in(key, axis), (), 0, dims[axis]) for axis in range(len(dims))]
    array = array.at[tuple(index_at)].set(low)
    longest = dims.index(max(dims))
    index_at[longest] = (index_at[longest] + 1) % dims[longest]
    return array.at[tuple(index_at)].set(top_value)


def centred(own_key, extent, scale, bound, kind=jnp.bfloat16):
    array = scale * jax.random.normal(own_key, extent, jnp.float32)
    return jnp.clip(array, min=-bound, max=bound).astype(kind)


def setup_inputs(seed: int = 0) -> dict:
    arg_keys = jax.random.split(jax.random.key(seed), 6)
    return {
        "features": draw_features(jax.random.fold_in(arg_keys[5], 71), 0),
        "band_points": draw_band_points(jax.random.fold_in(arg_keys[5], 71), 0),
        "survival_flags": touch_ends((jax.random.randint(arg_keys[2], (B, 2), 0, 5) < 4).astype(jnp.int32), jax.random.fold_in(arg_keys[2], 1), 0, 1),
        "first_kernel_weight": centred(arg_keys[3], (3, 3, C, C), (9 * C) ** -0.5, 0.125),
        "second_kernel_weight": centred(arg_keys[4], (3, 3, C, C), (9 * C) ** -0.5, 0.125),
    }


EPS = 1e-05
KEEP_RATE = 0.8

def activate(field_in, live_mask, live_count, group_size):
    samples = field_in.shape[0]
    masked = field_in * live_mask[None, :, :, None]
    group_means = lax.optimization_barrier(jnp.sum(masked, axis=(1, 2))).reshape(samples, GROUPS, group_size).sum(axis=2) / live_count
    shifted = field_in - jnp.repeat(group_means, group_size, axis=1)[:, None, None, :]
    squares = shifted * shifted * live_mask[None, :, :, None]
    group_vars = lax.optimization_barrier(jnp.sum(squares, axis=(1, 2))).reshape(samples, GROUPS, group_size).sum(axis=2) / live_count
    inv_std = jnp.repeat(lax.rsqrt(group_vars + EPS), group_size, axis=1)[:, None, None, :]
    return (jax.nn.silu(shifted * inv_std) * live_mask[None, :, :, None]).astype(jnp.bfloat16)

def apply_kernel(acts, weight, dilation):
    lat_total = acts.shape[1]
    lon_total = acts.shape[2]

    def one_sample(plane):
        wrapped = jnp.concatenate([plane[:, lon_total - dilation:], plane, plane[:, :dilation]], axis=1)
        padded = jnp.pad(wrapped, ((dilation, dilation), (0, 0), (0, 0)))
        summed = jnp.zeros((lat_total, lon_total, weight.shape[3]), jnp.float32)
        for row_tap in range(3):
            for col_tap in range(3):
                shifted = padded[row_tap * dilation:row_tap * dilation + lat_total, col_tap * dilation:col_tap * dilation + lon_total]
                summed = summed + jnp.einsum('ijc,cd->ijd', shifted.astype(jnp.float32), weight[row_tap, col_tap].astype(jnp.float32))
        return summed
    return lax.map(one_sample, acts)

def reference(features, band_points, survival_flags, first_kernel_weight, second_kernel_weight):
    lon_total = features.shape[2]
    channels = features.shape[3]
    group_size = channels // GROUPS
    live_mask = (jnp.arange(lon_total, dtype=jnp.int32)[None, :] < band_points[:, None]).astype(jnp.float32)
    live_count = jnp.sum(band_points).astype(jnp.float32) * group_size
    initial_feature_map = features.astype(jnp.float32)
    first_survival = survival_flags[:, 0].astype(jnp.float32) / KEEP_RATE
    second_survival = survival_flags[:, 1].astype(jnp.float32) / KEEP_RATE
    first_hidden = activate(initial_feature_map, live_mask, live_count, group_size)
    first_result = (initial_feature_map + first_survival[:, None, None, None] * apply_kernel(first_hidden, first_kernel_weight, FIRST_DILATION)).astype(jnp.bfloat16)
    first_result = lax.optimization_barrier(first_result)
    first_feature_map = first_result.astype(jnp.float32)
    second_hidden = activate(first_feature_map, live_mask, live_count, group_size)
    section_result = first_feature_map + second_survival[:, None, None, None] * apply_kernel(second_hidden, second_kernel_weight, SECOND_DILATION)
    return section_result.astype(jnp.bfloat16)
```

```python
import functools

import jax
import jax.numpy as jnp
from jax import lax
from jax.experimental import pallas as pl
from jax.experimental.pallas import tpu as pltpu
from jax.sharding import Mesh, PartitionSpec as P

GROUPS = 32
FIRST_DILATION = 2
SECOND_DILATION = 4
EPS = 1e-05
KEEP_RATE = 0.8

LAT = ("zh", "core")
LON = ("y", "zl", "x")
CHIPS = ("zh", "y", "zl", "x")
LANES = 128
VMEM_LIMIT = 56 * 1024 * 1024
HIGHEST = lax.Precision.HIGHEST


def exact_dot(a, b):
    return jnp.dot(a, b, precision=HIGHEST, preferred_element_type=jnp.float32)


def fold_matrix(channels, slot):
    size = channels // GROUPS
    row = lax.broadcasted_iota(jnp.int32, (channels, LANES), 0)
    col = lax.broadcasted_iota(jnp.int32, (channels, LANES), 1)
    low = row - (col - slot * GROUPS) * size
    inside = (col >= slot * GROUPS) & (col < (slot + 1) * GROUPS)
    return jnp.where(inside & (low >= 0) & (low < size), 1.0, 0.0).astype(jnp.float32)


def spread_matrix(channels, slot):
    size = channels // GROUPS
    row = lax.broadcasted_iota(jnp.int32, (LANES, channels), 0)
    col = lax.broadcasted_iota(jnp.int32, (LANES, channels), 1)
    low = col - (row - slot * GROUPS) * size
    inside = (row >= slot * GROUPS) & (row < (slot + 1) * GROUPS)
    return jnp.where(inside & (low >= 0) & (low < size), 1.0, 0.0).astype(jnp.float32)


def store_group_stats(sums_ref, squares_ref, count, out_ref):
    samples, channels = sums_ref.shape
    slots = LANES // GROUPS
    per_channel = jnp.maximum(count, 1.0)
    total = jnp.zeros((samples // slots, LANES), jnp.float32)
    spread = jnp.zeros((samples // slots, LANES), jnp.float32)
    size = channels // GROUPS
    for slot in range(slots):
        pick = [slot + k * slots for k in range(samples // slots)]
        sums = jnp.concatenate([sums_ref[b : b + 1] for b in pick], axis=0)
        squares = jnp.concatenate([squares_ref[b : b + 1] for b in pick], axis=0)
        fold = fold_matrix(channels, slot)
        group_sum = exact_dot(sums, fold)
        centre = exact_dot(group_sum, spread_matrix(channels, slot)) / (per_channel * size)
        offset = sums / per_channel - centre
        total = total + group_sum
        spread = spread + exact_dot(squares + count * offset * offset, fold)
    out_ref[0] = total
    out_ref[1] = spread


def row_statistics(rows, limits, count, sums_ref, squares_ref, b):
    cols, channels = rows(0).shape
    lane = lax.broadcasted_iota(jnp.int32, (cols, channels), 0)
    acc = jnp.zeros((8, channels), jnp.float32)
    for h in range(len(limits)):
        value = jnp.where(lane < limits[h], rows(h), 0.0)
        acc = acc + value.reshape(cols // 8, 8, channels).sum(axis=0)
    sums = acc.sum(axis=0, keepdims=True)
    centre = sums / jnp.maximum(count, 1.0)
    acc = jnp.zeros((8, channels), jnp.float32)
    for h in range(len(limits)):
        value = jnp.where(lane < limits[h], rows(h) - centre, 0.0)
        acc = acc + (value * value).reshape(cols // 8, 8, channels).sum(axis=0)
    sums_ref[pl.ds(b, 1)] = sums
    squares_ref[pl.ds(b, 1)] = acc.sum(axis=0, keepdims=True)


def live_in_tile(points_ref, origin, rows, cols, margin):
    return [jnp.clip(points_ref[margin + h] - origin, 0, cols) for h in range(rows)]


def stats_kernel(points_ref, cols_ref, x_ref, out_ref, sums_ref, squares_ref):
    b = pl.program_id(0)
    _, rows, cols, _ = x_ref.shape
    limits = live_in_tile(points_ref, cols_ref[1], rows, cols, FIRST_DILATION)
    count = functools.reduce(lambda a, c: a + c, limits).astype(jnp.float32)
    row_statistics(
        lambda h: x_ref[0, h].astype(jnp.float32), limits, count, sums_ref, squares_ref, b
    )

    @pl.when(b == pl.num_programs(0) - 1)
    def _():
        store_group_stats(sums_ref, squares_ref, count, out_ref)


def local_statistics(x, points, cols):
    samples, rows, width, channels = x.shape
    return pl.pallas_call(
        stats_kernel,
        out_shape=jax.ShapeDtypeStruct((2, samples * GROUPS // LANES, LANES), jnp.float32),
        grid_spec=pltpu.PrefetchScalarGridSpec(
            num_scalar_prefetch=2,
            grid=(samples,),
            in_specs=[pl.BlockSpec((1, rows, width, channels), lambda b, *_: (b, 0, 0, 0))],
            out_specs=pl.BlockSpec(
                (2, samples * GROUPS // LANES, LANES), lambda b, *_: (0, 0, 0)
            ),
            scratch_shapes=[
                pltpu.VMEM((samples, channels), jnp.float32),
                pltpu.VMEM((samples, channels), jnp.float32),
            ],
        ),
        compiler_params=pltpu.CompilerParams(
            dimension_semantics=("arbitrary",), vmem_limit_bytes=VMEM_LIMIT
        ),
        cost_estimate=pl.CostEstimate(
            flops=8 * x.size, bytes_accessed=2 * x.size, transcendentals=0
        ),
        name="stats",
    )(points, cols, x)


def combine_statistics(parts_ref, counts_ref, norm_ref, samples, channels):
    slots = LANES // GROUPS
    counts = counts_ref[...][:, None, :]
    sums = parts_ref[:, 0]
    squares = parts_ref[:, 1]
    count = counts.sum(axis=0)
    mean = sums.sum(axis=0) / count
    offset = sums / jnp.maximum(counts, 1.0) - mean[None]
    var = (squares + counts * offset * offset).sum(axis=0) / count
    half = 0.5 * lax.rsqrt(var + EPS)
    for slot in range(slots):
        spread = spread_matrix(channels, slot)
        means = exact_dot(mean, spread)
        halves = exact_dot(half, spread)
        for k in range(samples // slots):
            norm_ref[slot + k * slots, 0:1] = means[k : k + 1]
            norm_ref[slot + k * slots, 1:2] = halves[k : k + 1]


def conv_kernel(
    dilation, chunk, with_stats, points_ref, cols_ref, scale_ref, parts_ref, counts_ref, x_ref, top_ref, bottom_ref,
    left_ref, right_ref, w_ref, out_ref, *rest
):
    if with_stats:
        stats_ref, norm_ref, act_ref, sums_ref, squares_ref = rest
    else:
        norm_ref, act_ref = rest
    b = pl.program_id(0)
    d = dilation
    _, rows, cols, channels = x_ref.shape

    @pl.when(b == 0)
    def _():
        combine_statistics(parts_ref, counts_ref, norm_ref, pl.num_programs(0), channels)

    mean = norm_ref[b, 0:1]
    half = norm_ref[b, 1:2]

    def activated(value):
        t = (value.astype(jnp.float32) - mean) * half
        return t + t * jnp.tanh(t)

    column = lax.broadcasted_iota(jnp.int32, (cols, channels), 0)
    edge = lax.broadcasted_iota(jnp.int32, (d, channels), 0)
    left = activated(left_ref[0])
    right = activated(right_ref[0])
    for e in range(rows + 2 * d):
        if e < d:
            source = top_ref[0, e]
        elif e < rows + d:
            source = x_ref[0, e - d]
        else:
            source = bottom_ref[0, e - rows - d]
        points = points_ref[e]
        mid = jnp.where(column < points - cols_ref[1], activated(source), 0.0)
        lhs = jnp.where(edge < points - cols_ref[0], left[e * d : (e + 1) * d], 0.0)
        rhs = jnp.where(edge < points - cols_ref[2], right[e * d : (e + 1) * d], 0.0)
        before = jnp.concatenate([lhs, mid[: cols - d]], axis=0)
        after = jnp.concatenate([mid[d:], rhs], axis=0)
        act_ref[e, :, 0:channels] = before.astype(jnp.bfloat16)
        act_ref[e, :, channels : 2 * channels] = mid.astype(jnp.bfloat16)
        act_ref[e, :, 2 * channels :] = after.astype(jnp.bfloat16)

    scale = scale_ref[b]
    for start in range(0, rows, chunk):
        acc = None
        for tap in range(3):
            lo = start + tap * d
            taken = act_ref[lo : lo + chunk].reshape(chunk * cols, 3 * channels)
            term = jnp.dot(taken, w_ref[tap], preferred_element_type=jnp.float32)
            acc = term if acc is None else acc + term
        base = x_ref[0, start : start + chunk].astype(jnp.float32)
        result = base + scale * acc.reshape(chunk, cols, channels)
        out_ref[0, start : start + chunk] = result.astype(jnp.bfloat16)

    if with_stats:
        limits = live_in_tile(points_ref, cols_ref[1], rows, cols, d)
        count = functools.reduce(lambda a, c: a + c, limits).astype(jnp.float32)
        row_statistics(
            lambda h: out_ref[0, h].astype(jnp.float32), limits, count, sums_ref, squares_ref, b
        )

        @pl.when(b == pl.num_programs(0) - 1)
        def _():
            store_group_stats(sums_ref, squares_ref, count, stats_ref)


def convolve(x, halos, weight, parts, counts, points, cols, scale, dilation, with_stats):
    samples, rows, width, channels = x.shape
    d = dilation
    top, bottom, left, right = halos
    out_shape = [jax.ShapeDtypeStruct(x.shape, jnp.bfloat16)]
    out_specs = [pl.BlockSpec((1, rows, width, channels), lambda b, *_: (b, 0, 0, 0))]
    scratch = [
        pltpu.VMEM((samples, 2, channels), jnp.float32),
        pltpu.VMEM((rows + 2 * d, width, 3 * channels), jnp.bfloat16),
    ]
    if with_stats:
        shape = (2, samples * GROUPS // LANES, LANES)
        out_shape.append(jax.ShapeDtypeStruct(shape, jnp.float32))
        out_specs.append(pl.BlockSpec(shape, lambda b, *_: (0, 0, 0)))
        scratch += [pltpu.VMEM((samples, channels), jnp.float32)] * 2
    edge = (rows + 2 * d) * d
    return pl.pallas_call(
        functools.partial(conv_kernel, d, 8, with_stats),
        out_shape=out_shape,
        grid_spec=pltpu.PrefetchScalarGridSpec(
            num_scalar_prefetch=3,
            grid=(samples,),
            in_specs=[
                pl.BlockSpec(parts.shape, lambda b, *_: (0, 0, 0, 0)),
                pl.BlockSpec(counts.shape, lambda b, *_: (0, 0)),
                pl.BlockSpec((1, rows, width, channels), lambda b, *_: (b, 0, 0, 0)),
                pl.BlockSpec((1, d, width, channels), lambda b, *_: (b, 0, 0, 0)),
                pl.BlockSpec((1, d, width, channels), lambda b, *_: (b, 0, 0, 0)),
                pl.BlockSpec((1, edge, channels), lambda b, *_: (b, 0, 0)),
                pl.BlockSpec((1, edge, channels), lambda b, *_: (b, 0, 0)),
                pl.BlockSpec(weight.shape, lambda b, *_: (0, 0, 0)),
            ],
            out_specs=out_specs,
            scratch_shapes=scratch,
        ),
        compiler_params=pltpu.CompilerParams(
            dimension_semantics=("arbitrary",), vmem_limit_bytes=VMEM_LIMIT
        ),
        cost_estimate=pl.CostEstimate(
            flops=2 * x.size * 9 * channels, bytes_accessed=5 * x.size, transcendentals=2 * x.size
        ),
        name="conv%d" % d,
    )(points, cols, scale, parts, counts, x, top, bottom, left, right, weight)


def exchange(x, d):
    samples, rows, width, channels = x.shape
    lat, lon = lax.axis_size(LAT), lax.axis_size(LON)
    up = [(i, i + 1) for i in range(lat - 1)]
    down = [(i + 1, i) for i in range(lat - 1)]
    top = lax.ppermute(x[:, rows - d :], LAT, up)
    bottom = lax.ppermute(x[:, :d], LAT, down)
    east = [(i, (i + 1) % lon) for i in range(lon)]
    west = [((i + 1) % lon, i) for i in range(lon)]

    def packed(lo, hi):
        strip = jnp.concatenate([top[:, :, lo:hi], x[:, :, lo:hi], bottom[:, :, lo:hi]], axis=1)
        return strip.reshape(samples, (rows + 2 * d) * d, channels)

    left = lax.ppermute(packed(width - d, width), LON, east)
    right = lax.ppermute(packed(0, d), LON, west)
    return top, bottom, left, right


def share_statistics(local, own_count, other_count, core_axis="core"):
    other = lax.ppermute(local, core_axis, [(0, 1), (1, 0)])
    both = own_count + other_count
    gap = local[0] / jnp.maximum(own_count, 1.0) - other[0] / jnp.maximum(other_count, 1.0)
    squares = local[1] + other[1] + gap * gap * (own_count * other_count / jnp.maximum(both, 1.0))
    merged = jnp.stack([local[0] + other[0], squares])
    chips = lax.axis_size(CHIPS)
    return lax.all_to_all(jnp.broadcast_to(merged[None], (chips, *merged.shape)), CHIPS, 0, 0)


def per_device(features, band_points, survival_flags, first_kernel_weight, second_kernel_weight):
    _, rows, width, channels = features.shape
    lat_total = band_points.shape[0]
    lat, lon = lax.axis_size(LAT), lax.axis_size(LON)
    i, j = lax.axis_index(LAT), lax.axis_index(LON)
    lon_total = lon * width
    origin = j * width

    def placed(d):
        padded = jnp.pad(band_points, (d, d))
        points = lax.dynamic_slice(padded, (i * rows,), (rows + 2 * d,))
        cols = jnp.stack([(origin - d) % lon_total, origin, (origin + width) % lon_total])
        return points, cols.astype(jnp.int32)

    group_size = channels // GROUPS
    starts = jnp.arange(lon, dtype=jnp.int32) * width
    inside = jnp.clip(band_points[:, None] - starts[None, :], 0, width)
    tile_counts = inside.reshape(lat, rows, lon).sum(axis=1) * group_size
    tile_counts = tile_counts.astype(jnp.float32)
    core_counts = tile_counts.reshape(lax.axis_size("zh"), lax.axis_size("core"), lon)
    chip_counts = core_counts.sum(axis=1).reshape(-1, 1)
    counts = jnp.broadcast_to(chip_counts, (chip_counts.shape[0], LANES))
    own_count = tile_counts[i, j]
    both_count = core_counts.sum(axis=1)[lax.axis_index("zh"), j]
    other_count = both_count - own_count
    scales = survival_flags.astype(jnp.float32) / KEEP_RATE

    points, cols = placed(FIRST_DILATION)
    local = local_statistics(features, points, cols)
    halos = exchange(features, FIRST_DILATION)
    parts = share_statistics(local, own_count, other_count)
    weight = first_kernel_weight.reshape(3, 3 * channels, channels)
    first, local = convolve(
        features, halos, weight, parts, counts, points, cols, scales[:, 0], FIRST_DILATION, True
    )

    points, cols = placed(SECOND_DILATION)
    halos = exchange(first, SECOND_DILATION)
    parts = share_statistics(local, own_count, other_count)
    weight = second_kernel_weight.reshape(3, 3 * channels, channels)
    (section,) = convolve(
        first, halos, weight, parts, counts, points, cols, scales[:, 1], SECOND_DILATION, False
    )
    return section


def solution(mesh):
    grid = Mesh(mesh.devices.reshape(2, 2, 4, 2, 4), (LAT + LON))
    spec = P(None, LAT, LON, None)
    return jax.shard_map(
        per_device, mesh=grid, in_specs=(spec, P(), P(), P(), P()), out_specs=spec, check_vma=False
    )
```

```python
import functools

import jax
import jax.numpy as jnp
from jax import lax
from jax.experimental import pallas as pl
from jax.experimental.pallas import tpu as pltpu
from jax.sharding import Mesh, PartitionSpec as P

GROUPS = 32
FIRST_DILATION = 2
SECOND_DILATION = 4
EPS = 1e-05
KEEP_RATE = 0.8

LAT = ("zh", "core")
LON = ("y", "zl", "x")
CHIPS = ("zh", "y", "zl", "x")
LANES = 128
VMEM_LIMIT = 59_300_000
CHUNK = 8


def exact_dot(a, selection):
    high = a.astype(jnp.bfloat16)
    rest = a - high.astype(jnp.float32)
    middle = rest.astype(jnp.bfloat16)
    low = (rest - middle.astype(jnp.float32)).astype(jnp.bfloat16)
    m = a.shape[0]
    parts = jnp.concatenate([high.astype(jnp.float32), middle.astype(jnp.float32), low.astype(jnp.float32)], axis=0)
    terms = jnp.dot(parts.astype(jnp.bfloat16), selection, preferred_element_type=jnp.float32)
    return terms[:m] + terms[m : 2 * m] + terms[2 * m :]


def selection_matrix(shape, channel_dim, channels):
    size = channels // GROUPS
    channel = lax.broadcasted_iota(jnp.int32, shape, channel_dim)
    lane = lax.broadcasted_iota(jnp.int32, shape, 1 - channel_dim)
    return jnp.where(channel // size == lane % GROUPS, 1.0, 0.0).astype(jnp.bfloat16)


def slot_lanes(samples):
    row = lax.broadcasted_iota(jnp.int32, (samples, LANES), 0)
    lane = lax.broadcasted_iota(jnp.int32, (samples, LANES), 1)
    return lane // GROUPS == row % (LANES // GROUPS)


def store_group_stats(sums_ref, squares_ref, count, out_ref):
    samples, channels = sums_ref.shape
    slots = LANES // GROUPS
    size = channels // GROUPS
    own = slot_lanes(samples)
    fold = selection_matrix((channels, LANES), 0, channels)
    spread = selection_matrix((LANES, channels), 1, channels)
    per_channel = jnp.maximum(count, 1.0)
    sums = sums_ref[...]

    def packed(value):
        return jnp.where(own, value, 0.0).reshape(samples // slots, slots, LANES).sum(axis=1)

    group_sum = exact_dot(sums, fold)
    centre = exact_dot(jnp.where(own, group_sum, 0.0), spread) / (per_channel * size)
    offset = sums / per_channel - centre
    group_squares = exact_dot(squares_ref[...] + count * offset * offset, fold)
    out_ref[0] = packed(group_sum)
    out_ref[1] = packed(group_squares)


def row_statistics(rows, limits, count, sums_ref, squares_ref, b):
    some = 16
    cols, channels = rows(0, None).shape
    column = lax.broadcasted_iota(jnp.int32, (cols, channels), 0)
    few = sum(jnp.minimum(limit, some) for limit in limits).astype(jnp.float32)
    total = jnp.zeros((some, channels), jnp.float32)
    for h in range(len(limits)):
        total = total + jnp.where(column[:some] < limits[h], rows(h, some), 0.0)
    pivot = total.sum(axis=0, keepdims=True) / jnp.maximum(few, 1.0)
    first = jnp.zeros((cols, channels), jnp.float32)
    second = jnp.zeros((cols, channels), jnp.float32)
    for h in range(len(limits)):
        value = jnp.where(column < limits[h], rows(h, None) - pivot, 0.0)
        first = first + value
        second = second + value * value
    moved = first.sum(axis=0, keepdims=True)
    squares = second.sum(axis=0, keepdims=True) - moved * moved / jnp.maximum(count, 1.0)
    sums_ref[pl.ds(b, 1)] = moved + count * pivot
    squares_ref[pl.ds(b, 1)] = jnp.maximum(squares, 0.0)


def tile_position():
    lat = lax.axis_index("zh") * lax.axis_size("core") + lax.axis_index("core")
    lon = (lax.axis_index("y") * lax.axis_size("zl") + lax.axis_index("zl")) * lax.axis_size("x")
    return lat, lon + lax.axis_index("x")


def row_points(points_ref, lat, rows, e):
    row = lat * rows + e
    if 0 <= e < rows:
        return points_ref[row]
    total = points_ref.shape[0]
    inside = (row >= 0) & (row < total)
    return jnp.where(inside, points_ref[jnp.clip(row, 0, total - 1)], 0)


def live_limits(points_ref, rows, cols):
    lat, lon = tile_position()
    return [jnp.clip(points_ref[lat * rows + h] - lon * cols, 0, cols) for h in range(rows)]


def live_count(limits):
    return functools.reduce(lambda a, c: a + c, limits).astype(jnp.float32)


def in_vmem():
    return pl.BlockSpec(memory_space=pltpu.VMEM)


def fetch(x_hbm_ref, x_ref, sems, b):
    return pltpu.make_async_copy(x_hbm_ref.at[b], x_ref.at[b], sems.at[b])


def stats_kernel(points_ref, x_hbm_ref, out_ref, x_ref, sems, sums_ref, squares_ref):
    g = pl.program_id(0)

    @pl.when(g == 0)
    def _():
        for b in range(x_ref.shape[0]):
            fetch(x_hbm_ref, x_ref, sems, b).start()

    fetch(x_hbm_ref, x_ref, sems, g).wait()
    _, rows, cols, _ = x_ref.shape
    limits = live_limits(points_ref, rows, cols)
    count = live_count(limits)
    row_statistics(
        lambda h, n: x_ref[g, h, :n].astype(jnp.float32), limits, count, sums_ref, squares_ref, g
    )

    @pl.when(g == pl.num_programs(0) - 1)
    def _():
        store_group_stats(sums_ref, squares_ref, count, out_ref)


def local_statistics(x, points):
    samples, rows, width, channels = x.shape
    shape = (2, samples * GROUPS // LANES, LANES)
    return pl.pallas_call(
        stats_kernel,
        out_shape=jax.ShapeDtypeStruct(shape, jnp.float32),
        grid_spec=pltpu.PrefetchScalarGridSpec(
            num_scalar_prefetch=1,
            grid=(samples,),
            in_specs=[pl.BlockSpec(memory_space=pltpu.HBM)],
            out_specs=pl.BlockSpec(shape, lambda g, *_: (0, 0, 0)),
            scratch_shapes=[
                pltpu.VMEM(x.shape, x.dtype),
                pltpu.SemaphoreType.DMA((samples,)),
                pltpu.VMEM((samples, channels), jnp.float32),
                pltpu.VMEM((samples, channels), jnp.float32),
            ],
        ),
        compiler_params=pltpu.CompilerParams(
            dimension_semantics=("arbitrary",), vmem_limit_bytes=VMEM_LIMIT
        ),
        cost_estimate=pl.CostEstimate(
            flops=8 * x.size, bytes_accessed=2 * x.size, transcendentals=0
        ),
        name="stats",
    )(points, x)


def chip_counts(points, chips, rows, cols, size):
    total = points.shape[1]
    lons = chips // lax.axis_size("zh")
    chip = lax.broadcasted_iota(jnp.int32, (chips, total), 0)
    row = lax.broadcasted_iota(jnp.int32, (chips, total), 1)
    live = jnp.clip(points - (chip % lons) * cols, 0, cols)
    mine = row // (rows * lax.axis_size("core")) == chip // lons
    return jnp.where(mine, live, 0).astype(jnp.float32).sum(axis=1, keepdims=True) * size


def combine_statistics(parts_ref, points_ref, norm_ref, rows, cols):
    _, samples, channels = norm_ref.shape
    slots = LANES // GROUPS
    chips = parts_ref.shape[0]
    counts = chip_counts(points_ref[...], chips, rows, cols, channels // GROUPS)[:, None, :]
    sums = parts_ref[:, 0]
    squares = parts_ref[:, 1]
    count = counts.sum(axis=0)
    mean = sums.sum(axis=0) / count
    offset = sums / jnp.maximum(counts, 1.0) - mean[None]
    var = (squares + counts * offset * offset).sum(axis=0) / count
    half = 0.5 * lax.rsqrt(var + EPS)
    own = slot_lanes(samples)
    spread = selection_matrix((LANES, channels), 1, channels)

    def unpacked(value):
        rows = jnp.broadcast_to(value[:, None], (samples // slots, slots, LANES)).reshape(samples, LANES)
        return jnp.where(own, rows, 0.0)

    both = exact_dot(jnp.concatenate([unpacked(mean), unpacked(half)], axis=0), spread)
    norm_ref[0] = both[:samples]
    norm_ref[1] = both[samples:]


def conv_kernel(dilation, chunk, which, with_stats, points_ref, flags_ref, parts_ref, points_row_ref, *refs):
    d = dilation
    x_hbm_ref, top_ref, bottom_ref, left_ref, right_ref, left_end_ref, right_end_ref, w_ref, out_hbm_ref, *rest = refs
    if with_stats:
        stats_ref, x_ref, sems, out_ref, out_sems, norm_ref, even_ref, odd_ref, sums_ref, squares_ref, kept_ref = rest
    else:
        x_ref, sems, out_ref, out_sems, norm_ref, even_ref, odd_ref = rest
    g = pl.program_id(0)
    samples = norm_ref.shape[1]
    _, rows, cols, channels = x_ref.shape
    lat, lon = tile_position()
    lon_total = lax.axis_size(LON) * cols
    origin = lon * cols
    column = lax.broadcasted_iota(jnp.int32, (cols, channels), 0)
    edge = lax.broadcasted_iota(jnp.int32, (d, channels), 0)
    points = [row_points(points_ref, lat, rows, e - d) for e in range(rows + 2 * d)]
    limits = [jnp.clip(points[d + h] - origin, 0, cols) for h in range(rows)]
    before_origin = (origin + lon_total - d) % lon_total
    after_origin = (origin + cols) % lon_total

    def activate_rows(b, act_ref, lo, hi):
        mean = norm_ref[0, pl.ds(b, 1)]
        half = norm_ref[1, pl.ds(b, 1)]

        def activated(value):
            t = (value.astype(jnp.float32) - mean) * half
            return t + t * jnp.tanh(t)

        for e in range(lo, hi):
            if e < d:
                row, side = top_ref[b, e], (left_end_ref, right_end_ref, e)
            elif e < rows + d:
                row, side = x_ref[b, e - d], (left_ref, right_ref, e - d)
            else:
                row, side = bottom_ref[b, e - rows - d], (left_end_ref, right_end_ref, e - rows)
            at = slice(side[2] * d, (side[2] + 1) * d)
            left = activated(side[0][b, at])
            right = activated(side[1][b, at])
            mid = jnp.where(column < points[e] - origin, activated(row), 0.0)
            lhs = jnp.where(edge < points[e] - before_origin, left, 0.0)
            rhs = jnp.where(edge < points[e] - after_origin, right, 0.0)
            before = jnp.concatenate([lhs, mid[: cols - d]], axis=0)
            after = jnp.concatenate([mid[d:], rhs], axis=0)
            act_ref[e, :, 0:channels] = before.astype(jnp.bfloat16)
            act_ref[e, :, channels : 2 * channels] = mid.astype(jnp.bfloat16)
            act_ref[e, :, 2 * channels :] = after.astype(jnp.bfloat16)

    def convolve_rows(k, scale, act_ref, start):
        acc = None
        for tap in range(3):
            lo = start + tap * d
            taken = act_ref[lo : lo + chunk].reshape(chunk * cols, 3 * channels)
            term = jnp.dot(taken, w_ref[tap], preferred_element_type=jnp.float32)
            acc = term if acc is None else acc + term
        base = x_ref[2 * g + k, start : start + chunk].astype(jnp.float32)
        result = (base + scale * acc.reshape(chunk, cols, channels)).astype(jnp.bfloat16)
        out_ref[2 * g + k, start : start + chunk] = result
        if with_stats and k == 1:
            kept_ref[start : start + chunk] = result

    def phase(k, act_ref, follow, next_ref):
        scale = flags_ref[2 * g + k, which].astype(jnp.float32) * (1.0 / KEEP_RATE)
        steps = rows // chunk
        each = (rows + 2 * d) // steps
        for step in range(steps):
            last = rows + 2 * d if step == steps - 1 else (step + 1) * each
            activate_rows(follow, next_ref, step * each, last)
            convolve_rows(k, scale, act_ref, step * chunk)
        store(2 * g + k).start()

    def store(b):
        return pltpu.make_async_copy(out_ref.at[b], out_hbm_ref.at[b], out_sems.at[b])

    @pl.when(g == 0)
    def _():
        for b in range(samples):
            fetch(x_hbm_ref, x_ref, sems, b).start()
        combine_statistics(parts_ref, points_row_ref, norm_ref, rows, cols)
        fetch(x_hbm_ref, x_ref, sems, 0).wait()
        activate_rows(0, even_ref, 0, rows + 2 * d)
        if with_stats:
            kept_ref[...] = jnp.zeros_like(kept_ref)

    @pl.when(g < samples // 2 - 1)
    def _():
        fetch(x_hbm_ref, x_ref, sems, 2 * g + 2).wait()

    fetch(x_hbm_ref, x_ref, sems, 2 * g + 1).wait()
    count = live_count(limits)
    phase(0, even_ref, 2 * g + 1, odd_ref)
    if with_stats:
        row_statistics(
            lambda h, n: kept_ref[h, :n].astype(jnp.float32), limits, count, sums_ref, squares_ref, jnp.maximum(2 * g - 1, 0)
        )
    phase(1, odd_ref, jnp.minimum(2 * g + 2, samples - 1), even_ref)
    if with_stats:
        row_statistics(
            lambda h, n: out_ref[2 * g, h, :n].astype(jnp.float32), limits, count, sums_ref, squares_ref, 2 * g
        )

        @pl.when(g == pl.num_programs(0) - 1)
        def _():
            row_statistics(
                lambda h, n: out_ref[2 * g + 1, h, :n].astype(jnp.float32), limits, count, sums_ref, squares_ref, samples - 1
            )
            store_group_stats(sums_ref, squares_ref, count, stats_ref)

    @pl.when(g == pl.num_programs(0) - 1)
    def _():
        for b in range(samples):
            store(b).wait()


def convolve(x, halos, weight, parts, points, flags, dilation, which, with_stats):
    samples, rows, width, channels = x.shape
    d = dilation
    def whole(shape):
        return pl.BlockSpec(shape, lambda g, *_: (0,) * len(shape))

    out_shape = [jax.ShapeDtypeStruct(x.shape, jnp.bfloat16)]
    out_specs = [pl.BlockSpec(memory_space=pltpu.HBM)]
    act = pltpu.VMEM((rows + 2 * d, width, 3 * channels), jnp.bfloat16)
    scratch = [pltpu.VMEM(x.shape, x.dtype), pltpu.SemaphoreType.DMA((samples,))] * 2
    scratch += [pltpu.VMEM((2, samples, channels), jnp.float32), act, act]
    if with_stats:
        shape = (2, samples * GROUPS // LANES, LANES)
        out_shape.append(jax.ShapeDtypeStruct(shape, jnp.float32))
        out_specs.append(whole(shape))
        scratch += [pltpu.VMEM((samples, channels), jnp.float32)] * 2
        scratch += [pltpu.VMEM((rows, width, channels), jnp.bfloat16)]
    return pl.pallas_call(
        functools.partial(conv_kernel, d, CHUNK, which, with_stats),
        out_shape=out_shape,
        grid_spec=pltpu.PrefetchScalarGridSpec(
            num_scalar_prefetch=2,
            grid=(samples // 2,),
            in_specs=[
                in_vmem(),
                in_vmem(),
                pl.BlockSpec(memory_space=pltpu.HBM),
                *[in_vmem()] * len(halos),
                in_vmem(),
            ],
            out_specs=out_specs,
            scratch_shapes=scratch,
        ),
        compiler_params=pltpu.CompilerParams(
            dimension_semantics=("arbitrary",), vmem_limit_bytes=VMEM_LIMIT
        ),
        cost_estimate=pl.CostEstimate(
            flops=2 * x.size * 9 * channels, bytes_accessed=5 * x.size, transcendentals=2 * x.size
        ),
        name="conv%d" % d,
    )(points, flags, parts, points[None], x, *halos, weight)


def exchange_sides(x, d):
    samples, rows, width, channels = x.shape
    lat, lon = lax.axis_size(LAT), lax.axis_size(LON)
    up = [(i, i + 1) for i in range(lat - 1)]
    down = [(i + 1, i) for i in range(lat - 1)]
    top = lax.ppermute(x[:, rows - d :], LAT, up)
    bottom = lax.ppermute(x[:, :d], LAT, down)
    east = [(i, (i + 1) % lon) for i in range(lon)]
    west = [((i + 1) % lon, i) for i in range(lon)]
    left = lax.ppermute(x[:, :, width - d :].reshape(samples, rows * d, channels), LON, east)
    right = lax.ppermute(x[:, :, :d].reshape(samples, rows * d, channels), LON, west)
    return top, bottom, left, right


def exchange_corners(top, bottom):
    samples, d, width, channels = top.shape
    lon = lax.axis_size(LON)
    east = [(i, (i + 1) % lon) for i in range(lon)]
    west = [((i + 1) % lon, i) for i in range(lon)]

    def packed(lo, hi):
        ends = jnp.concatenate([top[:, :, lo:hi], bottom[:, :, lo:hi]], axis=1)
        return ends.reshape(samples, 2 * d * d, channels)

    left = lax.ppermute(packed(width - d, width), LON, east)
    right = lax.ppermute(packed(0, d), LON, west)
    return left, right


def share_statistics(local, own_count, other_count, core_axis="core"):
    other = lax.ppermute(local, core_axis, [(0, 1), (1, 0)])
    both = own_count + other_count
    gap = local[0] / jnp.maximum(own_count, 1.0) - other[0] / jnp.maximum(other_count, 1.0)
    squares = local[1] + other[1] + gap * gap * (own_count * other_count / jnp.maximum(both, 1.0))
    merged = jnp.stack([local[0] + other[0], squares])
    chips = lax.axis_size(CHIPS)
    return lax.all_to_all(jnp.broadcast_to(merged[None], (chips, *merged.shape)), CHIPS, 0, 0)


def tile_count(band_points, rows, width, size, core):
    _, lon = tile_position()
    lat = lax.axis_index("zh") * lax.axis_size("core") + core
    row = jnp.arange(band_points.shape[0], dtype=jnp.int32)
    live = jnp.clip(band_points - lon * width, 0, width)
    return jnp.where(row // rows == lat, live, 0).sum().astype(jnp.float32) * size


def per_device(features, band_points, survival_flags, first_kernel_weight, second_kernel_weight):
    _, rows, width, channels = features.shape
    core = lax.axis_index("core")
    size = channels // GROUPS
    own_count = tile_count(band_points, rows, width, size, core)
    other_count = tile_count(band_points, rows, width, size, 1 - core)
    first_weight = first_kernel_weight.reshape(3, 3 * channels, channels)
    second_weight = second_kernel_weight.reshape(3, 3 * channels, channels)

    top, bottom, left, right = exchange_sides(features, FIRST_DILATION)
    local = local_statistics(features, band_points)
    local, top, bottom = lax.optimization_barrier((local, top, bottom))
    ends = exchange_corners(top, bottom)
    parts = share_statistics(local, own_count, other_count)
    halos = (top, bottom, left, right, *ends)
    first, local = convolve(
        features, halos, first_weight, parts, band_points, survival_flags, FIRST_DILATION, 0, True
    )
    top, bottom, left, right = exchange_sides(first, SECOND_DILATION)
    parts = share_statistics(local, own_count, other_count)
    ends = exchange_corners(top, bottom)
    halos = (top, bottom, left, right, *ends)
    (section,) = convolve(
        first, halos, second_weight, parts, band_points, survival_flags, SECOND_DILATION, 1, False
    )
    return section


def solution(mesh):
    grid = Mesh(mesh.devices.reshape(2, 2, 4, 2, 4), (LAT + LON))
    spec = P(None, LAT, LON, None)
    return jax.shard_map(
        per_device, mesh=grid, in_specs=(spec, P(), P(), P(), P()), out_specs=spec, check_vma=False
    )
```

```python
import functools

import jax
import jax.numpy as jnp
from jax import lax
from jax.experimental import pallas as pl
from jax.experimental.pallas import tpu as pltpu
from jax.sharding import Mesh, PartitionSpec as P

GROUPS = 32
FIRST_DILATION = 2
SECOND_DILATION = 4
EPS = 1e-05
KEEP_RATE = 0.8

LAT = ("zh", "core")
LON = ("y", "zl", "x")
CHIPS = ("zh", "y", "zl", "x")
LANES = 128
VMEM_LIMIT = 59_300_000
CHUNK = 8


def exact_dot(a, selection):
    high = a.astype(jnp.bfloat16)
    rest = a - high.astype(jnp.float32)
    middle = rest.astype(jnp.bfloat16)
    low = (rest - middle.astype(jnp.float32)).astype(jnp.bfloat16)
    m = a.shape[0]
    parts = jnp.concatenate([high.astype(jnp.float32), middle.astype(jnp.float32), low.astype(jnp.float32)], axis=0)
    terms = jnp.dot(parts.astype(jnp.bfloat16), selection, preferred_element_type=jnp.float32)
    return terms[:m] + terms[m : 2 * m] + terms[2 * m :]


def selection_matrix(shape, channel_dim, channels):
    size = channels // GROUPS
    channel = lax.broadcasted_iota(jnp.int32, shape, channel_dim)
    lane = lax.broadcasted_iota(jnp.int32, shape, 1 - channel_dim)
    return jnp.where(channel // size == lane % GROUPS, 1.0, 0.0).astype(jnp.bfloat16)


def slot_lanes(samples):
    row = lax.broadcasted_iota(jnp.int32, (samples, LANES), 0)
    lane = lax.broadcasted_iota(jnp.int32, (samples, LANES), 1)
    return lane // GROUPS == row % (LANES // GROUPS)


def store_group_stats(sums_ref, squares_ref, count, out_ref):
    samples, channels = sums_ref.shape
    slots = LANES // GROUPS
    size = channels // GROUPS
    own = slot_lanes(samples)
    fold = selection_matrix((channels, LANES), 0, channels)
    spread = selection_matrix((LANES, channels), 1, channels)
    per_channel = jnp.maximum(count, 1.0)
    sums = sums_ref[...]

    def packed(value):
        return jnp.where(own, value, 0.0).reshape(samples // slots, slots, LANES).sum(axis=1)

    group_sum = exact_dot(sums, fold)
    centre = exact_dot(jnp.where(own, group_sum, 0.0), spread) / (per_channel * size)
    offset = sums / per_channel - centre
    group_squares = exact_dot(squares_ref[...] + count * offset * offset, fold)
    out_ref[0] = packed(group_sum)
    out_ref[1] = packed(group_squares)
    out_ref[2] = jnp.full(out_ref.shape[1:], count * size, jnp.float32)


def row_statistics(rows, limits, count, sums_ref, squares_ref, b):
    some = 16
    cols, channels = rows(0, None).shape
    column = lax.broadcasted_iota(jnp.int32, (cols, channels), 0)
    few = sum(jnp.minimum(limit, some) for limit in limits).astype(jnp.float32)
    total = jnp.zeros((some, channels), jnp.float32)
    for h in range(len(limits)):
        total = total + jnp.where(column[:some] < limits[h], rows(h, some), 0.0)
    pivot = total.sum(axis=0, keepdims=True) / jnp.maximum(few, 1.0)
    first = jnp.zeros((cols, channels), jnp.float32)
    second = jnp.zeros((cols, channels), jnp.float32)
    for h in range(len(limits)):
        value = jnp.where(column < limits[h], rows(h, None) - pivot, 0.0)
        first = first + value
        second = second + value * value
    moved = first.sum(axis=0, keepdims=True)
    squares = second.sum(axis=0, keepdims=True) - moved * moved / jnp.maximum(count, 1.0)
    sums_ref[pl.ds(b, 1)] = moved + count * pivot
    squares_ref[pl.ds(b, 1)] = jnp.maximum(squares, 0.0)


def tile_position():
    lat = lax.axis_index("zh") * lax.axis_size("core") + lax.axis_index("core")
    lon = (lax.axis_index("y") * lax.axis_size("zl") + lax.axis_index("zl")) * lax.axis_size("x")
    return lat, lon + lax.axis_index("x")


def row_points(points_ref, lat, rows, e):
    row = lat * rows + e
    if 0 <= e < rows:
        return points_ref[row]
    total = points_ref.shape[0]
    inside = (row >= 0) & (row < total)
    return jnp.where(inside, points_ref[jnp.clip(row, 0, total - 1)], 0)


def live_limits(points_ref, rows, cols):
    lat, lon = tile_position()
    return [jnp.clip(points_ref[lat * rows + h] - lon * cols, 0, cols) for h in range(rows)]


def live_count(limits):
    return functools.reduce(lambda a, c: a + c, limits).astype(jnp.float32)


def in_vmem():
    return pl.BlockSpec(memory_space=pltpu.VMEM)


def fetch(x_hbm_ref, x_ref, sems, b, base=0):
    return pltpu.make_async_copy(x_hbm_ref.at[base + b], x_ref.at[b], sems.at[b])


def pack_edges(x_ref, b, d, edges, k):
    _, rows, cols, _ = x_ref.shape
    first_row_ref, last_row_ref, first_col_ref, last_col_ref = edges
    first_row_ref[k] = x_ref[b, :d]
    last_row_ref[k] = x_ref[b, rows - d :]
    for h in range(rows):
        first_col_ref[k, h * d : (h + 1) * d] = x_ref[b, h, :d]
        last_col_ref[k, h * d : (h + 1) * d] = x_ref[b, h, cols - d :]


def edge_shapes(x, d):
    samples, rows, width, channels = x.shape
    shapes = [(samples, d, width, channels)] * 2 + [(samples, rows * d, channels)] * 2
    return [jax.ShapeDtypeStruct(shape, x.dtype) for shape in shapes]


def edge_specs(x, d, block):
    return [
        pl.BlockSpec((block, *e.shape[1:]), lambda g, *_, n=len(e.shape): (g,) + (0,) * (n - 1))
        for e in edge_shapes(x, d)
    ]


def stats_kernel(points_ref, x_hbm_ref, out_ref, *refs):
    *edges, x_ref, sems, sums_ref, squares_ref = refs
    g = pl.program_id(0)

    @pl.when(g == 0)
    def _():
        for b in range(x_ref.shape[0]):
            fetch(x_hbm_ref, x_ref, sems, b).start()

    fetch(x_hbm_ref, x_ref, sems, g).wait()
    _, rows, cols, _ = x_ref.shape
    limits = live_limits(points_ref, rows, cols)
    count = live_count(limits)
    row_statistics(
        lambda h, n: x_ref[g, h, :n].astype(jnp.float32), limits, count, sums_ref, squares_ref, g
    )
    pack_edges(x_ref, g, FIRST_DILATION, edges, 0)

    @pl.when(g == pl.num_programs(0) - 1)
    def _():
        store_group_stats(sums_ref, squares_ref, count, out_ref)


def local_statistics(x, points):
    samples, rows, width, channels = x.shape
    shape = (3, samples * GROUPS // LANES, LANES)
    return pl.pallas_call(
        stats_kernel,
        out_shape=[jax.ShapeDtypeStruct(shape, jnp.float32), *edge_shapes(x, FIRST_DILATION)],
        grid_spec=pltpu.PrefetchScalarGridSpec(
            num_scalar_prefetch=1,
            grid=(samples,),
            in_specs=[pl.BlockSpec(memory_space=pltpu.HBM)],
            out_specs=[
                pl.BlockSpec(shape, lambda g, *_: (0, 0, 0)),
                *edge_specs(x, FIRST_DILATION, 1),
            ],
            scratch_shapes=[
                pltpu.VMEM(x.shape, x.dtype),
                pltpu.SemaphoreType.DMA((samples,)),
                pltpu.VMEM((samples, channels), jnp.float32),
                pltpu.VMEM((samples, channels), jnp.float32),
            ],
        ),
        compiler_params=pltpu.CompilerParams(
            dimension_semantics=("arbitrary",), vmem_limit_bytes=VMEM_LIMIT
        ),
        cost_estimate=pl.CostEstimate(
            flops=8 * x.size, bytes_accessed=2 * x.size, transcendentals=0
        ),
        name="stats",
    )(points, x)


def chip_counts(points, chips, rows, cols, size):
    total = points.shape[1]
    lons = chips // lax.axis_size("zh")
    chip = lax.broadcasted_iota(jnp.int32, (chips, total), 0)
    row = lax.broadcasted_iota(jnp.int32, (chips, total), 1)
    live = jnp.clip(points - (chip % lons) * cols, 0, cols)
    mine = row // (rows * lax.axis_size("core")) == chip // lons
    return jnp.where(mine, live, 0).astype(jnp.float32).sum(axis=1, keepdims=True) * size


def combine_statistics(parts_ref, points_ref, norm_ref, rows, cols):
    _, samples, channels = norm_ref.shape
    slots = LANES // GROUPS
    chips = parts_ref.shape[0]
    counts = chip_counts(points_ref[...], chips, rows, cols, channels // GROUPS)[:, None, :]
    sums = parts_ref[:, 0]
    squares = parts_ref[:, 1]
    count = counts.sum(axis=0)
    mean = sums.sum(axis=0) / count
    offset = sums / jnp.maximum(counts, 1.0) - mean[None]
    var = (squares + counts * offset * offset).sum(axis=0) / count
    half = 0.5 * lax.rsqrt(var + EPS)
    own = slot_lanes(samples)
    spread = selection_matrix((LANES, channels), 1, channels)

    def unpacked(value):
        rows = jnp.broadcast_to(value[:, None], (samples // slots, slots, LANES)).reshape(samples, LANES)
        return jnp.where(own, rows, 0.0)

    both = exact_dot(jnp.concatenate([unpacked(mean), unpacked(half)], axis=0), spread)
    norm_ref[0] = both[:samples]
    norm_ref[1] = both[samples:]


def conv_kernel(dilation, chunk, which, with_stats, first, base, halo, points_ref, flags_ref, parts_ref, *refs):
    d = dilation
    points_row_ref, x_hbm_ref, top_ref, bottom_ref, left_ref, right_ref, w_ref, *refs = refs
    if first:
        given_ref, *refs = refs
    out_hbm_ref, *rest = refs
    if with_stats:
        stats_ref, *edges = rest[:5]
        x_ref, sems, out_ref, out_sems, norm_ref, even_ref, odd_ref, sums_ref, squares_ref, kept_ref = rest[5:]
    else:
        x_ref, sems, out_ref, out_sems, norm_ref, even_ref, odd_ref = rest
    g = pl.program_id(0)
    samples = x_ref.shape[0]
    _, rows, cols, channels = x_ref.shape
    lat, lon = tile_position()
    lon_total = lax.axis_size(LON) * cols
    origin = lon * cols
    column = lax.broadcasted_iota(jnp.int32, (cols, channels), 0)
    edge = lax.broadcasted_iota(jnp.int32, (d, channels), 0)
    points = [row_points(points_ref, lat, rows, e - d) for e in range(rows + 2 * d)]
    limits = [jnp.clip(points[d + h] - origin, 0, cols) for h in range(rows)]
    before_origin = (origin + lon_total - d) % lon_total
    after_origin = (origin + cols) % lon_total

    def activate_rows(b, act_ref, lo, hi):
        mean = norm_ref[0, pl.ds(first + b, 1)]
        half = norm_ref[1, pl.ds(first + b, 1)]

        def activated(value):
            t = (value.astype(jnp.float32) - mean) * half
            return t + t * jnp.tanh(t)

        for e in range(lo, hi):
            if e < d:
                row = top_ref[halo + b, e]
            elif e < rows + d:
                row = x_ref[b, e - d]
            else:
                row = bottom_ref[halo + b, e - rows - d]
            at = slice(e * d, (e + 1) * d)
            left = activated(left_ref[halo + b, at])
            right = activated(right_ref[halo + b, at])
            mid = jnp.where(column < points[e] - origin, activated(row), 0.0)
            lhs = jnp.where(edge < points[e] - before_origin, left, 0.0)
            rhs = jnp.where(edge < points[e] - after_origin, right, 0.0)
            before = jnp.concatenate([lhs, mid[: cols - d]], axis=0)
            after = jnp.concatenate([mid[d:], rhs], axis=0)
            act_ref[e, :, 0:channels] = before.astype(jnp.bfloat16)
            act_ref[e, :, channels : 2 * channels] = mid.astype(jnp.bfloat16)
            act_ref[e, :, 2 * channels :] = after.astype(jnp.bfloat16)

    def convolve_rows(k, scale, act_ref, start):
        acc = None
        for tap in range(3):
            lo = start + tap * d
            taken = act_ref[lo : lo + chunk].reshape(chunk * cols, 3 * channels)
            term = jnp.dot(taken, w_ref[tap], preferred_element_type=jnp.float32)
            acc = term if acc is None else acc + term
        base = x_ref[2 * g + k, start : start + chunk].astype(jnp.float32)
        result = (base + scale * acc.reshape(chunk, cols, channels)).astype(jnp.bfloat16)
        out_ref[2 * g + k, start : start + chunk] = result
        if with_stats and k == 1:
            kept_ref[start : start + chunk] = result

    def phase(k, act_ref, follow, next_ref):
        scale = flags_ref[first + 2 * g + k, which].astype(jnp.float32) * (1.0 / KEEP_RATE)
        steps = rows // chunk
        each = (rows + 2 * d) // steps
        for step in range(steps):
            last = rows + 2 * d if step == steps - 1 else (step + 1) * each
            activate_rows(follow, next_ref, step * each, last)
            convolve_rows(k, scale, act_ref, step * chunk)
        store(2 * g + k).start()
        if with_stats:
            pack_edges(out_ref, 2 * g + k, SECOND_DILATION, edges, k)

    def store(b):
        place = b if with_stats else first + b
        return pltpu.make_async_copy(out_ref.at[b], out_hbm_ref.at[place], out_sems.at[b])

    @pl.when(g == 0)
    def _():
        for b in range(samples):
            fetch(x_hbm_ref, x_ref, sems, b, base).start()
        combine_statistics(parts_ref, points_row_ref, norm_ref, rows, cols)
        fetch(x_hbm_ref, x_ref, sems, 0, base).wait()
        activate_rows(0, even_ref, 0, rows + 2 * d)
        if with_stats:
            kept_ref[...] = jnp.zeros_like(kept_ref)

    @pl.when(g < samples // 2 - 1)
    def _():
        fetch(x_hbm_ref, x_ref, sems, 2 * g + 2, base).wait()

    fetch(x_hbm_ref, x_ref, sems, 2 * g + 1, base).wait()
    count = live_count(limits)
    phase(0, even_ref, 2 * g + 1, odd_ref)
    if with_stats:
        row_statistics(
            lambda h, n: kept_ref[h, :n].astype(jnp.float32), limits, count, sums_ref, squares_ref, jnp.maximum(2 * g - 1, 0)
        )
    phase(1, odd_ref, jnp.minimum(2 * g + 2, samples - 1), even_ref)
    if with_stats:
        row_statistics(
            lambda h, n: out_ref[2 * g, h, :n].astype(jnp.float32), limits, count, sums_ref, squares_ref, 2 * g
        )

        @pl.when(g == pl.num_programs(0) - 1)
        def _():
            row_statistics(
                lambda h, n: out_ref[2 * g + 1, h, :n].astype(jnp.float32), limits, count, sums_ref, squares_ref, samples - 1
            )
            at = pl.ds(first // (LANES // GROUPS), samples * GROUPS // LANES)
            if first:
                stats_ref[...] = given_ref[...]
            store_group_stats(sums_ref, squares_ref, count, stats_ref.at[:, at])

    @pl.when(g == pl.num_programs(0) - 1)
    def _():
        for b in range(samples):
            store(b).wait()


def convolve(x, halos, weight, parts, points, flags, given, dilation, which, with_stats, first, base, halo):
    _, rows, width, channels = x.shape
    d = dilation
    total = flags.shape[0]
    samples = total // 2

    def whole(shape):
        return pl.BlockSpec(shape, lambda g, *_: (0,) * len(shape))

    half = jax.ShapeDtypeStruct((samples, rows, width, channels), jnp.bfloat16)
    out_shape = [half if with_stats else jax.ShapeDtypeStruct((total, *half.shape[1:]), jnp.bfloat16)]
    out_specs = [pl.BlockSpec(memory_space=pltpu.HBM)]
    act = pltpu.VMEM((rows + 2 * d, width, 3 * channels), jnp.bfloat16)
    scratch = [pltpu.VMEM(half.shape, x.dtype), pltpu.SemaphoreType.DMA((samples,))] * 2
    scratch += [pltpu.VMEM((2, total, channels), jnp.float32), act, act]
    if with_stats:
        shape = (3, total * GROUPS // LANES, LANES)
        out_shape += [jax.ShapeDtypeStruct(shape, jnp.float32), *edge_shapes(half, SECOND_DILATION)]
        out_specs += [whole(shape), *edge_specs(half, SECOND_DILATION, 2)]
        scratch += [pltpu.VMEM((samples, channels), jnp.float32)] * 2
        scratch += [pltpu.VMEM((rows, width, channels), jnp.bfloat16)]
    return pl.pallas_call(
        functools.partial(conv_kernel, d, CHUNK, which, with_stats, first, base, halo),
        out_shape=out_shape,
        grid_spec=pltpu.PrefetchScalarGridSpec(
            num_scalar_prefetch=2,
            grid=(samples // 2,),
            in_specs=[
                in_vmem(),
                in_vmem(),
                pl.BlockSpec(memory_space=pltpu.HBM),
                *[in_vmem()] * len(halos),
                in_vmem(),
                *([in_vmem() if with_stats else pl.BlockSpec(memory_space=pltpu.HBM)] if first else []),
            ],
            out_specs=out_specs,
            scratch_shapes=scratch,
        ),
        input_output_aliases={10: 0} if first and not with_stats else {},
        compiler_params=pltpu.CompilerParams(
            dimension_semantics=("arbitrary",), vmem_limit_bytes=VMEM_LIMIT
        ),
        cost_estimate=pl.CostEstimate(
            flops=18 * samples * rows * width * channels * channels,
            bytes_accessed=5 * samples * rows * width * channels,
            transcendentals=2 * samples * rows * width * channels,
        ),
        name="conv%d_%d" % (d, first),
    )(points, flags, parts, points[None], x, *halos, weight, *([given] if first else []))


def exchange_rows(edges):
    lat = lax.axis_size(LAT)
    top = lax.ppermute(edges[1], LAT, [(i, i + 1) for i in range(lat - 1)])
    bottom = lax.ppermute(edges[0], LAT, [(i + 1, i) for i in range(lat - 1)])
    return top, bottom


def exchange_columns(edges, top, bottom):
    samples, d, width, channels = top.shape
    lon = lax.axis_size(LON)

    def packed(cols, lo, hi):
        above = top[:, :, lo:hi].reshape(samples, d * d, channels)
        below = bottom[:, :, lo:hi].reshape(samples, d * d, channels)
        return jnp.concatenate([above, cols, below], axis=1)

    left = lax.ppermute(packed(edges[3], width - d, width), LON, [(i, (i + 1) % lon) for i in range(lon)])
    right = lax.ppermute(packed(edges[2], 0, d), LON, [((i + 1) % lon, i) for i in range(lon)])
    return left, right


def merge_cores(local):
    other = lax.ppermute(local, "core", [(0, 1), (1, 0)])
    own_count, other_count = local[2], other[2]
    both = jnp.maximum(own_count + other_count, 1.0)
    gap = local[0] / jnp.maximum(own_count, 1.0) - other[0] / jnp.maximum(other_count, 1.0)
    squares = local[1] + other[1] + gap * gap * (own_count * other_count / both)
    merged = jnp.stack([local[0] + other[0], squares])
    return jnp.broadcast_to(merged[None], (lax.axis_size(CHIPS), *merged.shape))


def per_device(features, band_points, survival_flags, first_kernel_weight, second_kernel_weight):
    samples, _, _, channels = features.shape
    half = samples // 2
    first_weight = first_kernel_weight.reshape(3, 3 * channels, channels)
    second_weight = second_kernel_weight.reshape(3, 3 * channels, channels)

    local, *edges = local_statistics(features, band_points)
    top, bottom = exchange_rows(edges)
    mine = merge_cores(local)
    mine, top, bottom = lax.optimization_barrier((mine, top, bottom))
    parts = lax.all_to_all(mine, CHIPS, 0, 0)
    halos = (top, bottom, *exchange_columns(edges, top, bottom))

    def first_half(start, given):
        return convolve(
            features, halos, first_weight, parts, band_points, survival_flags, given, FIRST_DILATION, 0, True, start, start, start
        )

    def second_half(start, x, halos, parts, given):
        return convolve(
            x, halos, second_weight, parts, band_points, survival_flags, given, SECOND_DILATION, 1, False, start, 0, 0
        )[0]

    early, local, *early_edges = first_half(0, None)
    early_rows = exchange_rows(early_edges)
    late, local, *late_edges = first_half(half, local)
    local, *early_rows = lax.optimization_barrier((local, *early_rows))
    late_rows = exchange_rows(late_edges)
    early_columns = exchange_columns(early_edges, *early_rows)
    mine = merge_cores(local)
    parts = lax.all_to_all(mine, CHIPS, 0, 0)
    late_columns = exchange_columns(late_edges, *late_rows)
    section = second_half(0, early, (*early_rows, *early_columns), parts, None)
    return second_half(half, late, (*late_rows, *late_columns), parts, section)


def solution(mesh):
    grid = Mesh(mesh.devices.reshape(2, 2, 4, 2, 4), (LAT + LON))
    spec = P(None, LAT, LON, None)
    return jax.shard_map(
        per_device, mesh=grid, in_specs=(spec, P(), P(), P(), P()), out_specs=spec, check_vma=False
    )
```

```python
import functools

import jax
import jax.numpy as jnp
from jax import lax
from jax.experimental import pallas as pl
from jax.experimental.pallas import tpu as pltpu
from jax.sharding import Mesh, PartitionSpec as P

GROUPS = 32
FIRST_DILATION = 2
SECOND_DILATION = 4
EPS = 1e-05
KEEP_RATE = 0.8

LAT = ("zh", "core")
LON = ("y", "zl", "x")
CHIPS = ("zh", "y", "zl", "x")
LANES = 128
VMEM_LIMIT = 59_300_000
CHUNK = 8


def exact_dot(a, selection):
    high = a.astype(jnp.bfloat16)
    rest = a - high.astype(jnp.float32)
    middle = rest.astype(jnp.bfloat16)
    low = (rest - middle.astype(jnp.float32)).astype(jnp.bfloat16)
    m = a.shape[0]
    parts = jnp.concatenate([high.astype(jnp.float32), middle.astype(jnp.float32), low.astype(jnp.float32)], axis=0)
    terms = jnp.dot(parts.astype(jnp.bfloat16), selection, preferred_element_type=jnp.float32)
    return terms[:m] + terms[m : 2 * m] + terms[2 * m :]


def selection_matrix(shape, channel_dim, channels):
    size = channels // GROUPS
    channel = lax.broadcasted_iota(jnp.int32, shape, channel_dim)
    lane = lax.broadcasted_iota(jnp.int32, shape, 1 - channel_dim)
    return jnp.where(channel // size == lane % GROUPS, 1.0, 0.0).astype(jnp.bfloat16)


def slot_lanes(samples):
    row = lax.broadcasted_iota(jnp.int32, (samples, LANES), 0)
    lane = lax.broadcasted_iota(jnp.int32, (samples, LANES), 1)
    return lane // GROUPS == row % (LANES // GROUPS)


def store_group_stats(sums_ref, squares_ref, count, out_ref):
    samples, channels = sums_ref.shape
    slots = LANES // GROUPS
    size = channels // GROUPS
    own = slot_lanes(samples)
    fold = selection_matrix((channels, LANES), 0, channels)
    spread = selection_matrix((LANES, channels), 1, channels)
    per_channel = jnp.maximum(count, 1.0)
    sums = sums_ref[...]

    def packed(value):
        return jnp.where(own, value, 0.0).reshape(samples // slots, slots, LANES).sum(axis=1)

    group_sum = exact_dot(sums, fold)
    centre = exact_dot(jnp.where(own, group_sum, 0.0), spread) / (per_channel * size)
    offset = sums / per_channel - centre
    group_squares = exact_dot(squares_ref[...] + count * offset * offset, fold)
    out_ref[0] = packed(group_sum)
    out_ref[1] = packed(group_squares)
    out_ref[2] = jnp.full(out_ref.shape[1:], count * size, jnp.float32)


def row_statistics(rows, limits, count, sums_ref, squares_ref, b):
    some = 16
    cols, channels = rows(0, None).shape
    column = lax.broadcasted_iota(jnp.int32, (cols, channels), 0)
    few = sum(jnp.minimum(limit, some) for limit in limits).astype(jnp.float32)
    total = jnp.zeros((some, channels), jnp.float32)
    for h in range(len(limits)):
        total = total + jnp.where(column[:some] < limits[h], rows(h, some), 0.0)
    pivot = total.sum(axis=0, keepdims=True) / jnp.maximum(few, 1.0)
    first = jnp.zeros((cols, channels), jnp.float32)
    second = jnp.zeros((cols, channels), jnp.float32)
    for h in range(len(limits)):
        value = jnp.where(column < limits[h], rows(h, None) - pivot, 0.0)
        first = first + value
        second = second + value * value
    moved = first.sum(axis=0, keepdims=True)
    squares = second.sum(axis=0, keepdims=True) - moved * moved / jnp.maximum(count, 1.0)
    sums_ref[pl.ds(b, 1)] = moved + count * pivot
    squares_ref[pl.ds(b, 1)] = jnp.maximum(squares, 0.0)


def tile_position():
    lat = lax.axis_index("zh") * lax.axis_size("core") + lax.axis_index("core")
    lon = (lax.axis_index("y") * lax.axis_size("zl") + lax.axis_index("zl")) * lax.axis_size("x")
    return lat, lon + lax.axis_index("x")


def row_points(points_ref, lat, rows, e):
    row = lat * rows + e
    if 0 <= e < rows:
        return points_ref[row]
    total = points_ref.shape[0]
    inside = (row >= 0) & (row < total)
    return jnp.where(inside, points_ref[jnp.clip(row, 0, total - 1)], 0)


def live_limits(points_ref, rows, cols):
    lat, lon = tile_position()
    return [jnp.clip(points_ref[lat * rows + h] - lon * cols, 0, cols) for h in range(rows)]


def live_count(limits):
    return functools.reduce(lambda a, c: a + c, limits).astype(jnp.float32)


def in_vmem():
    return pl.BlockSpec(memory_space=pltpu.VMEM)


def fetch(x_hbm_ref, x_ref, sems, b):
    return pltpu.make_async_copy(x_hbm_ref.at[b], x_ref.at[b], sems.at[b])


def pack_edges(x_ref, b, d, edges, k):
    _, rows, cols, _ = x_ref.shape
    first_row_ref, last_row_ref, first_col_ref, last_col_ref = edges
    first_row_ref[k] = x_ref[b, :d]
    last_row_ref[k] = x_ref[b, rows - d :]
    for h in range(rows):
        first_col_ref[k, h * d : (h + 1) * d] = x_ref[b, h, :d]
        last_col_ref[k, h * d : (h + 1) * d] = x_ref[b, h, cols - d :]


def edge_shapes(x, d):
    samples, rows, width, channels = x.shape
    shapes = [(samples, d, width, channels)] * 2 + [(samples, rows * d, channels)] * 2
    return [jax.ShapeDtypeStruct(shape, x.dtype) for shape in shapes]


def edge_specs(x, d, block):
    return [
        pl.BlockSpec((block, *e.shape[1:]), lambda g, *_, n=len(e.shape): (g,) + (0,) * (n - 1))
        for e in edge_shapes(x, d)
    ]


def stats_kernel(points_ref, x_hbm_ref, out_ref, *refs):
    *edges, x_ref, sems, sums_ref, squares_ref = refs
    g = pl.program_id(0)

    @pl.when(g == 0)
    def _():
        for b in range(x_ref.shape[0]):
            fetch(x_hbm_ref, x_ref, sems, b).start()

    fetch(x_hbm_ref, x_ref, sems, g).wait()
    _, rows, cols, _ = x_ref.shape
    limits = live_limits(points_ref, rows, cols)
    count = live_count(limits)
    row_statistics(
        lambda h, n: x_ref[g, h, :n].astype(jnp.float32), limits, count, sums_ref, squares_ref, g
    )
    pack_edges(x_ref, g, FIRST_DILATION, edges, 0)

    @pl.when(g == pl.num_programs(0) - 1)
    def _():
        store_group_stats(sums_ref, squares_ref, count, out_ref)


def local_statistics(x, points):
    samples, rows, width, channels = x.shape
    shape = (3, samples * GROUPS // LANES, LANES)
    return pl.pallas_call(
        stats_kernel,
        out_shape=[jax.ShapeDtypeStruct(shape, jnp.float32), *edge_shapes(x, FIRST_DILATION)],
        grid_spec=pltpu.PrefetchScalarGridSpec(
            num_scalar_prefetch=1,
            grid=(samples,),
            in_specs=[pl.BlockSpec(memory_space=pltpu.HBM)],
            out_specs=[
                pl.BlockSpec(shape, lambda g, *_: (0, 0, 0)),
                *edge_specs(x, FIRST_DILATION, 1),
            ],
            scratch_shapes=[
                pltpu.VMEM(x.shape, x.dtype),
                pltpu.SemaphoreType.DMA((samples,)),
                pltpu.VMEM((samples, channels), jnp.float32),
                pltpu.VMEM((samples, channels), jnp.float32),
            ],
        ),
        compiler_params=pltpu.CompilerParams(
            dimension_semantics=("arbitrary",), vmem_limit_bytes=VMEM_LIMIT
        ),
        cost_estimate=pl.CostEstimate(
            flops=8 * x.size, bytes_accessed=2 * x.size, transcendentals=0
        ),
        name="stats",
    )(points, x)


def chip_counts(points, chips, rows, cols, size):
    total = points.shape[1]
    lons = chips // lax.axis_size("zh")
    chip = lax.broadcasted_iota(jnp.int32, (chips, total), 0)
    row = lax.broadcasted_iota(jnp.int32, (chips, total), 1)
    live = jnp.clip(points - (chip % lons) * cols, 0, cols)
    mine = row // (rows * lax.axis_size("core")) == chip // lons
    return jnp.where(mine, live, 0).astype(jnp.float32).sum(axis=1, keepdims=True) * size


def combine_statistics(parts_ref, points_ref, norm_ref, rows, cols):
    _, samples, channels = norm_ref.shape
    slots = LANES // GROUPS
    chips = parts_ref.shape[0]
    counts = chip_counts(points_ref[...], chips, rows, cols, channels // GROUPS)[:, None, :]
    sums = parts_ref[:, 0]
    squares = parts_ref[:, 1]
    count = counts.sum(axis=0)
    mean = sums.sum(axis=0) / count
    offset = sums / jnp.maximum(counts, 1.0) - mean[None]
    var = (squares + counts * offset * offset).sum(axis=0) / count
    half = 0.5 * lax.rsqrt(var + EPS)
    own = slot_lanes(samples)
    spread = selection_matrix((LANES, channels), 1, channels)

    def unpacked(value):
        rows = jnp.broadcast_to(value[:, None], (samples // slots, slots, LANES)).reshape(samples, LANES)
        return jnp.where(own, rows, 0.0)

    both = exact_dot(jnp.concatenate([unpacked(mean), unpacked(half)], axis=0), spread)
    norm_ref[0] = both[:samples]
    norm_ref[1] = both[samples:]


def conv_kernel(dilation, chunk, which, with_stats, points_ref, flags_ref, parts_ref, points_row_ref, *refs):
    d = dilation
    x_hbm_ref, top_ref, bottom_ref, left_ref, right_ref, left_end_ref, right_end_ref, w_ref, out_hbm_ref, *rest = refs
    if with_stats:
        stats_ref, *edges = rest[:5]
        x_ref, sems, out_ref, out_sems, norm_ref, even_ref, odd_ref, sums_ref, squares_ref, kept_ref = rest[5:]
    else:
        x_ref, sems, out_ref, out_sems, norm_ref, even_ref, odd_ref = rest
    g = pl.program_id(0)
    samples = norm_ref.shape[1]
    _, rows, cols, channels = x_ref.shape
    lat, lon = tile_position()
    lon_total = lax.axis_size(LON) * cols
    origin = lon * cols
    column = lax.broadcasted_iota(jnp.int32, (cols, channels), 0)
    edge = lax.broadcasted_iota(jnp.int32, (d, channels), 0)
    points = [row_points(points_ref, lat, rows, e - d) for e in range(rows + 2 * d)]
    limits = [jnp.clip(points[d + h] - origin, 0, cols) for h in range(rows)]
    before_origin = (origin + lon_total - d) % lon_total
    after_origin = (origin + cols) % lon_total

    def activate_rows(b, act_ref, lo, hi):
        mean = norm_ref[0, pl.ds(b, 1)]
        half = norm_ref[1, pl.ds(b, 1)]

        def activated(value):
            t = (value.astype(jnp.float32) - mean) * half
            return t + t * jnp.tanh(t)

        for e in range(lo, hi):
            if e < d:
                row, side = top_ref[b, e], (left_end_ref, right_end_ref, e)
            elif e < rows + d:
                row, side = x_ref[b, e - d], (left_ref, right_ref, e - d)
            else:
                row, side = bottom_ref[b, e - rows - d], (left_end_ref, right_end_ref, e - rows)
            at = slice(side[2] * d, (side[2] + 1) * d)
            left = activated(side[0][b, at])
            right = activated(side[1][b, at])
            mid = jnp.where(column < points[e] - origin, activated(row), 0.0)
            lhs = jnp.where(edge < points[e] - before_origin, left, 0.0)
            rhs = jnp.where(edge < points[e] - after_origin, right, 0.0)
            before = jnp.concatenate([lhs, mid[: cols - d]], axis=0)
            after = jnp.concatenate([mid[d:], rhs], axis=0)
            act_ref[e, :, 0:channels] = before.astype(jnp.bfloat16)
            act_ref[e, :, channels : 2 * channels] = mid.astype(jnp.bfloat16)
            act_ref[e, :, 2 * channels :] = after.astype(jnp.bfloat16)

    def convolve_rows(k, scale, act_ref, start):
        acc = None
        for tap in range(3):
            lo = start + tap * d
            taken = act_ref[lo : lo + chunk].reshape(chunk * cols, 3 * channels)
            term = jnp.dot(taken, w_ref[tap], preferred_element_type=jnp.float32)
            acc = term if acc is None else acc + term
        base = x_ref[2 * g + k, start : start + chunk].astype(jnp.float32)
        result = (base + scale * acc.reshape(chunk, cols, channels)).astype(jnp.bfloat16)
        out_ref[2 * g + k, start : start + chunk] = result
        if with_stats and k == 1:
            kept_ref[start : start + chunk] = result

    def phase(k, act_ref, follow, next_ref):
        scale = flags_ref[2 * g + k, which].astype(jnp.float32) * (1.0 / KEEP_RATE)
        steps = rows // chunk
        each = (rows + 2 * d) // steps
        for step in range(steps):
            last = rows + 2 * d if step == steps - 1 else (step + 1) * each
            activate_rows(follow, next_ref, step * each, last)
            convolve_rows(k, scale, act_ref, step * chunk)
        store(2 * g + k).start()
        if with_stats:
            pack_edges(out_ref, 2 * g + k, SECOND_DILATION, edges, k)

    def store(b):
        return pltpu.make_async_copy(out_ref.at[b], out_hbm_ref.at[b], out_sems.at[b])

    @pl.when(g == 0)
    def _():
        for b in range(samples):
            fetch(x_hbm_ref, x_ref, sems, b).start()
        combine_statistics(parts_ref, points_row_ref, norm_ref, rows, cols)
        fetch(x_hbm_ref, x_ref, sems, 0).wait()
        activate_rows(0, even_ref, 0, rows + 2 * d)
        if with_stats:
            kept_ref[...] = jnp.zeros_like(kept_ref)

    @pl.when(g < samples // 2 - 1)
    def _():
        fetch(x_hbm_ref, x_ref, sems, 2 * g + 2).wait()

    fetch(x_hbm_ref, x_ref, sems, 2 * g + 1).wait()
    count = live_count(limits)
    phase(0, even_ref, 2 * g + 1, odd_ref)
    if with_stats:
        row_statistics(
            lambda h, n: kept_ref[h, :n].astype(jnp.float32), limits, count, sums_ref, squares_ref, jnp.maximum(2 * g - 1, 0)
        )
    phase(1, odd_ref, jnp.minimum(2 * g + 2, samples - 1), even_ref)
    if with_stats:
        row_statistics(
            lambda h, n: out_ref[2 * g, h, :n].astype(jnp.float32), limits, count, sums_ref, squares_ref, 2 * g
        )

        @pl.when(g == pl.num_programs(0) - 1)
        def _():
            row_statistics(
                lambda h, n: out_ref[2 * g + 1, h, :n].astype(jnp.float32), limits, count, sums_ref, squares_ref, samples - 1
            )
            store_group_stats(sums_ref, squares_ref, count, stats_ref)

    @pl.when(g == pl.num_programs(0) - 1)
    def _():
        for b in range(samples):
            store(b).wait()


def convolve(x, halos, weight, parts, points, flags, dilation, which, with_stats):
    samples, rows, width, channels = x.shape
    d = dilation
    def whole(shape):
        return pl.BlockSpec(shape, lambda g, *_: (0,) * len(shape))

    out_shape = [jax.ShapeDtypeStruct(x.shape, jnp.bfloat16)]
    out_specs = [pl.BlockSpec(memory_space=pltpu.HBM)]
    act = pltpu.VMEM((rows + 2 * d, width, 3 * channels), jnp.bfloat16)
    scratch = [pltpu.VMEM(x.shape, x.dtype), pltpu.SemaphoreType.DMA((samples,))] * 2
    scratch += [pltpu.VMEM((2, samples, channels), jnp.float32), act, act]
    if with_stats:
        shape = (3, samples * GROUPS // LANES, LANES)
        out_shape += [jax.ShapeDtypeStruct(shape, jnp.float32), *edge_shapes(x, SECOND_DILATION)]
        out_specs += [whole(shape), *edge_specs(x, SECOND_DILATION, 2)]
        scratch += [pltpu.VMEM((samples, channels), jnp.float32)] * 2
        scratch += [pltpu.VMEM((rows, width, channels), jnp.bfloat16)]
    return pl.pallas_call(
        functools.partial(conv_kernel, d, CHUNK, which, with_stats),
        out_shape=out_shape,
        grid_spec=pltpu.PrefetchScalarGridSpec(
            num_scalar_prefetch=2,
            grid=(samples // 2,),
            in_specs=[
                in_vmem(),
                in_vmem(),
                pl.BlockSpec(memory_space=pltpu.HBM),
                *[in_vmem()] * len(halos),
                in_vmem(),
            ],
            out_specs=out_specs,
            scratch_shapes=scratch,
        ),
        compiler_params=pltpu.CompilerParams(
            dimension_semantics=("arbitrary",), vmem_limit_bytes=VMEM_LIMIT
        ),
        cost_estimate=pl.CostEstimate(
            flops=2 * x.size * 9 * channels, bytes_accessed=5 * x.size, transcendentals=2 * x.size
        ),
        name="conv%d" % d,
    )(points, flags, parts, points[None], x, *halos, weight)


def exchange_sides(edges):
    first_row, last_row, first_col, last_col = edges
    lat, lon = lax.axis_size(LAT), lax.axis_size(LON)
    up = [(i, i + 1) for i in range(lat - 1)]
    down = [(i + 1, i) for i in range(lat - 1)]
    east = [(i, (i + 1) % lon) for i in range(lon)]
    west = [((i + 1) % lon, i) for i in range(lon)]
    top = lax.ppermute(last_row, LAT, up)
    bottom = lax.ppermute(first_row, LAT, down)
    left = lax.ppermute(last_col, LON, east)
    right = lax.ppermute(first_col, LON, west)
    return top, bottom, left, right


def exchange_corners(top, bottom):
    samples, d, width, channels = top.shape
    lon = lax.axis_size(LON)
    east = [(i, (i + 1) % lon) for i in range(lon)]
    west = [((i + 1) % lon, i) for i in range(lon)]

    def packed(lo, hi):
        ends = jnp.concatenate([top[:, :, lo:hi], bottom[:, :, lo:hi]], axis=1)
        return ends.reshape(samples, 2 * d * d, channels)

    left = lax.ppermute(packed(width - d, width), LON, east)
    right = lax.ppermute(packed(0, d), LON, west)
    return left, right


def merge_cores(local):
    other = lax.ppermute(local, "core", [(0, 1), (1, 0)])
    own_count, other_count = local[2], other[2]
    both = jnp.maximum(own_count + other_count, 1.0)
    gap = local[0] / jnp.maximum(own_count, 1.0) - other[0] / jnp.maximum(other_count, 1.0)
    squares = local[1] + other[1] + gap * gap * (own_count * other_count / both)
    merged = jnp.stack([local[0] + other[0], squares])
    return jnp.broadcast_to(merged[None], (lax.axis_size(CHIPS), *merged.shape))


def exchange(local, edges):
    top, bottom, left, right = exchange_sides(edges)
    parts = lax.all_to_all(merge_cores(local), CHIPS, 0, 0)
    parts, top, bottom = lax.optimization_barrier((parts, top, bottom))
    return parts, (top, bottom, left, right, *exchange_corners(top, bottom))


def per_device(features, band_points, survival_flags, first_kernel_weight, second_kernel_weight):
    channels = features.shape[3]
    first_weight = first_kernel_weight.reshape(3, 3 * channels, channels)
    second_weight = second_kernel_weight.reshape(3, 3 * channels, channels)
    local, *edges = local_statistics(features, band_points)
    parts, halos = exchange(local, edges)
    first, local, *edges = convolve(
        features, halos, first_weight, parts, band_points, survival_flags, FIRST_DILATION, 0, True
    )
    parts, halos = exchange(local, edges)
    (section,) = convolve(
        first, halos, second_weight, parts, band_points, survival_flags, SECOND_DILATION, 1, False
    )
    return section


def solution(mesh):
    grid = Mesh(mesh.devices.reshape(2, 2, 4, 2, 4), (LAT + LON))
    spec = P(None, LAT, LON, None)
    return jax.shard_map(
        per_device, mesh=grid, in_specs=(spec, P(), P(), P(), P()), out_specs=spec, check_vma=False
    )
```

```python
import functools

import jax
import jax.numpy as jnp
from jax import lax
from jax.experimental import pallas as pl
from jax.experimental.pallas import tpu as pltpu
from jax.sharding import Mesh, PartitionSpec as P

GROUPS = 32
FIRST_DILATION = 2
SECOND_DILATION = 4
EPS = 1e-05
KEEP_RATE = 0.8

LAT = ("zh", "core")
LON = ("y", "zl", "x")
CHIPS = ("zh", "y", "zl", "x")
LANES = 128
VMEM_LIMIT = 59_300_000
CHUNK = 8
NORM_FLOPS = 10 * 10**9


def exact_dot(a, selection):
    high = a.astype(jnp.bfloat16)
    rest = a - high.astype(jnp.float32)
    middle = rest.astype(jnp.bfloat16)
    low = (rest - middle.astype(jnp.float32)).astype(jnp.bfloat16)
    m = a.shape[0]
    parts = jnp.concatenate([high.astype(jnp.float32), middle.astype(jnp.float32), low.astype(jnp.float32)], axis=0)
    terms = jnp.dot(parts.astype(jnp.bfloat16), selection, preferred_element_type=jnp.float32)
    return terms[:m] + terms[m : 2 * m] + terms[2 * m :]


def selection_matrix(shape, channel_dim, channels):
    size = channels // GROUPS
    channel = lax.broadcasted_iota(jnp.int32, shape, channel_dim)
    lane = lax.broadcasted_iota(jnp.int32, shape, 1 - channel_dim)
    return jnp.where(channel // size == lane % GROUPS, 1.0, 0.0).astype(jnp.bfloat16)


def slot_lanes(samples):
    row = lax.broadcasted_iota(jnp.int32, (samples, LANES), 0)
    lane = lax.broadcasted_iota(jnp.int32, (samples, LANES), 1)
    return lane // GROUPS == row % (LANES // GROUPS)


def store_group_stats(sums_ref, squares_ref, count, out_ref):
    samples, channels = sums_ref.shape
    slots = LANES // GROUPS
    size = channels // GROUPS
    own = slot_lanes(samples)
    fold = selection_matrix((channels, LANES), 0, channels)
    spread = selection_matrix((LANES, channels), 1, channels)
    per_channel = jnp.maximum(count, 1.0)
    sums = sums_ref[...]

    def packed(value):
        return jnp.where(own, value, 0.0).reshape(samples // slots, slots, LANES).sum(axis=1)

    group_sum = exact_dot(sums, fold)
    centre = exact_dot(jnp.where(own, group_sum, 0.0), spread) / (per_channel * size)
    offset = sums / per_channel - centre
    group_squares = exact_dot(squares_ref[...] + count * offset * offset, fold)
    out_ref[0] = packed(group_sum)
    out_ref[1] = packed(group_squares)
    out_ref[2] = jnp.full(out_ref.shape[1:], count * size, jnp.float32)


def row_statistics(rows, limits, count, sums_ref, squares_ref, b):
    some = 16
    cols, channels = rows(0, None).shape
    column = lax.broadcasted_iota(jnp.int32, (cols, channels), 0)
    few = sum(jnp.minimum(limit, some) for limit in limits).astype(jnp.float32)
    total = jnp.zeros((some, channels), jnp.float32)
    for h in range(len(limits)):
        total = total + jnp.where(column[:some] < limits[h], rows(h, some), 0.0)
    pivot = total.sum(axis=0, keepdims=True) / jnp.maximum(few, 1.0)
    first = jnp.zeros((cols, channels), jnp.float32)
    second = jnp.zeros((cols, channels), jnp.float32)
    for h in range(len(limits)):
        value = jnp.where(column < limits[h], rows(h, None) - pivot, 0.0)
        first = first + value
        second = second + value * value
    moved = first.sum(axis=0, keepdims=True)
    squares = second.sum(axis=0, keepdims=True) - moved * moved / jnp.maximum(count, 1.0)
    sums_ref[pl.ds(b, 1)] = moved + count * pivot
    squares_ref[pl.ds(b, 1)] = jnp.maximum(squares, 0.0)


def tile_position():
    lat = lax.axis_index("zh") * lax.axis_size("core") + lax.axis_index("core")
    lon = (lax.axis_index("y") * lax.axis_size("zl") + lax.axis_index("zl")) * lax.axis_size("x")
    return lat, lon + lax.axis_index("x")


def row_points(points_ref, lat, rows, e):
    row = lat * rows + e
    if 0 <= e < rows:
        return points_ref[row]
    total = points_ref.shape[0]
    inside = (row >= 0) & (row < total)
    return jnp.where(inside, points_ref[jnp.clip(row, 0, total - 1)], 0)


def live_limits(points_ref, rows, cols):
    lat, lon = tile_position()
    return [jnp.clip(points_ref[lat * rows + h] - lon * cols, 0, cols) for h in range(rows)]


def live_count(limits):
    return functools.reduce(lambda a, c: a + c, limits).astype(jnp.float32)


def in_vmem():
    return pl.BlockSpec(memory_space=pltpu.VMEM)


def fetch(x_hbm_ref, x_ref, sems, b):
    return pltpu.make_async_copy(x_hbm_ref.at[b], x_ref.at[b], sems.at[b])


def pack_edges(x_ref, b, d, edges, k):
    _, rows, cols, _ = x_ref.shape
    first_row_ref, last_row_ref, first_col_ref, last_col_ref = edges
    first_row_ref[k] = x_ref[b, :d]
    last_row_ref[k] = x_ref[b, rows - d :]
    for h in range(rows):
        first_col_ref[k, h * d : (h + 1) * d] = x_ref[b, h, :d]
        last_col_ref[k, h * d : (h + 1) * d] = x_ref[b, h, cols - d :]


def edge_shapes(x, d):
    samples, rows, width, channels = x.shape
    shapes = [(samples, d, width, channels)] * 2 + [(samples, rows * d, channels)] * 2
    return [jax.ShapeDtypeStruct(shape, x.dtype) for shape in shapes]


def edge_specs(x, d, block):
    return [
        pl.BlockSpec((block, *e.shape[1:]), lambda g, *_, n=len(e.shape): (g,) + (0,) * (n - 1))
        for e in edge_shapes(x, d)
    ]


def stats_kernel(points_ref, x_hbm_ref, out_ref, *refs):
    *edges, x_ref, sems, sums_ref, squares_ref = refs
    g = pl.program_id(0)

    @pl.when(g == 0)
    def _():
        for b in range(x_ref.shape[0]):
            fetch(x_hbm_ref, x_ref, sems, b).start()

    fetch(x_hbm_ref, x_ref, sems, g).wait()
    _, rows, cols, _ = x_ref.shape
    limits = live_limits(points_ref, rows, cols)
    count = live_count(limits)
    row_statistics(
        lambda h, n: x_ref[g, h, :n].astype(jnp.float32), limits, count, sums_ref, squares_ref, g
    )
    pack_edges(x_ref, g, FIRST_DILATION, edges, 0)

    @pl.when(g == pl.num_programs(0) - 1)
    def _():
        store_group_stats(sums_ref, squares_ref, count, out_ref)


def local_statistics(x, points):
    samples, rows, width, channels = x.shape
    shape = (3, samples * GROUPS // LANES, LANES)
    return pl.pallas_call(
        stats_kernel,
        out_shape=[jax.ShapeDtypeStruct(shape, jnp.float32), *edge_shapes(x, FIRST_DILATION)],
        grid_spec=pltpu.PrefetchScalarGridSpec(
            num_scalar_prefetch=1,
            grid=(samples,),
            in_specs=[pl.BlockSpec(memory_space=pltpu.HBM)],
            out_specs=[
                pl.BlockSpec(shape, lambda g, *_: (0, 0, 0)),
                *edge_specs(x, FIRST_DILATION, 1),
            ],
            scratch_shapes=[
                pltpu.VMEM(x.shape, x.dtype),
                pltpu.SemaphoreType.DMA((samples,)),
                pltpu.VMEM((samples, channels), jnp.float32),
                pltpu.VMEM((samples, channels), jnp.float32),
            ],
        ),
        compiler_params=pltpu.CompilerParams(
            dimension_semantics=("arbitrary",), vmem_limit_bytes=VMEM_LIMIT
        ),
        cost_estimate=pl.CostEstimate(
            flops=8 * x.size, bytes_accessed=2 * x.size, transcendentals=0
        ),
        name="stats",
    )(points, x)


def chip_counts(points, chips, rows, cols, size):
    total = points.shape[1]
    lons = chips // lax.axis_size("zh")
    chip = lax.broadcasted_iota(jnp.int32, (chips, total), 0)
    row = lax.broadcasted_iota(jnp.int32, (chips, total), 1)
    live = jnp.clip(points - (chip % lons) * cols, 0, cols)
    mine = row // (rows * lax.axis_size("core")) == chip // lons
    return jnp.where(mine, live, 0).astype(jnp.float32).sum(axis=1, keepdims=True) * size


def combine_kernel(rows, cols, parts_ref, points_ref, norm_ref):
    _, samples, channels = norm_ref.shape
    slots = LANES // GROUPS
    chips = parts_ref.shape[0]
    counts = chip_counts(points_ref[...], chips, rows, cols, channels // GROUPS)[:, None, :]
    sums = parts_ref[:, 0]
    squares = parts_ref[:, 1]
    count = counts.sum(axis=0)
    mean = sums.sum(axis=0) / count
    offset = sums / jnp.maximum(counts, 1.0) - mean[None]
    var = (squares + counts * offset * offset).sum(axis=0) / count
    half = 0.5 * lax.rsqrt(var + EPS)
    own = slot_lanes(samples)
    spread = selection_matrix((LANES, channels), 1, channels)

    def unpacked(value):
        rows = jnp.broadcast_to(value[:, None], (samples // slots, slots, LANES)).reshape(samples, LANES)
        return jnp.where(own, rows, 0.0)

    both = exact_dot(jnp.concatenate([unpacked(mean), unpacked(half)], axis=0), spread)
    norm_ref[0] = both[:samples]
    norm_ref[1] = both[samples:]


def combine_statistics(parts, points, x):
    samples, rows, cols, channels = x.shape
    return pl.pallas_call(
        functools.partial(combine_kernel, rows, cols),
        out_shape=jax.ShapeDtypeStruct((2, samples, channels), jnp.float32),
        in_specs=[in_vmem(), in_vmem()],
        out_specs=in_vmem(),
        cost_estimate=pl.CostEstimate(flops=NORM_FLOPS, bytes_accessed=parts.size * 4, transcendentals=0),
        name="norm",
    )(parts, points[None])


def conv_kernel(dilation, chunk, which, with_stats, points_ref, flags_ref, norm_ref, *refs):
    d = dilation
    x_hbm_ref, top_ref, bottom_ref, left_ref, right_ref, w_ref, out_hbm_ref, *rest = refs
    if with_stats:
        stats_ref, *edges = rest[:5]
        x_ref, sems, out_ref, out_sems, even_ref, odd_ref, sums_ref, squares_ref, kept_ref = rest[5:]
    else:
        x_ref, sems, out_ref, out_sems, even_ref, odd_ref = rest
    g = pl.program_id(0)
    samples = norm_ref.shape[1]
    _, rows, cols, channels = x_ref.shape
    lat, lon = tile_position()
    lon_total = lax.axis_size(LON) * cols
    origin = lon * cols
    column = lax.broadcasted_iota(jnp.int32, (cols, channels), 0)
    edge = lax.broadcasted_iota(jnp.int32, (d, channels), 0)
    points = [row_points(points_ref, lat, rows, e - d) for e in range(rows + 2 * d)]
    limits = [jnp.clip(points[d + h] - origin, 0, cols) for h in range(rows)]
    before_origin = (origin + lon_total - d) % lon_total
    after_origin = (origin + cols) % lon_total

    def activate_rows(b, act_ref, lo, hi):
        mean = norm_ref[0, pl.ds(b, 1)]
        half = norm_ref[1, pl.ds(b, 1)]

        def activated(value):
            t = (value.astype(jnp.float32) - mean) * half
            return t + t * jnp.tanh(t)

        for e in range(lo, hi):
            if e < d:
                row = top_ref[b, e]
            elif e < rows + d:
                row = x_ref[b, e - d]
            else:
                row = bottom_ref[b, e - rows - d]
            at = slice(e * d, (e + 1) * d)
            left = activated(left_ref[b, at])
            right = activated(right_ref[b, at])
            mid = jnp.where(column < points[e] - origin, activated(row), 0.0)
            lhs = jnp.where(edge < points[e] - before_origin, left, 0.0)
            rhs = jnp.where(edge < points[e] - after_origin, right, 0.0)
            before = jnp.concatenate([lhs, mid[: cols - d]], axis=0)
            after = jnp.concatenate([mid[d:], rhs], axis=0)
            act_ref[e, :, 0:channels] = before.astype(jnp.bfloat16)
            act_ref[e, :, channels : 2 * channels] = mid.astype(jnp.bfloat16)
            act_ref[e, :, 2 * channels :] = after.astype(jnp.bfloat16)

    def convolve_rows(k, scale, act_ref, start):
        acc = None
        for tap in range(3):
            lo = start + tap * d
            taken = act_ref[lo : lo + chunk].reshape(chunk * cols, 3 * channels)
            term = jnp.dot(taken, w_ref[tap], preferred_element_type=jnp.float32)
            acc = term if acc is None else acc + term
        base = x_ref[2 * g + k, start : start + chunk].astype(jnp.float32)
        result = (base + scale * acc.reshape(chunk, cols, channels)).astype(jnp.bfloat16)
        out_ref[2 * g + k, start : start + chunk] = result
        if with_stats and k == 1:
            kept_ref[start : start + chunk] = result

    def phase(k, act_ref, follow, next_ref):
        scale = flags_ref[2 * g + k, which].astype(jnp.float32) * (1.0 / KEEP_RATE)
        steps = rows // chunk
        each = (rows + 2 * d) // steps
        for step in range(steps):
            last = rows + 2 * d if step == steps - 1 else (step + 1) * each
            activate_rows(follow, next_ref, step * each, last)
            convolve_rows(k, scale, act_ref, step * chunk)
        store(2 * g + k).start()
        if with_stats:
            pack_edges(out_ref, 2 * g + k, SECOND_DILATION, edges, k)

    def store(b):
        return pltpu.make_async_copy(out_ref.at[b], out_hbm_ref.at[b], out_sems.at[b])

    @pl.when(g == 0)
    def _():
        for b in range(samples):
            fetch(x_hbm_ref, x_ref, sems, b).start()
        fetch(x_hbm_ref, x_ref, sems, 0).wait()
        activate_rows(0, even_ref, 0, rows + 2 * d)
        if with_stats:
            kept_ref[...] = jnp.zeros_like(kept_ref)

    @pl.when(g < samples // 2 - 1)
    def _():
        fetch(x_hbm_ref, x_ref, sems, 2 * g + 2).wait()

    fetch(x_hbm_ref, x_ref, sems, 2 * g + 1).wait()
    count = live_count(limits)
    phase(0, even_ref, 2 * g + 1, odd_ref)
    if with_stats:
        row_statistics(
            lambda h, n: kept_ref[h, :n].astype(jnp.float32), limits, count, sums_ref, squares_ref, jnp.maximum(2 * g - 1, 0)
        )
    phase(1, odd_ref, jnp.minimum(2 * g + 2, samples - 1), even_ref)
    if with_stats:
        row_statistics(
            lambda h, n: out_ref[2 * g, h, :n].astype(jnp.float32), limits, count, sums_ref, squares_ref, 2 * g
        )

        @pl.when(g == pl.num_programs(0) - 1)
        def _():
            row_statistics(
                lambda h, n: out_ref[2 * g + 1, h, :n].astype(jnp.float32), limits, count, sums_ref, squares_ref, samples - 1
            )
            store_group_stats(sums_ref, squares_ref, count, stats_ref)

    @pl.when(g == pl.num_programs(0) - 1)
    def _():
        for b in range(samples):
            store(b).wait()


def convolve(x, halos, weight, norm, points, flags, dilation, which, with_stats):
    samples, rows, width, channels = x.shape
    d = dilation
    def whole(shape):
        return pl.BlockSpec(shape, lambda g, *_: (0,) * len(shape))

    out_shape = [jax.ShapeDtypeStruct(x.shape, jnp.bfloat16)]
    out_specs = [pl.BlockSpec(memory_space=pltpu.HBM)]
    act = pltpu.VMEM((rows + 2 * d, width, 3 * channels), jnp.bfloat16)
    scratch = [pltpu.VMEM(x.shape, x.dtype), pltpu.SemaphoreType.DMA((samples,))] * 2
    scratch += [act, act]
    if with_stats:
        shape = (3, samples * GROUPS // LANES, LANES)
        out_shape += [jax.ShapeDtypeStruct(shape, jnp.float32), *edge_shapes(x, SECOND_DILATION)]
        out_specs += [whole(shape), *edge_specs(x, SECOND_DILATION, 2)]
        scratch += [pltpu.VMEM((samples, channels), jnp.float32)] * 2
        scratch += [pltpu.VMEM((rows, width, channels), jnp.bfloat16)]
    return pl.pallas_call(
        functools.partial(conv_kernel, d, CHUNK, which, with_stats),
        out_shape=out_shape,
        grid_spec=pltpu.PrefetchScalarGridSpec(
            num_scalar_prefetch=2,
            grid=(samples // 2,),
            in_specs=[
                in_vmem(),
                pl.BlockSpec(memory_space=pltpu.HBM),
                *[in_vmem()] * len(halos),
                in_vmem(),
            ],
            out_specs=out_specs,
            scratch_shapes=scratch,
        ),
        compiler_params=pltpu.CompilerParams(
            dimension_semantics=("arbitrary",), vmem_limit_bytes=VMEM_LIMIT
        ),
        cost_estimate=pl.CostEstimate(
            flops=2 * x.size * 9 * channels, bytes_accessed=5 * x.size, transcendentals=2 * x.size
        ),
        name="conv%d" % d,
    )(points, flags, norm, x, *halos, weight)


def exchange_rows(edges):
    lat = lax.axis_size(LAT)
    top = lax.ppermute(edges[1], LAT, [(i, i + 1) for i in range(lat - 1)])
    bottom = lax.ppermute(edges[0], LAT, [(i + 1, i) for i in range(lat - 1)])
    return top, bottom


def exchange_columns(edges, top, bottom):
    samples, d, width, channels = top.shape
    lon = lax.axis_size(LON)

    def packed(cols, lo, hi):
        above = top[:, :, lo:hi].reshape(samples, d * d, channels)
        below = bottom[:, :, lo:hi].reshape(samples, d * d, channels)
        return jnp.concatenate([above, cols, below], axis=1)

    left = lax.ppermute(packed(edges[3], width - d, width), LON, [(i, (i + 1) % lon) for i in range(lon)])
    right = lax.ppermute(packed(edges[2], 0, d), LON, [((i + 1) % lon, i) for i in range(lon)])
    return left, right


def merge_cores(local):
    other = lax.ppermute(local, "core", [(0, 1), (1, 0)])
    own_count, other_count = local[2], other[2]
    both = jnp.maximum(own_count + other_count, 1.0)
    gap = local[0] / jnp.maximum(own_count, 1.0) - other[0] / jnp.maximum(other_count, 1.0)
    squares = local[1] + other[1] + gap * gap * (own_count * other_count / both)
    merged = jnp.stack([local[0] + other[0], squares])
    return jnp.broadcast_to(merged[None], (lax.axis_size(CHIPS), *merged.shape))


def exchange(local, edges, points, x):
    mine = merge_cores(local)
    top, bottom = exchange_rows(edges)
    norm = combine_statistics(lax.all_to_all(mine, CHIPS, 0, 0), points, x)
    return norm, (top, bottom, *exchange_columns(edges, top, bottom))


def per_device(features, band_points, survival_flags, first_kernel_weight, second_kernel_weight):
    channels = features.shape[3]
    first_weight = first_kernel_weight.reshape(3, 3 * channels, channels)
    second_weight = second_kernel_weight.reshape(3, 3 * channels, channels)
    local, *edges = local_statistics(features, band_points)
    norm, halos = exchange(local, edges, band_points, features)
    first, local, *edges = convolve(
        features, halos, first_weight, norm, band_points, survival_flags, FIRST_DILATION, 0, True
    )
    norm, halos = exchange(local, edges, band_points, first)
    (section,) = convolve(
        first, halos, second_weight, norm, band_points, survival_flags, SECOND_DILATION, 1, False
    )
    return section


def solution(mesh):
    grid = Mesh(mesh.devices.reshape(2, 2, 4, 2, 4), (LAT + LON))
    spec = P(None, LAT, LON, None)
    return jax.shard_map(
        per_device, mesh=grid, in_specs=(spec, P(), P(), P(), P()), out_specs=spec, check_vma=False
    )
```

```python
import functools

import jax
import jax.numpy as jnp
from jax import lax
from jax.experimental import pallas as pl
from jax.experimental.pallas import tpu as pltpu
from jax.sharding import Mesh, PartitionSpec as P

GROUPS = 32
FIRST_DILATION = 2
SECOND_DILATION = 4
EPS = 1e-05
KEEP_RATE = 0.8

LAT = ("zh", "core")
LON = ("y", "zl", "x")
CHIPS = ("zh", "y", "zl", "x")
LANES = 128
VMEM_LIMIT = 52_000_000
CHUNK = 8
NORM_FLOPS = 10 * 10**9


def exact_dot(a, selection):
    high = a.astype(jnp.bfloat16)
    rest = a - high.astype(jnp.float32)
    middle = rest.astype(jnp.bfloat16)
    low = (rest - middle.astype(jnp.float32)).astype(jnp.bfloat16)
    m = a.shape[0]
    parts = jnp.concatenate([high.astype(jnp.float32), middle.astype(jnp.float32), low.astype(jnp.float32)], axis=0)
    terms = jnp.dot(parts.astype(jnp.bfloat16), selection, preferred_element_type=jnp.float32)
    return terms[:m] + terms[m : 2 * m] + terms[2 * m :]


def selection_matrix(shape, channel_dim, channels):
    size = channels // GROUPS
    channel = lax.broadcasted_iota(jnp.int32, shape, channel_dim)
    lane = lax.broadcasted_iota(jnp.int32, shape, 1 - channel_dim)
    return jnp.where(channel // size == lane % GROUPS, 1.0, 0.0).astype(jnp.bfloat16)


def slot_lanes(samples):
    row = lax.broadcasted_iota(jnp.int32, (samples, LANES), 0)
    lane = lax.broadcasted_iota(jnp.int32, (samples, LANES), 1)
    return lane // GROUPS == row % (LANES // GROUPS)


def store_group_stats(sums_ref, squares_ref, count, out_ref):
    samples, channels = sums_ref.shape
    slots = LANES // GROUPS
    size = channels // GROUPS
    own = slot_lanes(samples)
    fold = selection_matrix((channels, LANES), 0, channels)
    spread = selection_matrix((LANES, channels), 1, channels)
    per_channel = jnp.maximum(count, 1.0)
    sums = sums_ref[...]

    def packed(value):
        return jnp.where(own, value, 0.0).reshape(samples // slots, slots, LANES).sum(axis=1)

    group_sum = exact_dot(sums, fold)
    centre = exact_dot(jnp.where(own, group_sum, 0.0), spread) / (per_channel * size)
    offset = sums / per_channel - centre
    group_squares = exact_dot(squares_ref[...] + count * offset * offset, fold)
    out_ref[0] = packed(group_sum)
    out_ref[1] = packed(group_squares)
    out_ref[2] = jnp.full(out_ref.shape[1:], count * size, jnp.float32)


def row_statistics(rows, limits, count, sums_ref, squares_ref, b):
    some = 16
    cols, channels = rows(0, None).shape
    column = lax.broadcasted_iota(jnp.int32, (cols, channels), 0)
    few = sum(jnp.minimum(limit, some) for limit in limits).astype(jnp.float32)
    total = jnp.zeros((some, channels), jnp.float32)
    for h in range(len(limits)):
        total = total + jnp.where(column[:some] < limits[h], rows(h, some), 0.0)
    pivot = total.sum(axis=0, keepdims=True) / jnp.maximum(few, 1.0)
    first = jnp.zeros((cols, channels), jnp.float32)
    second = jnp.zeros((cols, channels), jnp.float32)
    for h in range(len(limits)):
        value = jnp.where(column < limits[h], rows(h, None) - pivot, 0.0)
        first = first + value
        second = second + value * value
    moved = first.sum(axis=0, keepdims=True)
    squares = second.sum(axis=0, keepdims=True) - moved * moved / jnp.maximum(count, 1.0)
    sums_ref[pl.ds(b, 1)] = moved + count * pivot
    squares_ref[pl.ds(b, 1)] = jnp.maximum(squares, 0.0)


def tile_position():
    lat = lax.axis_index("zh") * lax.axis_size("core") + lax.axis_index("core")
    lon = (lax.axis_index("y") * lax.axis_size("zl") + lax.axis_index("zl")) * lax.axis_size("x")
    return lat, lon + lax.axis_index("x")


def row_points(points_ref, lat, rows, e):
    row = lat * rows + e
    if 0 <= e < rows:
        return points_ref[row]
    total = points_ref.shape[0]
    inside = (row >= 0) & (row < total)
    return jnp.where(inside, points_ref[jnp.clip(row, 0, total - 1)], 0)


def live_limits(points_ref, rows, cols):
    lat, lon = tile_position()
    return [jnp.clip(points_ref[lat * rows + h] - lon * cols, 0, cols) for h in range(rows)]


def live_count(limits):
    return functools.reduce(lambda a, c: a + c, limits).astype(jnp.float32)


def in_vmem():
    return pl.BlockSpec(memory_space=pltpu.VMEM)


def fetch(x_hbm_ref, x_ref, sems, b):
    return pltpu.make_async_copy(x_hbm_ref.at[b], x_ref.at[b], sems.at[b])


def pack_edges(x_ref, b, d, edges, k):
    _, rows, cols, _ = x_ref.shape
    first_row_ref, last_row_ref, first_col_ref, last_col_ref = edges
    first_row_ref[k] = x_ref[b, :d]
    last_row_ref[k] = x_ref[b, rows - d :]
    for h in range(rows):
        first_col_ref[k, h * d : (h + 1) * d] = x_ref[b, h, :d]
        last_col_ref[k, h * d : (h + 1) * d] = x_ref[b, h, cols - d :]


def edge_shapes(x, d):
    samples, rows, width, channels = x.shape
    shapes = [(samples, d, width, channels)] * 2 + [(samples, rows * d, channels)] * 2
    return [jax.ShapeDtypeStruct(shape, x.dtype) for shape in shapes]


def edge_specs(x, d, block):
    return [
        pl.BlockSpec((block, *e.shape[1:]), lambda g, *_, n=len(e.shape): (g,) + (0,) * (n - 1))
        for e in edge_shapes(x, d)
    ]


def stats_kernel(points_ref, x_hbm_ref, out_ref, *refs):
    *edges, x_ref, sems, sums_ref, squares_ref = refs
    g = pl.program_id(0)

    @pl.when(g == 0)
    def _():
        for b in range(x_ref.shape[0]):
            fetch(x_hbm_ref, x_ref, sems, b).start()

    fetch(x_hbm_ref, x_ref, sems, g).wait()
    _, rows, cols, _ = x_ref.shape
    limits = live_limits(points_ref, rows, cols)
    count = live_count(limits)
    row_statistics(
        lambda h, n: x_ref[g, h, :n].astype(jnp.float32), limits, count, sums_ref, squares_ref, g
    )
    pack_edges(x_ref, g, FIRST_DILATION, edges, 0)

    @pl.when(g == pl.num_programs(0) - 1)
    def _():
        store_group_stats(sums_ref, squares_ref, count, out_ref)


def local_statistics(x, points):
    samples, rows, width, channels = x.shape
    shape = (3, samples * GROUPS // LANES, LANES)
    return pl.pallas_call(
        stats_kernel,
        out_shape=[jax.ShapeDtypeStruct(shape, jnp.float32), *edge_shapes(x, FIRST_DILATION)],
        grid_spec=pltpu.PrefetchScalarGridSpec(
            num_scalar_prefetch=1,
            grid=(samples,),
            in_specs=[pl.BlockSpec(memory_space=pltpu.HBM)],
            out_specs=[
                pl.BlockSpec(shape, lambda g, *_: (0, 0, 0)),
                *edge_specs(x, FIRST_DILATION, 1),
            ],
            scratch_shapes=[
                pltpu.VMEM(x.shape, x.dtype),
                pltpu.SemaphoreType.DMA((samples,)),
                pltpu.VMEM((samples, channels), jnp.float32),
                pltpu.VMEM((samples, channels), jnp.float32),
            ],
        ),
        compiler_params=pltpu.CompilerParams(
            dimension_semantics=("arbitrary",), vmem_limit_bytes=58_000_000
        ),
        cost_estimate=pl.CostEstimate(
            flops=8 * x.size, bytes_accessed=2 * x.size, transcendentals=0
        ),
        name="stats",
    )(points, x)


def chip_counts(points, chips, rows, cols, size):
    total = points.shape[1]
    lons = chips // lax.axis_size("zh")
    chip = lax.broadcasted_iota(jnp.int32, (chips, total), 0)
    row = lax.broadcasted_iota(jnp.int32, (chips, total), 1)
    live = jnp.clip(points - (chip % lons) * cols, 0, cols)
    mine = row // (rows * lax.axis_size("core")) == chip // lons
    return jnp.where(mine, live, 0).astype(jnp.float32).sum(axis=1, keepdims=True) * size


def combine_kernel(rows, cols, parts_ref, points_ref, norm_ref):
    _, samples, channels = norm_ref.shape
    slots = LANES // GROUPS
    chips = parts_ref.shape[0]
    counts = chip_counts(points_ref[...], chips, rows, cols, channels // GROUPS)[:, None, :]
    sums = parts_ref[:, 0]
    squares = parts_ref[:, 1]
    count = counts.sum(axis=0)
    mean = sums.sum(axis=0) / count
    offset = sums / jnp.maximum(counts, 1.0) - mean[None]
    var = (squares + counts * offset * offset).sum(axis=0) / count
    half = 0.5 * lax.rsqrt(var + EPS)
    own = slot_lanes(samples)
    spread = selection_matrix((LANES, channels), 1, channels)

    def unpacked(value):
        rows = jnp.broadcast_to(value[:, None], (samples // slots, slots, LANES)).reshape(samples, LANES)
        return jnp.where(own, rows, 0.0)

    both = exact_dot(jnp.concatenate([unpacked(mean), unpacked(half)], axis=0), spread)
    norm_ref[0] = both[:samples]
    norm_ref[1] = both[samples:]


def combine_statistics(parts, points, x):
    samples, rows, cols, channels = x.shape
    return pl.pallas_call(
        functools.partial(combine_kernel, rows, cols),
        out_shape=jax.ShapeDtypeStruct((2, samples, channels), jnp.float32),
        in_specs=[in_vmem(), in_vmem()],
        out_specs=in_vmem(),
        compiler_params=pltpu.CompilerParams(vmem_limit_bytes=4_000_000),
        cost_estimate=pl.CostEstimate(flops=NORM_FLOPS, bytes_accessed=parts.size * 4, transcendentals=0),
        name="norm",
    )(parts, points[None])


def conv_kernel(dilation, chunk, which, with_stats, points_ref, flags_ref, norm_ref, *refs):
    d = dilation
    x_hbm_ref, top_ref, bottom_ref, left_ref, right_ref, w_ref, out_hbm_ref, *rest = refs
    if with_stats:
        stats_ref, *edges = rest[:5]
        x_ref, sems, out_ref, out_sems, even_ref, odd_ref, sums_ref, squares_ref, kept_ref = rest[5:]
    else:
        x_ref, sems, out_ref, out_sems, even_ref, odd_ref = rest
    g = pl.program_id(0)
    samples = norm_ref.shape[1]
    _, rows, cols, channels = x_ref.shape
    lat, lon = tile_position()
    lon_total = lax.axis_size(LON) * cols
    origin = lon * cols
    column = lax.broadcasted_iota(jnp.int32, (cols, channels), 0)
    edge = lax.broadcasted_iota(jnp.int32, (d, channels), 0)
    points = [row_points(points_ref, lat, rows, e - d) for e in range(rows + 2 * d)]
    limits = [jnp.clip(points[d + h] - origin, 0, cols) for h in range(rows)]
    before_origin = (origin + lon_total - d) % lon_total
    after_origin = (origin + cols) % lon_total

    def activate_rows(b, act_ref, lo, hi):
        mean = norm_ref[0, pl.ds(b, 1)]
        half = norm_ref[1, pl.ds(b, 1)]

        def activated(value):
            t = (value.astype(jnp.float32) - mean) * half
            return t + t * jnp.tanh(t)

        left = activated(left_ref[b, lo * d : hi * d])
        right = activated(right_ref[b, lo * d : hi * d])
        for e in range(lo, hi):
            if e < d:
                row = top_ref[b, e]
            elif e < rows + d:
                row = x_ref[b, e - d]
            else:
                row = bottom_ref[b, e - rows - d]
            at = slice((e - lo) * d, (e - lo + 1) * d)
            mid = jnp.where(column < points[e] - origin, activated(row), 0.0).astype(jnp.bfloat16)
            lhs = jnp.where(edge < points[e] - before_origin, left[at], 0.0).astype(jnp.bfloat16)
            rhs = jnp.where(edge < points[e] - after_origin, right[at], 0.0).astype(jnp.bfloat16)
            act_ref[e, d:, 0:channels] = mid[: cols - d]
            act_ref[e, :d, 0:channels] = lhs
            act_ref[e, :, channels : 2 * channels] = mid
            act_ref[e, : cols - d, 2 * channels :] = mid[d:]
            act_ref[e, cols - d :, 2 * channels :] = rhs

    def convolve_rows(k, scale, act_ref, start):
        acc = None
        for tap in range(3):
            lo = start + tap * d
            taken = act_ref[lo : lo + chunk].reshape(chunk * cols, 3 * channels)
            term = jnp.dot(taken, w_ref[tap], preferred_element_type=jnp.float32)
            acc = term if acc is None else acc + term
        base = x_ref[2 * g + k, start : start + chunk].astype(jnp.float32)
        result = (base + scale * acc.reshape(chunk, cols, channels)).astype(jnp.bfloat16)
        out_ref[2 * g + k, start : start + chunk] = result
        if with_stats and k == 1:
            kept_ref[start : start + chunk] = result

    def phase(k, act_ref, follow, next_ref):
        scale = flags_ref[which, 2 * g + k].astype(jnp.float32) * (1.0 / KEEP_RATE)
        steps = rows // chunk
        each = (rows + 2 * d) // steps
        for step in range(steps):
            last = rows + 2 * d if step == steps - 1 else (step + 1) * each
            activate_rows(follow, next_ref, step * each, last)
            convolve_rows(k, scale, act_ref, step * chunk)
        store(2 * g + k).start()
        if with_stats:
            pack_edges(out_ref, 2 * g + k, SECOND_DILATION, edges, k)

    def store(b):
        return pltpu.make_async_copy(out_ref.at[b], out_hbm_ref.at[b], out_sems.at[b])

    @pl.when(g == 0)
    def _():
        for b in range(samples):
            fetch(x_hbm_ref, x_ref, sems, b).start()
        fetch(x_hbm_ref, x_ref, sems, 0).wait()
        activate_rows(0, even_ref, 0, rows + 2 * d)
        if with_stats:
            kept_ref[...] = jnp.zeros_like(kept_ref)

    @pl.when(g < samples // 2 - 1)
    def _():
        fetch(x_hbm_ref, x_ref, sems, 2 * g + 2).wait()

    fetch(x_hbm_ref, x_ref, sems, 2 * g + 1).wait()
    count = live_count(limits)
    phase(0, even_ref, 2 * g + 1, odd_ref)
    if with_stats:
        row_statistics(
            lambda h, n: kept_ref[h, :n].astype(jnp.float32), limits, count, sums_ref, squares_ref, jnp.maximum(2 * g - 1, 0)
        )
    phase(1, odd_ref, jnp.minimum(2 * g + 2, samples - 1), even_ref)
    if with_stats:
        row_statistics(
            lambda h, n: out_ref[2 * g, h, :n].astype(jnp.float32), limits, count, sums_ref, squares_ref, 2 * g
        )

        @pl.when(g == pl.num_programs(0) - 1)
        def _():
            row_statistics(
                lambda h, n: out_ref[2 * g + 1, h, :n].astype(jnp.float32), limits, count, sums_ref, squares_ref, samples - 1
            )
            store_group_stats(sums_ref, squares_ref, count, stats_ref)

    @pl.when(g == pl.num_programs(0) - 1)
    def _():
        for b in range(samples):
            store(b).wait()


def convolve(x, halos, weight, norm, points, flags, dilation, which, with_stats):
    samples, rows, width, channels = x.shape
    d = dilation
    def whole(shape):
        return pl.BlockSpec(shape, lambda g, *_: (0,) * len(shape))

    out_shape = [jax.ShapeDtypeStruct(x.shape, jnp.bfloat16)]
    out_specs = [pl.BlockSpec(memory_space=pltpu.HBM)]
    act = pltpu.VMEM((rows + 2 * d, width, 3 * channels), jnp.bfloat16)
    scratch = [pltpu.VMEM(x.shape, x.dtype), pltpu.SemaphoreType.DMA((samples,))] * 2
    scratch += [act, act]
    if with_stats:
        shape = (3, samples * GROUPS // LANES, LANES)
        out_shape += [jax.ShapeDtypeStruct(shape, jnp.float32), *edge_shapes(x, SECOND_DILATION)]
        out_specs += [whole(shape), *edge_specs(x, SECOND_DILATION, 2)]
        scratch += [pltpu.VMEM((samples, channels), jnp.float32)] * 2
        scratch += [pltpu.VMEM((rows, width, channels), jnp.bfloat16)]
    return pl.pallas_call(
        functools.partial(conv_kernel, d, CHUNK, which, with_stats),
        out_shape=out_shape,
        grid_spec=pltpu.PrefetchScalarGridSpec(
            num_scalar_prefetch=2,
            grid=(samples // 2,),
            in_specs=[
                in_vmem(),
                pl.BlockSpec(memory_space=pltpu.HBM),
                *[in_vmem()] * len(halos),
                in_vmem(),
            ],
            out_specs=out_specs,
            scratch_shapes=scratch,
        ),
        compiler_params=pltpu.CompilerParams(
            dimension_semantics=("arbitrary",), vmem_limit_bytes=VMEM_LIMIT
        ),
        cost_estimate=pl.CostEstimate(
            flops=2 * x.size * 9 * channels, bytes_accessed=5 * x.size, transcendentals=2 * x.size
        ),
        name="conv%d" % d,
    )(points, flags, norm, x, *halos, weight)


def exchange_rows(edges):
    lat = lax.axis_size(LAT)
    top = lax.ppermute(edges[1], LAT, [(i, i + 1) for i in range(lat - 1)])
    bottom = lax.ppermute(edges[0], LAT, [(i + 1, i) for i in range(lat - 1)])
    return top, bottom


def exchange_columns(edges, top, bottom):
    samples, d, width, channels = top.shape
    lon = lax.axis_size(LON)

    def packed(cols, lo, hi):
        above = top[:, :, lo:hi].reshape(samples, d * d, channels)
        below = bottom[:, :, lo:hi].reshape(samples, d * d, channels)
        return jnp.concatenate([above, cols, below], axis=1)

    left = lax.ppermute(packed(edges[3], width - d, width), LON, [(i, (i + 1) % lon) for i in range(lon)])
    right = lax.ppermute(packed(edges[2], 0, d), LON, [((i + 1) % lon, i) for i in range(lon)])
    return left, right


def merge_cores(local):
    other = lax.ppermute(local, "core", [(0, 1), (1, 0)])
    own_count, other_count = local[2], other[2]
    both = jnp.maximum(own_count + other_count, 1.0)
    gap = local[0] / jnp.maximum(own_count, 1.0) - other[0] / jnp.maximum(other_count, 1.0)
    squares = local[1] + other[1] + gap * gap * (own_count * other_count / both)
    merged = jnp.stack([local[0] + other[0], squares])
    return jnp.broadcast_to(merged[None], (lax.axis_size(CHIPS), *merged.shape))


def exchange(local, edges, points, x):
    mine = merge_cores(local)
    top, bottom = exchange_rows(edges)
    norm = combine_statistics(lax.all_to_all(mine, CHIPS, 0, 0), points, x)
    return norm, (top, bottom, *exchange_columns(edges, top, bottom))


def per_device(features, band_points, survival_flags, first_kernel_weight, second_kernel_weight):
    channels = features.shape[3]
    flags = survival_flags.T
    first_weight = first_kernel_weight.reshape(3, 3 * channels, channels)
    second_weight = second_kernel_weight.reshape(3, 3 * channels, channels)
    local, *edges = local_statistics(features, band_points)
    norm, halos = exchange(local, edges, band_points, features)
    first, local, *edges = convolve(
        features, halos, first_weight, norm, band_points, flags, FIRST_DILATION, 0, True
    )
    norm, halos = exchange(local, edges, band_points, first)
    (section,) = convolve(
        first, halos, second_weight, norm, band_points, flags, SECOND_DILATION, 1, False
    )
    return section


def solution(mesh):
    grid = Mesh(mesh.devices.reshape(2, 2, 4, 2, 4), (LAT + LON))
    spec = P(None, LAT, LON, None)
    return jax.shard_map(
        per_device, mesh=grid, in_specs=(spec, P(), P(), P(), P()), out_specs=spec, check_vma=False
    )
```

```python
import functools

import jax
import jax.numpy as jnp
from jax import lax
from jax.experimental import pallas as pl
from jax.experimental.pallas import tpu as pltpu
from jax.sharding import Mesh, PartitionSpec as P

GROUPS = 32
FIRST_DILATION = 2
SECOND_DILATION = 4
EPS = 1e-05
KEEP_RATE = 0.8

LAT = ("zh", "core")
LON = ("y", "zl", "x")
CHIPS = ("zh", "y", "zl", "x")
LANES = 128
VMEM_LIMIT = 52_000_000
CHUNK = 8
NORM_FLOPS = 10 * 10**9


def exact_dot(a, selection):
    high = a.astype(jnp.bfloat16)
    rest = a - high.astype(jnp.float32)
    middle = rest.astype(jnp.bfloat16)
    low = (rest - middle.astype(jnp.float32)).astype(jnp.bfloat16)
    m = a.shape[0]
    parts = jnp.concatenate([high.astype(jnp.float32), middle.astype(jnp.float32), low.astype(jnp.float32)], axis=0)
    terms = jnp.dot(parts.astype(jnp.bfloat16), selection, preferred_element_type=jnp.float32)
    return terms[:m] + terms[m : 2 * m] + terms[2 * m :]


def selection_matrix(shape, channel_dim, channels):
    size = channels // GROUPS
    channel = lax.broadcasted_iota(jnp.int32, shape, channel_dim)
    lane = lax.broadcasted_iota(jnp.int32, shape, 1 - channel_dim)
    return jnp.where(channel // size == lane % GROUPS, 1.0, 0.0).astype(jnp.bfloat16)


def slot_lanes(samples):
    row = lax.broadcasted_iota(jnp.int32, (samples, LANES), 0)
    lane = lax.broadcasted_iota(jnp.int32, (samples, LANES), 1)
    return lane // GROUPS == row % (LANES // GROUPS)


def store_group_stats(sums_ref, squares_ref, count, out_ref):
    samples, channels = sums_ref.shape
    slots = LANES // GROUPS
    size = channels // GROUPS
    own = slot_lanes(samples)
    fold = selection_matrix((channels, LANES), 0, channels)
    spread = selection_matrix((LANES, channels), 1, channels)
    per_channel = jnp.maximum(count, 1.0)
    sums = sums_ref[...]

    def packed(value):
        return jnp.where(own, value, 0.0).reshape(samples // slots, slots, LANES).sum(axis=1)

    group_sum = exact_dot(sums, fold)
    centre = exact_dot(jnp.where(own, group_sum, 0.0), spread) / (per_channel * size)
    offset = sums / per_channel - centre
    group_squares = exact_dot(squares_ref[...] + count * offset * offset, fold)
    out_ref[0] = packed(group_sum)
    out_ref[1] = packed(group_squares)
    out_ref[2] = jnp.full(out_ref.shape[1:], count * size, jnp.float32)


def row_statistics(rows, limits, count, sums_ref, squares_ref, b):
    some = 16
    cols, channels = rows(0, None).shape
    column = lax.broadcasted_iota(jnp.int32, (cols, channels), 0)
    few = sum(jnp.minimum(limit, some) for limit in limits).astype(jnp.float32)
    total = jnp.zeros((some, channels), jnp.float32)
    for h in range(len(limits)):
        total = total + jnp.where(column[:some] < limits[h], rows(h, some), 0.0)
    pivot = total.sum(axis=0, keepdims=True) / jnp.maximum(few, 1.0)
    first = jnp.zeros((cols, channels), jnp.float32)
    second = jnp.zeros((cols, channels), jnp.float32)
    for h in range(len(limits)):
        value = jnp.where(column < limits[h], rows(h, None) - pivot, 0.0)
        first = first + value
        second = second + value * value
    moved = first.sum(axis=0, keepdims=True)
    squares = second.sum(axis=0, keepdims=True) - moved * moved / jnp.maximum(count, 1.0)
    sums_ref[pl.ds(b, 1)] = moved + count * pivot
    squares_ref[pl.ds(b, 1)] = jnp.maximum(squares, 0.0)


def tile_position():
    lat = lax.axis_index("zh") * lax.axis_size("core") + lax.axis_index("core")
    lon = (lax.axis_index("y") * lax.axis_size("zl") + lax.axis_index("zl")) * lax.axis_size("x")
    return lat, lon + lax.axis_index("x")


def row_points(points_ref, lat, rows, e):
    row = lat * rows + e
    if 0 <= e < rows:
        return points_ref[row]
    total = points_ref.shape[0]
    inside = (row >= 0) & (row < total)
    return jnp.where(inside, points_ref[jnp.clip(row, 0, total - 1)], 0)


def live_limits(points_ref, rows, cols):
    lat, lon = tile_position()
    return [jnp.clip(points_ref[lat * rows + h] - lon * cols, 0, cols) for h in range(rows)]


def live_count(limits):
    return functools.reduce(lambda a, c: a + c, limits).astype(jnp.float32)


def in_vmem():
    return pl.BlockSpec(memory_space=pltpu.VMEM)


def fetch(x_hbm_ref, x_ref, sems, b):
    return pltpu.make_async_copy(x_hbm_ref.at[b], x_ref.at[b], sems.at[b])


def pack_edges(x_ref, b, d, edges, k):
    _, rows, cols, _ = x_ref.shape
    first_row_ref, last_row_ref, first_col_ref, last_col_ref = edges
    first_row_ref[k] = x_ref[b, :d]
    last_row_ref[k] = x_ref[b, rows - d :]
    for h in range(rows):
        first_col_ref[k, h * d : (h + 1) * d] = x_ref[b, h, :d]
        last_col_ref[k, h * d : (h + 1) * d] = x_ref[b, h, cols - d :]


def edge_shapes(x, d):
    samples, rows, width, channels = x.shape
    shapes = [(samples, d, width, channels)] * 2 + [(samples, rows * d, channels)] * 2
    return [jax.ShapeDtypeStruct(shape, x.dtype) for shape in shapes]


def edge_specs(x, d, block):
    return [
        pl.BlockSpec((block, *e.shape[1:]), lambda g, *_, n=len(e.shape): (g,) + (0,) * (n - 1))
        for e in edge_shapes(x, d)
    ]


def stats_kernel(points_ref, x_hbm_ref, out_ref, *refs):
    *edges, x_ref, sems, sums_ref, squares_ref = refs
    g = pl.program_id(0)

    @pl.when(g == 0)
    def _():
        for b in range(x_ref.shape[0]):
            fetch(x_hbm_ref, x_ref, sems, b).start()

    fetch(x_hbm_ref, x_ref, sems, g).wait()
    _, rows, cols, _ = x_ref.shape
    limits = live_limits(points_ref, rows, cols)
    count = live_count(limits)
    row_statistics(
        lambda h, n: x_ref[g, h, :n].astype(jnp.float32), limits, count, sums_ref, squares_ref, g
    )
    pack_edges(x_ref, g, FIRST_DILATION, edges, 0)

    @pl.when(g == pl.num_programs(0) - 1)
    def _():
        store_group_stats(sums_ref, squares_ref, count, out_ref)


def local_statistics(x, points):
    samples, rows, width, channels = x.shape
    shape = (3, samples * GROUPS // LANES, LANES)
    return pl.pallas_call(
        stats_kernel,
        out_shape=[jax.ShapeDtypeStruct(shape, jnp.float32), *edge_shapes(x, FIRST_DILATION)],
        grid_spec=pltpu.PrefetchScalarGridSpec(
            num_scalar_prefetch=1,
            grid=(samples,),
            in_specs=[pl.BlockSpec(memory_space=pltpu.HBM)],
            out_specs=[
                pl.BlockSpec(shape, lambda g, *_: (0, 0, 0)),
                *edge_specs(x, FIRST_DILATION, 1),
            ],
            scratch_shapes=[
                pltpu.VMEM(x.shape, x.dtype),
                pltpu.SemaphoreType.DMA((samples,)),
                pltpu.VMEM((samples, channels), jnp.float32),
                pltpu.VMEM((samples, channels), jnp.float32),
            ],
        ),
        compiler_params=pltpu.CompilerParams(
            dimension_semantics=("arbitrary",), vmem_limit_bytes=58_000_000
        ),
        cost_estimate=pl.CostEstimate(
            flops=8 * x.size, bytes_accessed=2 * x.size, transcendentals=0
        ),
        name="stats",
    )(points, x)


def chip_counts(points, chips, rows, cols, size):
    total = points.shape[1]
    lons = chips // lax.axis_size("zh")
    chip = lax.broadcasted_iota(jnp.int32, (chips, total), 0)
    row = lax.broadcasted_iota(jnp.int32, (chips, total), 1)
    live = jnp.clip(points - (chip % lons) * cols, 0, cols)
    mine = row // (rows * lax.axis_size("core")) == chip // lons
    return jnp.where(mine, live, 0).astype(jnp.float32).sum(axis=1, keepdims=True) * size


def combine_kernel(rows, cols, parts_ref, points_ref, norm_ref):
    _, samples, channels = norm_ref.shape
    slots = LANES // GROUPS
    chips = parts_ref.shape[0]
    counts = chip_counts(points_ref[...], chips, rows, cols, channels // GROUPS)[:, None, :]
    sums = parts_ref[:, 0]
    squares = parts_ref[:, 1]
    count = counts.sum(axis=0)
    mean = sums.sum(axis=0) / count
    offset = sums / jnp.maximum(counts, 1.0) - mean[None]
    var = (squares + counts * offset * offset).sum(axis=0) / count
    half = 0.5 * lax.rsqrt(var + EPS)
    own = slot_lanes(samples)
    spread = selection_matrix((LANES, channels), 1, channels)

    def unpacked(value):
        rows = jnp.broadcast_to(value[:, None], (samples // slots, slots, LANES)).reshape(samples, LANES)
        return jnp.where(own, rows, 0.0)

    both = exact_dot(jnp.concatenate([unpacked(mean), unpacked(half)], axis=0), spread)
    norm_ref[0] = both[:samples]
    norm_ref[1] = both[samples:]


def combine_statistics(parts, points, x):
    samples, rows, cols, channels = x.shape
    return pl.pallas_call(
        functools.partial(combine_kernel, rows, cols),
        out_shape=jax.ShapeDtypeStruct((2, samples, channels), jnp.float32),
        in_specs=[in_vmem(), in_vmem()],
        out_specs=in_vmem(),
        compiler_params=pltpu.CompilerParams(vmem_limit_bytes=4_000_000),
        cost_estimate=pl.CostEstimate(flops=NORM_FLOPS, bytes_accessed=parts.size * 4, transcendentals=0),
        name="norm",
    )(parts, points[None])


def conv_kernel(dilation, chunk, which, with_stats, ends, points_ref, flags_ref, norm_ref, *refs):
    d = dilation
    x_hbm_ref, top_ref, bottom_ref, left_ref, right_ref, *refs = refs
    left_end_ref = right_end_ref = None
    if ends:
        left_end_ref, right_end_ref, *refs = refs
    w_ref, out_hbm_ref, *rest = refs
    if with_stats:
        stats_ref, *edges = rest[:5]
        x_ref, sems, out_ref, out_sems, even_ref, odd_ref, sums_ref, squares_ref, kept_ref = rest[5:]
    else:
        x_ref, sems, out_ref, out_sems, even_ref, odd_ref = rest
    g = pl.program_id(0)
    samples = norm_ref.shape[1]
    _, rows, cols, channels = x_ref.shape
    lat, lon = tile_position()
    lon_total = lax.axis_size(LON) * cols
    origin = lon * cols
    column = lax.broadcasted_iota(jnp.int32, (cols, channels), 0)
    edge = lax.broadcasted_iota(jnp.int32, (d, channels), 0)
    points = [row_points(points_ref, lat, rows, e - d) for e in range(rows + 2 * d)]
    limits = [jnp.clip(points[d + h] - origin, 0, cols) for h in range(rows)]
    before_origin = (origin + lon_total - d) % lon_total
    after_origin = (origin + cols) % lon_total

    def beside(side_ref, end_ref, b, lo, hi):
        if end_ref is None:
            return side_ref[b, lo * d : hi * d]
        above, below = min(hi, d), max(lo, rows + d)
        pieces = [
            end_ref[b, lo * d : above * d] if lo < above else None,
            side_ref[b, (max(lo, d) - d) * d : (min(hi, rows + d) - d) * d],
            end_ref[b, (below - rows) * d : (hi - rows) * d] if below < hi else None,
        ]
        return jnp.concatenate([p.astype(jnp.float32) for p in pieces if p is not None], axis=0)

    def activate_rows(b, act_ref, lo, hi):
        mean = norm_ref[0, pl.ds(b, 1)]
        half = norm_ref[1, pl.ds(b, 1)]

        def activated(value):
            t = (value.astype(jnp.float32) - mean) * half
            return t + t * jnp.tanh(t)

        left = activated(beside(left_ref, left_end_ref, b, lo, hi))
        right = activated(beside(right_ref, right_end_ref, b, lo, hi))
        for e in range(lo, hi):
            if e < d:
                row = top_ref[b, e]
            elif e < rows + d:
                row = x_ref[b, e - d]
            else:
                row = bottom_ref[b, e - rows - d]
            at = slice((e - lo) * d, (e - lo + 1) * d)
            mid = jnp.where(column < points[e] - origin, activated(row), 0.0).astype(jnp.bfloat16)
            lhs = jnp.where(edge < points[e] - before_origin, left[at], 0.0).astype(jnp.bfloat16)
            rhs = jnp.where(edge < points[e] - after_origin, right[at], 0.0).astype(jnp.bfloat16)
            act_ref[e, d:, 0:channels] = mid[: cols - d]
            act_ref[e, :d, 0:channels] = lhs
            act_ref[e, :, channels : 2 * channels] = mid
            act_ref[e, : cols - d, 2 * channels :] = mid[d:]
            act_ref[e, cols - d :, 2 * channels :] = rhs

    def convolve_rows(k, scale, act_ref, start):
        acc = None
        for tap in range(3):
            lo = start + tap * d
            taken = act_ref[lo : lo + chunk].reshape(chunk * cols, 3 * channels)
            term = jnp.dot(taken, w_ref[tap], preferred_element_type=jnp.float32)
            acc = term if acc is None else acc + term
        base = x_ref[2 * g + k, start : start + chunk].astype(jnp.float32)
        result = (base + scale * acc.reshape(chunk, cols, channels)).astype(jnp.bfloat16)
        out_ref[2 * g + k, start : start + chunk] = result
        if with_stats and k == 1:
            kept_ref[start : start + chunk] = result

    def phase(k, act_ref, follow, next_ref):
        scale = flags_ref[which, 2 * g + k].astype(jnp.float32) * (1.0 / KEEP_RATE)
        steps = rows // chunk
        each = (rows + 2 * d) // steps
        for step in range(steps):
            last = rows + 2 * d if step == steps - 1 else (step + 1) * each
            activate_rows(follow, next_ref, step * each, last)
            convolve_rows(k, scale, act_ref, step * chunk)
        store(2 * g + k).start()
        if with_stats:
            pack_edges(out_ref, 2 * g + k, SECOND_DILATION, edges, k)

    def store(b):
        return pltpu.make_async_copy(out_ref.at[b], out_hbm_ref.at[b], out_sems.at[b])

    @pl.when(g == 0)
    def _():
        for b in range(samples):
            fetch(x_hbm_ref, x_ref, sems, b).start()
        fetch(x_hbm_ref, x_ref, sems, 0).wait()
        activate_rows(0, even_ref, 0, rows + 2 * d)
        if with_stats:
            kept_ref[...] = jnp.zeros_like(kept_ref)

    @pl.when(g < samples // 2 - 1)
    def _():
        fetch(x_hbm_ref, x_ref, sems, 2 * g + 2).wait()

    fetch(x_hbm_ref, x_ref, sems, 2 * g + 1).wait()
    count = live_count(limits)
    phase(0, even_ref, 2 * g + 1, odd_ref)
    if with_stats:
        row_statistics(
            lambda h, n: kept_ref[h, :n].astype(jnp.float32), limits, count, sums_ref, squares_ref, jnp.maximum(2 * g - 1, 0)
        )
    phase(1, odd_ref, jnp.minimum(2 * g + 2, samples - 1), even_ref)
    if with_stats:
        row_statistics(
            lambda h, n: out_ref[2 * g, h, :n].astype(jnp.float32), limits, count, sums_ref, squares_ref, 2 * g
        )

        @pl.when(g == pl.num_programs(0) - 1)
        def _():
            row_statistics(
                lambda h, n: out_ref[2 * g + 1, h, :n].astype(jnp.float32), limits, count, sums_ref, squares_ref, samples - 1
            )
            store_group_stats(sums_ref, squares_ref, count, stats_ref)

    @pl.when(g == pl.num_programs(0) - 1)
    def _():
        for b in range(samples):
            store(b).wait()


def convolve(x, halos, weight, norm, points, flags, dilation, which, with_stats):
    samples, rows, width, channels = x.shape
    d = dilation
    def whole(shape):
        return pl.BlockSpec(shape, lambda g, *_: (0,) * len(shape))

    out_shape = [jax.ShapeDtypeStruct(x.shape, jnp.bfloat16)]
    out_specs = [pl.BlockSpec(memory_space=pltpu.HBM)]
    act = pltpu.VMEM((rows + 2 * d, width, 3 * channels), jnp.bfloat16)
    scratch = [pltpu.VMEM(x.shape, x.dtype), pltpu.SemaphoreType.DMA((samples,))] * 2
    scratch += [act, act]
    if with_stats:
        shape = (3, samples * GROUPS // LANES, LANES)
        out_shape += [jax.ShapeDtypeStruct(shape, jnp.float32), *edge_shapes(x, SECOND_DILATION)]
        out_specs += [whole(shape), *edge_specs(x, SECOND_DILATION, 2)]
        scratch += [pltpu.VMEM((samples, channels), jnp.float32)] * 2
        scratch += [pltpu.VMEM((rows, width, channels), jnp.bfloat16)]
    return pl.pallas_call(
        functools.partial(conv_kernel, d, CHUNK, which, with_stats, len(halos) > 4),
        out_shape=out_shape,
        grid_spec=pltpu.PrefetchScalarGridSpec(
            num_scalar_prefetch=2,
            grid=(samples // 2,),
            in_specs=[
                in_vmem(),
                pl.BlockSpec(memory_space=pltpu.HBM),
                *[in_vmem()] * len(halos),
                in_vmem(),
            ],
            out_specs=out_specs,
            scratch_shapes=scratch,
        ),
        compiler_params=pltpu.CompilerParams(
            dimension_semantics=("arbitrary",), vmem_limit_bytes=VMEM_LIMIT
        ),
        cost_estimate=pl.CostEstimate(
            flops=2 * x.size * 9 * channels, bytes_accessed=5 * x.size, transcendentals=2 * x.size
        ),
        name="conv%d" % d,
    )(points, flags, norm, x, *halos, weight)


def exchange_rows(edges):
    lat = lax.axis_size(LAT)
    top = lax.ppermute(edges[1], LAT, [(i, i + 1) for i in range(lat - 1)])
    bottom = lax.ppermute(edges[0], LAT, [(i + 1, i) for i in range(lat - 1)])
    return top, bottom


def exchange_columns(edges, top, bottom):
    samples, d, width, channels = top.shape
    lon = lax.axis_size(LON)

    def packed(cols, lo, hi):
        above = top[:, :, lo:hi].reshape(samples, d * d, channels)
        below = bottom[:, :, lo:hi].reshape(samples, d * d, channels)
        return jnp.concatenate([above, cols, below], axis=1)

    left = lax.ppermute(packed(edges[3], width - d, width), LON, [(i, (i + 1) % lon) for i in range(lon)])
    right = lax.ppermute(packed(edges[2], 0, d), LON, [((i + 1) % lon, i) for i in range(lon)])
    return left, right


def merge_cores(local):
    other = lax.ppermute(local, "core", [(0, 1), (1, 0)])
    own_count, other_count = local[2], other[2]
    both = jnp.maximum(own_count + other_count, 1.0)
    gap = local[0] / jnp.maximum(own_count, 1.0) - other[0] / jnp.maximum(other_count, 1.0)
    squares = local[1] + other[1] + gap * gap * (own_count * other_count / both)
    merged = jnp.stack([local[0] + other[0], squares])
    return jnp.broadcast_to(merged[None], (lax.axis_size(CHIPS), *merged.shape))


def exchange_apart(edges):
    lon = lax.axis_size(LON)
    east = [(i, (i + 1) % lon) for i in range(lon)]
    west = [((i + 1) % lon, i) for i in range(lon)]
    top, bottom = exchange_rows(edges)
    left = lax.ppermute(edges[3], LON, east)
    right = lax.ppermute(edges[2], LON, west)
    top, bottom, left, right = lax.optimization_barrier((top, bottom, left, right))
    samples, d, width, channels = top.shape

    def packed(lo, hi):
        above = top[:, :, lo:hi].reshape(samples, d * d, channels)
        below = bottom[:, :, lo:hi].reshape(samples, d * d, channels)
        return jnp.concatenate([above, below], axis=1)

    left_end = lax.ppermute(packed(width - d, width), LON, east)
    right_end = lax.ppermute(packed(0, d), LON, west)
    return top, bottom, left, right, left_end, right_end


def exchange_late(local, edges, points, x):
    mine = merge_cores(local)
    norm = combine_statistics(lax.all_to_all(mine, CHIPS, 0, 0), points, x)
    return norm, exchange_apart(edges)


def exchange(local, edges, points, x):
    mine = merge_cores(local)
    top, bottom = exchange_rows(edges)
    norm = combine_statistics(lax.all_to_all(mine, CHIPS, 0, 0), points, x)
    return norm, (top, bottom, *exchange_columns(edges, top, bottom))


def per_device(features, band_points, survival_flags, first_kernel_weight, second_kernel_weight):
    channels = features.shape[3]
    flags = survival_flags.T
    first_weight = first_kernel_weight.reshape(3, 3 * channels, channels)
    second_weight = second_kernel_weight.reshape(3, 3 * channels, channels)
    local, *edges = local_statistics(features, band_points)
    norm, halos = exchange(local, edges, band_points, features)
    first, local, *edges = convolve(
        features, halos, first_weight, norm, band_points, flags, FIRST_DILATION, 0, True
    )
    norm, halos = exchange_late(local, edges, band_points, first)
    (section,) = convolve(
        first, halos, second_weight, norm, band_points, flags, SECOND_DILATION, 1, False
    )
    return section


def solution(mesh):
    grid = Mesh(mesh.devices.reshape(2, 2, 4, 2, 4), (LAT + LON))
    spec = P(None, LAT, LON, None)
    return jax.shard_map(
        per_device, mesh=grid, in_specs=(spec, P(), P(), P(), P()), out_specs=spec, check_vma=False
    )
```

```python
import functools

import jax
import jax.numpy as jnp
from jax import lax
from jax.experimental import pallas as pl
from jax.experimental.pallas import tpu as pltpu
from jax.sharding import Mesh, PartitionSpec as P

GROUPS = 32
FIRST_DILATION = 2
SECOND_DILATION = 4
EPS = 1e-05
KEEP_RATE = 0.8

LAT = ("zh", "core")
LON = ("y", "zl", "x")
CHIPS = ("zh", "y", "zl", "x")
LANES = 128
VMEM_LIMIT = 52_000_000
CHUNK = 8


def exact_dot(a, selection):
    high = a.astype(jnp.bfloat16)
    rest = a - high.astype(jnp.float32)
    middle = rest.astype(jnp.bfloat16)
    low = (rest - middle.astype(jnp.float32)).astype(jnp.bfloat16)
    m = a.shape[0]
    parts = jnp.concatenate([high.astype(jnp.float32), middle.astype(jnp.float32), low.astype(jnp.float32)], axis=0)
    terms = jnp.dot(parts.astype(jnp.bfloat16), selection, preferred_element_type=jnp.float32)
    return terms[:m] + terms[m : 2 * m] + terms[2 * m :]


def selection_matrix(shape, channel_dim, channels):
    size = channels // GROUPS
    channel = lax.broadcasted_iota(jnp.int32, shape, channel_dim)
    lane = lax.broadcasted_iota(jnp.int32, shape, 1 - channel_dim)
    return jnp.where(channel // size == lane % GROUPS, 1.0, 0.0).astype(jnp.bfloat16)


def slot_lanes(samples):
    row = lax.broadcasted_iota(jnp.int32, (samples, LANES), 0)
    lane = lax.broadcasted_iota(jnp.int32, (samples, LANES), 1)
    return lane // GROUPS == row % (LANES // GROUPS)


def store_group_stats(sums_ref, squares_ref, count, out_ref):
    samples, channels = sums_ref.shape
    slots = LANES // GROUPS
    size = channels // GROUPS
    own = slot_lanes(samples)
    fold = selection_matrix((channels, LANES), 0, channels)
    spread = selection_matrix((LANES, channels), 1, channels)
    per_channel = jnp.maximum(count, 1.0)
    sums = sums_ref[...]

    def packed(value):
        return jnp.where(own, value, 0.0).reshape(samples // slots, slots, LANES).sum(axis=1)

    group_sum = exact_dot(sums, fold)
    centre = exact_dot(jnp.where(own, group_sum, 0.0), spread) / (per_channel * size)
    offset = sums / per_channel - centre
    group_squares = exact_dot(squares_ref[...] + count * offset * offset, fold)
    out_ref[0] = packed(group_sum)
    out_ref[1] = packed(group_squares)
    out_ref[2] = jnp.full(out_ref.shape[1:], count * size, jnp.float32)


def row_statistics(rows, limits, count, sums_ref, squares_ref, b):
    some = 16
    cols, channels = rows(0, None).shape
    column = lax.broadcasted_iota(jnp.int32, (cols, channels), 0)
    few = sum(jnp.minimum(limit, some) for limit in limits).astype(jnp.float32)
    total = jnp.zeros((some, channels), jnp.float32)
    for h in range(len(limits)):
        total = total + jnp.where(column[:some] < limits[h], rows(h, some), 0.0)
    pivot = total.sum(axis=0, keepdims=True) / jnp.maximum(few, 1.0)
    first = jnp.zeros((cols, channels), jnp.float32)
    second = jnp.zeros((cols, channels), jnp.float32)
    for h in range(len(limits)):
        value = jnp.where(column < limits[h], rows(h, None) - pivot, 0.0)
        first = first + value
        second = second + value * value
    moved = first.sum(axis=0, keepdims=True)
    squares = second.sum(axis=0, keepdims=True) - moved * moved / jnp.maximum(count, 1.0)
    sums_ref[pl.ds(b, 1)] = moved + count * pivot
    squares_ref[pl.ds(b, 1)] = jnp.maximum(squares, 0.0)


def tile_position():
    lat = lax.axis_index("zh") * lax.axis_size("core") + lax.axis_index("core")
    lon = (lax.axis_index("y") * lax.axis_size("zl") + lax.axis_index("zl")) * lax.axis_size("x")
    return lat, lon + lax.axis_index("x")


def row_points(points_ref, lat, rows, e):
    row = lat * rows + e
    if 0 <= e < rows:
        return points_ref[row]
    total = points_ref.shape[0]
    inside = (row >= 0) & (row < total)
    return jnp.where(inside, points_ref[jnp.clip(row, 0, total - 1)], 0)


def live_limits(points_ref, rows, cols):
    lat, lon = tile_position()
    return [jnp.clip(points_ref[lat * rows + h] - lon * cols, 0, cols) for h in range(rows)]


def live_count(limits):
    return functools.reduce(lambda a, c: a + c, limits).astype(jnp.float32)


def in_vmem():
    return pl.BlockSpec(memory_space=pltpu.VMEM)


def fetch(x_hbm_ref, x_ref, sems, b):
    return pltpu.make_async_copy(x_hbm_ref.at[b], x_ref.at[b], sems.at[b])


def pack_edges(x_ref, b, d, edges, k):
    _, rows, cols, _ = x_ref.shape
    first_row_ref, last_row_ref, first_col_ref, last_col_ref = edges
    first_row_ref[k] = x_ref[b, :d]
    last_row_ref[k] = x_ref[b, rows - d :]
    for h in range(rows):
        first_col_ref[k, h * d : (h + 1) * d] = x_ref[b, h, :d]
        last_col_ref[k, h * d : (h + 1) * d] = x_ref[b, h, cols - d :]


def edge_shapes(x, d):
    samples, rows, width, channels = x.shape
    shapes = [(samples, d, width, channels)] * 2 + [(samples, rows * d, channels)] * 2
    return [jax.ShapeDtypeStruct(shape, x.dtype) for shape in shapes]


def edge_specs(x, d, block):
    return [
        pl.BlockSpec((block, *e.shape[1:]), lambda g, *_, n=len(e.shape): (g,) + (0,) * (n - 1))
        for e in edge_shapes(x, d)
    ]


def stats_kernel(points_ref, x_hbm_ref, out_ref, *refs):
    *edges, x_ref, sems, sums_ref, squares_ref = refs
    g = pl.program_id(0)

    @pl.when(g == 0)
    def _():
        for b in range(x_ref.shape[0]):
            fetch(x_hbm_ref, x_ref, sems, b).start()

    fetch(x_hbm_ref, x_ref, sems, g).wait()
    _, rows, cols, _ = x_ref.shape
    limits = live_limits(points_ref, rows, cols)
    count = live_count(limits)
    row_statistics(
        lambda h, n: x_ref[g, h, :n].astype(jnp.float32), limits, count, sums_ref, squares_ref, g
    )
    pack_edges(x_ref, g, FIRST_DILATION, edges, 0)

    @pl.when(g == pl.num_programs(0) - 1)
    def _():
        store_group_stats(sums_ref, squares_ref, count, out_ref)


def local_statistics(x, points):
    samples, rows, width, channels = x.shape
    shape = (3, samples * GROUPS // LANES, LANES)
    return pl.pallas_call(
        stats_kernel,
        out_shape=[jax.ShapeDtypeStruct(shape, jnp.float32), *edge_shapes(x, FIRST_DILATION)],
        grid_spec=pltpu.PrefetchScalarGridSpec(
            num_scalar_prefetch=1,
            grid=(samples,),
            in_specs=[pl.BlockSpec(memory_space=pltpu.HBM)],
            out_specs=[
                pl.BlockSpec(shape, lambda g, *_: (0, 0, 0)),
                *edge_specs(x, FIRST_DILATION, 1),
            ],
            scratch_shapes=[
                pltpu.VMEM(x.shape, x.dtype),
                pltpu.SemaphoreType.DMA((samples,)),
                pltpu.VMEM((samples, channels), jnp.float32),
                pltpu.VMEM((samples, channels), jnp.float32),
            ],
        ),
        compiler_params=pltpu.CompilerParams(
            dimension_semantics=("arbitrary",), vmem_limit_bytes=58_000_000
        ),
        cost_estimate=pl.CostEstimate(
            flops=8 * x.size, bytes_accessed=2 * x.size, transcendentals=0
        ),
        name="stats",
    )(points, x)


def chip_counts(points, chips, rows, cols, size):
    total = points.shape[1]
    lons = chips // lax.axis_size("zh")
    chip = lax.broadcasted_iota(jnp.int32, (chips, total), 0)
    row = lax.broadcasted_iota(jnp.int32, (chips, total), 1)
    live = jnp.clip(points - (chip % lons) * cols, 0, cols)
    mine = row // (rows * lax.axis_size("core")) == chip // lons
    return jnp.where(mine, live, 0).astype(jnp.float32).sum(axis=1, keepdims=True) * size


def combine_kernel(rows, cols, parts_ref, points_ref, norm_ref):
    _, samples, channels = norm_ref.shape
    slots = LANES // GROUPS
    chips = parts_ref.shape[0]
    counts = chip_counts(points_ref[...], chips, rows, cols, channels // GROUPS)[:, None, :]
    sums = parts_ref[:, 0]
    squares = parts_ref[:, 1]
    count = counts.sum(axis=0)
    mean = sums.sum(axis=0) / count
    offset = sums / jnp.maximum(counts, 1.0) - mean[None]
    var = (squares + counts * offset * offset).sum(axis=0) / count
    half = 0.5 * lax.rsqrt(var + EPS)
    own = slot_lanes(samples)
    spread = selection_matrix((LANES, channels), 1, channels)

    def unpacked(value):
        rows = jnp.broadcast_to(value[:, None], (samples // slots, slots, LANES)).reshape(samples, LANES)
        return jnp.where(own, rows, 0.0)

    both = exact_dot(jnp.concatenate([unpacked(mean), unpacked(half)], axis=0), spread)
    norm_ref[0] = both[:samples]
    norm_ref[1] = both[samples:]


def combine_statistics(parts, points, x, flops):
    samples, rows, cols, channels = x.shape
    return pl.pallas_call(
        functools.partial(combine_kernel, rows, cols),
        out_shape=jax.ShapeDtypeStruct((2, samples, channels), jnp.float32),
        in_specs=[in_vmem(), in_vmem()],
        out_specs=in_vmem(),
        compiler_params=pltpu.CompilerParams(vmem_limit_bytes=4_000_000),
        cost_estimate=pl.CostEstimate(flops=flops, bytes_accessed=parts.size * 4, transcendentals=0),
        name="norm",
    )(parts, points[None])


def conv_kernel(dilation, chunk, which, with_stats, points_ref, flags_ref, norm_ref, *refs):
    d = dilation
    x_hbm_ref, top_ref, bottom_ref, left_ref, right_ref, w_ref, out_hbm_ref, *rest = refs
    if with_stats:
        stats_ref, *edges = rest[:5]
        x_ref, sems, out_ref, out_sems, even_ref, odd_ref, sums_ref, squares_ref, kept_ref = rest[5:]
    else:
        x_ref, sems, out_ref, out_sems, even_ref, odd_ref = rest
    g = pl.program_id(0)
    samples = norm_ref.shape[1]
    _, rows, cols, channels = x_ref.shape
    lat, lon = tile_position()
    lon_total = lax.axis_size(LON) * cols
    origin = lon * cols
    column = lax.broadcasted_iota(jnp.int32, (cols, channels), 0)
    edge = lax.broadcasted_iota(jnp.int32, (d, channels), 0)
    points = [row_points(points_ref, lat, rows, e - d) for e in range(rows + 2 * d)]
    limits = [jnp.clip(points[d + h] - origin, 0, cols) for h in range(rows)]
    before_origin = (origin + lon_total - d) % lon_total
    after_origin = (origin + cols) % lon_total

    def activate_rows(b, act_ref, lo, hi):
        mean = norm_ref[0, pl.ds(b, 1)]
        half = norm_ref[1, pl.ds(b, 1)]

        def activated(value):
            t = (value.astype(jnp.float32) - mean) * half
            return t + t * jnp.tanh(t)

        left = activated(left_ref[b, lo * d : hi * d])
        right = activated(right_ref[b, lo * d : hi * d])
        for e in range(lo, hi):
            if e < d:
                row = top_ref[b, e]
            elif e < rows + d:
                row = x_ref[b, e - d]
            else:
                row = bottom_ref[b, e - rows - d]
            at = slice((e - lo) * d, (e - lo + 1) * d)
            mid = jnp.where(column < points[e] - origin, activated(row), 0.0).astype(jnp.bfloat16)
            lhs = jnp.where(edge < points[e] - before_origin, left[at], 0.0).astype(jnp.bfloat16)
            rhs = jnp.where(edge < points[e] - after_origin, right[at], 0.0).astype(jnp.bfloat16)
            act_ref[e, d:, 0:channels] = mid[: cols - d]
            act_ref[e, :d, 0:channels] = lhs
            act_ref[e, :, channels : 2 * channels] = mid
            act_ref[e, : cols - d, 2 * channels :] = mid[d:]
            act_ref[e, cols - d :, 2 * channels :] = rhs

    def convolve_rows(k, scale, act_ref, start):
        acc = None
        for tap in range(3):
            lo = start + tap * d
            taken = act_ref[lo : lo + chunk].reshape(chunk * cols, 3 * channels)
            term = jnp.dot(taken, w_ref[tap], preferred_element_type=jnp.float32)
            acc = term if acc is None else acc + term
        base = x_ref[2 * g + k, start : start + chunk].astype(jnp.float32)
        result = (base + scale * acc.reshape(chunk, cols, channels)).astype(jnp.bfloat16)
        out_ref[2 * g + k, start : start + chunk] = result
        if with_stats and k == 1:
            kept_ref[start : start + chunk] = result

    def phase(k, act_ref, follow, next_ref):
        scale = flags_ref[which, 2 * g + k].astype(jnp.float32) * (1.0 / KEEP_RATE)
        steps = rows // chunk
        each = (rows + 2 * d) // steps
        for step in range(steps):
            last = rows + 2 * d if step == steps - 1 else (step + 1) * each
            activate_rows(follow, next_ref, step * each, last)
            convolve_rows(k, scale, act_ref, step * chunk)
        store(2 * g + k).start()
        if with_stats:
            pack_edges(out_ref, 2 * g + k, SECOND_DILATION, edges, k)

    def store(b):
        return pltpu.make_async_copy(out_ref.at[b], out_hbm_ref.at[b], out_sems.at[b])

    @pl.when(g == 0)
    def _():
        for b in range(samples):
            fetch(x_hbm_ref, x_ref, sems, b).start()
        fetch(x_hbm_ref, x_ref, sems, 0).wait()
        activate_rows(0, even_ref, 0, rows + 2 * d)
        if with_stats:
            kept_ref[...] = jnp.zeros_like(kept_ref)

    @pl.when(g < samples // 2 - 1)
    def _():
        fetch(x_hbm_ref, x_ref, sems, 2 * g + 2).wait()

    fetch(x_hbm_ref, x_ref, sems, 2 * g + 1).wait()
    count = live_count(limits)
    phase(0, even_ref, 2 * g + 1, odd_ref)
    if with_stats:
        row_statistics(
            lambda h, n: kept_ref[h, :n].astype(jnp.float32), limits, count, sums_ref, squares_ref, jnp.maximum(2 * g - 1, 0)
        )
    phase(1, odd_ref, jnp.minimum(2 * g + 2, samples - 1), even_ref)
    if with_stats:
        row_statistics(
            lambda h, n: out_ref[2 * g, h, :n].astype(jnp.float32), limits, count, sums_ref, squares_ref, 2 * g
        )

        @pl.when(g == pl.num_programs(0) - 1)
        def _():
            row_statistics(
                lambda h, n: out_ref[2 * g + 1, h, :n].astype(jnp.float32), limits, count, sums_ref, squares_ref, samples - 1
            )
            store_group_stats(sums_ref, squares_ref, count, stats_ref)

    @pl.when(g == pl.num_programs(0) - 1)
    def _():
        for b in range(samples):
            store(b).wait()


def convolve(x, halos, weight, norm, points, flags, dilation, which, with_stats):
    samples, rows, width, channels = x.shape
    d = dilation
    def whole(shape):
        return pl.BlockSpec(shape, lambda g, *_: (0,) * len(shape))

    out_shape = [jax.ShapeDtypeStruct(x.shape, jnp.bfloat16)]
    out_specs = [pl.BlockSpec(memory_space=pltpu.HBM)]
    act = pltpu.VMEM((rows + 2 * d, width, 3 * channels), jnp.bfloat16)
    scratch = [pltpu.VMEM(x.shape, x.dtype), pltpu.SemaphoreType.DMA((samples,))] * 2
    scratch += [act, act]
    if with_stats:
        shape = (3, samples * GROUPS // LANES, LANES)
        out_shape += [jax.ShapeDtypeStruct(shape, jnp.float32), *edge_shapes(x, SECOND_DILATION)]
        out_specs += [whole(shape), *edge_specs(x, SECOND_DILATION, 2)]
        scratch += [pltpu.VMEM((samples, channels), jnp.float32)] * 2
        scratch += [pltpu.VMEM((rows, width, channels), jnp.bfloat16)]
    return pl.pallas_call(
        functools.partial(conv_kernel, d, CHUNK, which, with_stats),
        out_shape=out_shape,
        grid_spec=pltpu.PrefetchScalarGridSpec(
            num_scalar_prefetch=2,
            grid=(samples // 2,),
            in_specs=[
                in_vmem(),
                pl.BlockSpec(memory_space=pltpu.HBM),
                *[in_vmem()] * len(halos),
                in_vmem(),
            ],
            out_specs=out_specs,
            scratch_shapes=scratch,
        ),
        compiler_params=pltpu.CompilerParams(
            dimension_semantics=("arbitrary",), vmem_limit_bytes=VMEM_LIMIT
        ),
        cost_estimate=pl.CostEstimate(
            flops=2 * x.size * 9 * channels, bytes_accessed=5 * x.size, transcendentals=2 * x.size
        ),
        name="conv%d" % d,
    )(points, flags, norm, x, *halos, weight)


def exchange_rows(edges):
    lat = lax.axis_size(LAT)
    top = lax.ppermute(edges[1], LAT, [(i, i + 1) for i in range(lat - 1)])
    bottom = lax.ppermute(edges[0], LAT, [(i + 1, i) for i in range(lat - 1)])
    return top, bottom


def exchange_columns(edges, top, bottom):
    samples, d, width, channels = top.shape
    lon = lax.axis_size(LON)

    def packed(cols, lo, hi):
        above = top[:, :, lo:hi].reshape(samples, d * d, channels)
        below = bottom[:, :, lo:hi].reshape(samples, d * d, channels)
        return jnp.concatenate([above, cols, below], axis=1)

    left = lax.ppermute(packed(edges[3], width - d, width), LON, [(i, (i + 1) % lon) for i in range(lon)])
    right = lax.ppermute(packed(edges[2], 0, d), LON, [((i + 1) % lon, i) for i in range(lon)])
    return left, right


def merge_cores(local):
    other = lax.ppermute(local, "core", [(0, 1), (1, 0)])
    own_count, other_count = local[2], other[2]
    both = jnp.maximum(own_count + other_count, 1.0)
    gap = local[0] / jnp.maximum(own_count, 1.0) - other[0] / jnp.maximum(other_count, 1.0)
    squares = local[1] + other[1] + gap * gap * (own_count * other_count / both)
    merged = jnp.stack([local[0] + other[0], squares])
    return jnp.broadcast_to(merged[None], (lax.axis_size(CHIPS), *merged.shape))


def exchange_first(local, edges, points, x):
    mine = merge_cores(local)
    top, bottom = exchange_rows(edges)
    norm = combine_statistics(lax.all_to_all(mine, CHIPS, 0, 0), points, x, 10**10)
    return norm, (top, bottom, *exchange_columns(edges, top, bottom))


def exchange_second(local, edges, points, x):
    mine = merge_cores(local)
    mine, top, bottom = lax.optimization_barrier((mine, *exchange_rows(edges)))
    columns = exchange_columns(edges, top, bottom)
    norm = combine_statistics(lax.all_to_all(mine, CHIPS, 0, 0), points, x, 10**9)
    return norm, (top, bottom, *columns)


def per_device(features, band_points, survival_flags, first_kernel_weight, second_kernel_weight):
    channels = features.shape[3]
    flags = survival_flags.T
    first_weight = first_kernel_weight.reshape(3, 3 * channels, channels)
    second_weight = second_kernel_weight.reshape(3, 3 * channels, channels)
    local, *edges = local_statistics(features, band_points)
    norm, halos = exchange_first(local, edges, band_points, features)
    first, local, *edges = convolve(
        features, halos, first_weight, norm, band_points, flags, FIRST_DILATION, 0, True
    )
    norm, halos = exchange_second(local, edges, band_points, first)
    (section,) = convolve(
        first, halos, second_weight, norm, band_points, flags, SECOND_DILATION, 1, False
    )
    return section


def solution(mesh):
    grid = Mesh(mesh.devices.reshape(2, 2, 4, 2, 4), (LAT + LON))
    spec = P(None, LAT, LON, None)
    return jax.shard_map(
        per_device, mesh=grid, in_specs=(spec, P(), P(), P(), P()), out_specs=spec, check_vma=False
    )
```

```python
import functools

import jax
import jax.numpy as jnp
from jax import lax
from jax.experimental import pallas as pl
from jax.experimental.pallas import tpu as pltpu
from jax.sharding import Mesh, PartitionSpec as P

GROUPS = 32
FIRST_DILATION = 2
SECOND_DILATION = 4
EPS = 1e-05
KEEP_RATE = 0.8

LAT = ("zh", "core")
LON = ("y", "zl", "x")
CHIPS = ("zh", "y", "zl", "x")
LANES = 128
VMEM_LIMIT = 52_000_000
CHUNK = 8
NORM_FLOPS = 10 * 10**9


def exact_dot(a, selection):
    high = a.astype(jnp.bfloat16)
    rest = a - high.astype(jnp.float32)
    middle = rest.astype(jnp.bfloat16)
    low = (rest - middle.astype(jnp.float32)).astype(jnp.bfloat16)
    m = a.shape[0]
    parts = jnp.concatenate([high.astype(jnp.float32), middle.astype(jnp.float32), low.astype(jnp.float32)], axis=0)
    terms = jnp.dot(parts.astype(jnp.bfloat16), selection, preferred_element_type=jnp.float32)
    return terms[:m] + terms[m : 2 * m] + terms[2 * m :]


def selection_matrix(shape, channel_dim, channels):
    size = channels // GROUPS
    channel = lax.broadcasted_iota(jnp.int32, shape, channel_dim)
    lane = lax.broadcasted_iota(jnp.int32, shape, 1 - channel_dim)
    return jnp.where(channel // size == lane % GROUPS, 1.0, 0.0).astype(jnp.bfloat16)


def slot_lanes(samples):
    row = lax.broadcasted_iota(jnp.int32, (samples, LANES), 0)
    lane = lax.broadcasted_iota(jnp.int32, (samples, LANES), 1)
    return lane // GROUPS == row % (LANES // GROUPS)


def store_group_stats(sums_ref, squares_ref, count, out_ref):
    samples, channels = sums_ref.shape
    slots = LANES // GROUPS
    size = channels // GROUPS
    own = slot_lanes(samples)
    fold = selection_matrix((channels, LANES), 0, channels)
    spread = selection_matrix((LANES, channels), 1, channels)
    per_channel = jnp.maximum(count, 1.0)
    sums = sums_ref[...]

    def packed(value):
        return jnp.where(own, value, 0.0).reshape(samples // slots, slots, LANES).sum(axis=1)

    group_sum = exact_dot(sums, fold)
    centre = exact_dot(jnp.where(own, group_sum, 0.0), spread) / (per_channel * size)
    offset = sums / per_channel - centre
    group_squares = exact_dot(squares_ref[...] + count * offset * offset, fold)
    out_ref[0] = packed(group_sum)
    out_ref[1] = packed(group_squares)
    out_ref[2] = jnp.full(out_ref.shape[1:], count * size, jnp.float32)


def row_statistics(rows, limits, count, sums_ref, squares_ref, b):
    some = 16
    cols, channels = rows(0, None).shape
    column = lax.broadcasted_iota(jnp.int32, (cols, channels), 0)
    few = sum(jnp.minimum(limit, some) for limit in limits).astype(jnp.float32)
    total = jnp.zeros((some, channels), jnp.float32)
    for h in range(len(limits)):
        total = total + jnp.where(column[:some] < limits[h], rows(h, some), 0.0)
    pivot = total.sum(axis=0, keepdims=True) / jnp.maximum(few, 1.0)
    first = jnp.zeros((cols, channels), jnp.float32)
    second = jnp.zeros((cols, channels), jnp.float32)
    for h in range(len(limits)):
        value = jnp.where(column < limits[h], rows(h, None) - pivot, 0.0)
        first = first + value
        second = second + value * value
    moved = first.sum(axis=0, keepdims=True)
    squares = second.sum(axis=0, keepdims=True) - moved * moved / jnp.maximum(count, 1.0)
    sums_ref[pl.ds(b, 1)] = moved + count * pivot
    squares_ref[pl.ds(b, 1)] = jnp.maximum(squares, 0.0)


def tile_position():
    lat = lax.axis_index("zh") * lax.axis_size("core") + lax.axis_index("core")
    lon = (lax.axis_index("y") * lax.axis_size("zl") + lax.axis_index("zl")) * lax.axis_size("x")
    return lat, lon + lax.axis_index("x")


def row_points(points_ref, lat, rows, e):
    row = lat * rows + e
    if 0 <= e < rows:
        return points_ref[row]
    total = points_ref.shape[0]
    inside = (row >= 0) & (row < total)
    return jnp.where(inside, points_ref[jnp.clip(row, 0, total - 1)], 0)


def live_limits(points_ref, rows, cols):
    lat, lon = tile_position()
    return [jnp.clip(points_ref[lat * rows + h] - lon * cols, 0, cols) for h in range(rows)]


def live_count(limits):
    return functools.reduce(lambda a, c: a + c, limits).astype(jnp.float32)


def in_vmem():
    return pl.BlockSpec(memory_space=pltpu.VMEM)


def fetch(x_hbm_ref, x_ref, sems, b):
    return pltpu.make_async_copy(x_hbm_ref.at[b], x_ref.at[b], sems.at[b])


def pack_edges(x_ref, b, d, edges, k):
    _, rows, cols, _ = x_ref.shape
    first_row_ref, last_row_ref, first_col_ref, last_col_ref = edges
    first_row_ref[k] = x_ref[b, :d]
    last_row_ref[k] = x_ref[b, rows - d :]
    for h in range(rows):
        first_col_ref[k, h * d : (h + 1) * d] = x_ref[b, h, :d]
        last_col_ref[k, h * d : (h + 1) * d] = x_ref[b, h, cols - d :]


def edge_shapes(x, d):
    samples, rows, width, channels = x.shape
    shapes = [(samples, d, width, channels)] * 2 + [(samples, rows * d, channels)] * 2
    return [jax.ShapeDtypeStruct(shape, x.dtype) for shape in shapes]


def edge_specs(x, d, block):
    return [
        pl.BlockSpec((block, *e.shape[1:]), lambda g, *_, n=len(e.shape): (g,) + (0,) * (n - 1))
        for e in edge_shapes(x, d)
    ]


def stats_kernel(points_ref, x_hbm_ref, out_ref, *refs):
    *edges, x_ref, sems, sums_ref, squares_ref = refs
    g = pl.program_id(0)

    @pl.when(g == 0)
    def _():
        for b in range(x_ref.shape[0]):
            fetch(x_hbm_ref, x_ref, sems, b).start()

    fetch(x_hbm_ref, x_ref, sems, g).wait()
    _, rows, cols, _ = x_ref.shape
    limits = live_limits(points_ref, rows, cols)
    count = live_count(limits)
    row_statistics(
        lambda h, n: x_ref[g, h, :n].astype(jnp.float32), limits, count, sums_ref, squares_ref, g
    )
    pack_edges(x_ref, g, FIRST_DILATION, edges, 0)

    @pl.when(g == pl.num_programs(0) - 1)
    def _():
        store_group_stats(sums_ref, squares_ref, count, out_ref)


def local_statistics(x, points):
    samples, rows, width, channels = x.shape
    shape = (3, samples * GROUPS // LANES, LANES)
    return pl.pallas_call(
        stats_kernel,
        out_shape=[jax.ShapeDtypeStruct(shape, jnp.float32), *edge_shapes(x, FIRST_DILATION)],
        grid_spec=pltpu.PrefetchScalarGridSpec(
            num_scalar_prefetch=1,
            grid=(samples,),
            in_specs=[pl.BlockSpec(memory_space=pltpu.HBM)],
            out_specs=[
                pl.BlockSpec(shape, lambda g, *_: (0, 0, 0)),
                *edge_specs(x, FIRST_DILATION, 1),
            ],
            scratch_shapes=[
                pltpu.VMEM(x.shape, x.dtype),
                pltpu.SemaphoreType.DMA((samples,)),
                pltpu.VMEM((samples, channels), jnp.float32),
                pltpu.VMEM((samples, channels), jnp.float32),
            ],
        ),
        compiler_params=pltpu.CompilerParams(
            dimension_semantics=("arbitrary",), vmem_limit_bytes=58_000_000
        ),
        cost_estimate=pl.CostEstimate(
            flops=8 * x.size, bytes_accessed=2 * x.size, transcendentals=0
        ),
        name="stats",
    )(points, x)


def chip_counts(points, chips, rows, cols, size):
    total = points.shape[1]
    lons = chips // lax.axis_size("zh")
    chip = lax.broadcasted_iota(jnp.int32, (chips, total), 0)
    row = lax.broadcasted_iota(jnp.int32, (chips, total), 1)
    live = jnp.clip(points - (chip % lons) * cols, 0, cols)
    mine = row // (rows * lax.axis_size("core")) == chip // lons
    return jnp.where(mine, live, 0).astype(jnp.float32).sum(axis=1, keepdims=True) * size


def combine_kernel(rows, cols, parts_ref, points_ref, norm_ref):
    _, samples, channels = norm_ref.shape
    slots = LANES // GROUPS
    chips = parts_ref.shape[0]
    counts = chip_counts(points_ref[...], chips, rows, cols, channels // GROUPS)[:, None, :]
    sums = parts_ref[:, 0]
    squares = parts_ref[:, 1]
    count = counts.sum(axis=0)
    mean = sums.sum(axis=0) / count
    offset = sums / jnp.maximum(counts, 1.0) - mean[None]
    var = (squares + counts * offset * offset).sum(axis=0) / count
    half = 0.5 * lax.rsqrt(var + EPS)
    own = slot_lanes(samples)
    spread = selection_matrix((LANES, channels), 1, channels)

    def unpacked(value):
        rows = jnp.broadcast_to(value[:, None], (samples // slots, slots, LANES)).reshape(samples, LANES)
        return jnp.where(own, rows, 0.0)

    both = exact_dot(jnp.concatenate([unpacked(mean), unpacked(half)], axis=0), spread)
    norm_ref[0] = both[:samples]
    norm_ref[1] = both[samples:]


def combine_statistics(parts, points, x):
    samples, rows, cols, channels = x.shape
    return pl.pallas_call(
        functools.partial(combine_kernel, rows, cols),
        out_shape=jax.ShapeDtypeStruct((2, samples, channels), jnp.float32),
        in_specs=[in_vmem(), in_vmem()],
        out_specs=in_vmem(),
        compiler_params=pltpu.CompilerParams(vmem_limit_bytes=4_000_000),
        cost_estimate=pl.CostEstimate(flops=NORM_FLOPS, bytes_accessed=parts.size * 4, transcendentals=0),
        name="norm",
    )(parts, points[None])


def conv_kernel(dilation, chunk, which, with_stats, points_ref, flags_ref, norm_ref, *refs):
    d = dilation
    x_hbm_ref, top_ref, bottom_ref, left_ref, right_ref, w_ref, out_hbm_ref, *rest = refs
    if with_stats:
        stats_ref, *edges = rest[:5]
        x_ref, sems, out_ref, out_sems, even_ref, odd_ref, sums_ref, squares_ref, kept_ref = rest[5:]
    else:
        x_ref, sems, out_ref, out_sems, even_ref, odd_ref = rest
    g = pl.program_id(0)
    samples = norm_ref.shape[1]
    _, rows, cols, channels = x_ref.shape
    lat, lon = tile_position()
    lon_total = lax.axis_size(LON) * cols
    origin = lon * cols
    column = lax.broadcasted_iota(jnp.int32, (cols, channels), 0)
    edge = lax.broadcasted_iota(jnp.int32, (d, channels), 0)
    points = [row_points(points_ref, lat, rows, e - d) for e in range(rows + 2 * d)]
    limits = [jnp.clip(points[d + h] - origin, 0, cols) for h in range(rows)]
    before_origin = (origin + lon_total - d) % lon_total
    after_origin = (origin + cols) % lon_total

    def activate_rows(b, act_ref, lo, hi):
        mean = norm_ref[0, pl.ds(b, 1)]
        half = norm_ref[1, pl.ds(b, 1)]

        def activated(value):
            t = (value.astype(jnp.float32) - mean) * half
            return t + t * jnp.tanh(t)

        left = activated(left_ref[b, lo * d : hi * d])
        right = activated(right_ref[b, lo * d : hi * d])
        for e in range(lo, hi):
            if e < d:
                row = top_ref[b, e]
            elif e < rows + d:
                row = x_ref[b, e - d]
            else:
                row = bottom_ref[b, e - rows - d]
            at = slice((e - lo) * d, (e - lo + 1) * d)
            mid = jnp.where(column < points[e] - origin, activated(row), 0.0).astype(jnp.bfloat16)
            lhs = jnp.where(edge < points[e] - before_origin, left[at], 0.0).astype(jnp.bfloat16)
            rhs = jnp.where(edge < points[e] - after_origin, right[at], 0.0).astype(jnp.bfloat16)
            act_ref[e, d:, 0:channels] = mid[: cols - d]
            act_ref[e, :d, 0:channels] = lhs
            act_ref[e, :, channels : 2 * channels] = mid
            act_ref[e, : cols - d, 2 * channels :] = mid[d:]
            act_ref[e, cols - d :, 2 * channels :] = rhs

    def convolve_rows(k, scale, act_ref, start):
        acc = None
        for tap in range(3):
            lo = start + tap * d
            taken = act_ref[lo : lo + chunk].reshape(chunk * cols, 3 * channels)
            term = jnp.dot(taken, w_ref[tap], preferred_element_type=jnp.float32)
            acc = term if acc is None else acc + term
        base = x_ref[2 * g + k, start : start + chunk].astype(jnp.float32)
        result = (base + scale * acc.reshape(chunk, cols, channels)).astype(jnp.bfloat16)
        out_ref[2 * g + k, start : start + chunk] = result
        if with_stats and k == 1:
            kept_ref[start : start + chunk] = result

    def phase(k, act_ref, follow, next_ref):
        scale = flags_ref[which, 2 * g + k].astype(jnp.float32) * (1.0 / KEEP_RATE)
        steps = rows // chunk
        each = (rows + 2 * d) // steps
        for step in range(steps):
            last = rows + 2 * d if step == steps - 1 else (step + 1) * each
            activate_rows(follow, next_ref, step * each, last)
            convolve_rows(k, scale, act_ref, step * chunk)
        store(2 * g + k).start()
        if with_stats:
            pack_edges(out_ref, 2 * g + k, SECOND_DILATION, edges, k)

    def store(b):
        return pltpu.make_async_copy(out_ref.at[b], out_hbm_ref.at[b], out_sems.at[b])

    @pl.when(g == 0)
    def _():
        for b in range(samples):
            fetch(x_hbm_ref, x_ref, sems, b).start()
        fetch(x_hbm_ref, x_ref, sems, 0).wait()
        activate_rows(0, even_ref, 0, rows + 2 * d)
        if with_stats:
            kept_ref[...] = jnp.zeros_like(kept_ref)

    @pl.when(g < samples // 2 - 1)
    def _():
        fetch(x_hbm_ref, x_ref, sems, 2 * g + 2).wait()

    fetch(x_hbm_ref, x_ref, sems, 2 * g + 1).wait()
    count = live_count(limits)
    phase(0, even_ref, 2 * g + 1, odd_ref)
    if with_stats:
        row_statistics(
            lambda h, n: kept_ref[h, :n].astype(jnp.float32), limits, count, sums_ref, squares_ref, jnp.maximum(2 * g - 1, 0)
        )
    phase(1, odd_ref, jnp.minimum(2 * g + 2, samples - 1), even_ref)
    if with_stats:
        row_statistics(
            lambda h, n: out_ref[2 * g, h, :n].astype(jnp.float32), limits, count, sums_ref, squares_ref, 2 * g
        )

        @pl.when(g == pl.num_programs(0) - 1)
        def _():
            row_statistics(
                lambda h, n: out_ref[2 * g + 1, h, :n].astype(jnp.float32), limits, count, sums_ref, squares_ref, samples - 1
            )
            store_group_stats(sums_ref, squares_ref, count, stats_ref)

    @pl.when(g == pl.num_programs(0) - 1)
    def _():
        for b in range(samples):
            store(b).wait()


def convolve(x, halos, weight, norm, points, flags, dilation, which, with_stats):
    samples, rows, width, channels = x.shape
    d = dilation
    def whole(shape):
        return pl.BlockSpec(shape, lambda g, *_: (0,) * len(shape))

    out_shape = [jax.ShapeDtypeStruct(x.shape, jnp.bfloat16)]
    out_specs = [pl.BlockSpec(memory_space=pltpu.HBM)]
    act = pltpu.VMEM((rows + 2 * d, width, 3 * channels), jnp.bfloat16)
    scratch = [pltpu.VMEM(x.shape, x.dtype), pltpu.SemaphoreType.DMA((samples,))] * 2
    scratch += [act, act]
    if with_stats:
        shape = (3, samples * GROUPS // LANES, LANES)
        out_shape += [jax.ShapeDtypeStruct(shape, jnp.float32), *edge_shapes(x, SECOND_DILATION)]
        out_specs += [whole(shape), *edge_specs(x, SECOND_DILATION, 2)]
        scratch += [pltpu.VMEM((samples, channels), jnp.float32)] * 2
        scratch += [pltpu.VMEM((rows, width, channels), jnp.bfloat16)]
    return pl.pallas_call(
        functools.partial(conv_kernel, d, CHUNK, which, with_stats),
        out_shape=out_shape,
        grid_spec=pltpu.PrefetchScalarGridSpec(
            num_scalar_prefetch=2,
            grid=(samples // 2,),
            in_specs=[
                in_vmem(),
                pl.BlockSpec(memory_space=pltpu.HBM),
                *[in_vmem()] * len(halos),
                in_vmem(),
            ],
            out_specs=out_specs,
            scratch_shapes=scratch,
        ),
        compiler_params=pltpu.CompilerParams(
            dimension_semantics=("arbitrary",), vmem_limit_bytes=VMEM_LIMIT
        ),
        cost_estimate=pl.CostEstimate(
            flops=2 * x.size * 9 * channels, bytes_accessed=5 * x.size, transcendentals=2 * x.size
        ),
        name="conv%d" % d,
    )(points, flags, norm, x, *halos, weight)


def exchange_rows(edges):
    lat = lax.axis_size(LAT)
    top = lax.ppermute(edges[1], LAT, [(i, i + 1) for i in range(lat - 1)])
    bottom = lax.ppermute(edges[0], LAT, [(i + 1, i) for i in range(lat - 1)])
    return top, bottom


def pack_kernel(top_ref, bottom_ref, first_ref, last_ref, east_ref, west_ref):
    samples, d, width, _ = top_ref.shape
    rows = first_ref.shape[1] // d
    for cols_ref, out_ref, lo in ((last_ref, east_ref, width - d), (first_ref, west_ref, 0)):
        for b in range(samples):
            for e in range(d):
                out_ref[b, e * d : (e + 1) * d] = top_ref[b, e, lo : lo + d]
                below = (rows + d + e) * d
                out_ref[b, below : below + d] = bottom_ref[b, e, lo : lo + d]
            out_ref[b, d * d : (rows + d) * d] = cols_ref[b]


def exchange_columns(edges, top, bottom):
    samples, d, width, channels = top.shape
    lon = lax.axis_size(LON)
    first_col, last_col = edges[2:]
    shape = (samples, first_col.shape[1] + 2 * d * d, channels)
    east, west = pl.pallas_call(
        pack_kernel,
        out_shape=[jax.ShapeDtypeStruct(shape, top.dtype)] * 2,
        in_specs=[in_vmem()] * 4,
        out_specs=[in_vmem()] * 2,
        compiler_params=pltpu.CompilerParams(vmem_limit_bytes=8_000_000),
        cost_estimate=pl.CostEstimate(flops=0, bytes_accessed=4 * first_col.size, transcendentals=0),
        name="pack",
    )(top, bottom, first_col, last_col)
    left = lax.ppermute(east, LON, [(i, (i + 1) % lon) for i in range(lon)])
    right = lax.ppermute(west, LON, [((i + 1) % lon, i) for i in range(lon)])
    return left, right


def merge_kernel(local_ref, other_ref, out_ref):
    sums, other_sums = local_ref[0], other_ref[0]
    count, other_count = local_ref[2], other_ref[2]
    both = jnp.maximum(count + other_count, 1.0)
    gap = sums / jnp.maximum(count, 1.0) - other_sums / jnp.maximum(other_count, 1.0)
    squares = local_ref[1] + other_ref[1] + gap * gap * (count * other_count / both)
    out_ref[:, 0] = jnp.broadcast_to((sums + other_sums)[None], out_ref[:, 0].shape)
    out_ref[:, 1] = jnp.broadcast_to(squares[None], out_ref[:, 1].shape)


def merge_cores(local):
    other = lax.ppermute(local, "core", [(0, 1), (1, 0)])
    shape = (lax.axis_size(CHIPS), 2, *local.shape[1:])
    return pl.pallas_call(
        merge_kernel,
        out_shape=jax.ShapeDtypeStruct(shape, jnp.float32),
        in_specs=[in_vmem()] * 2,
        out_specs=in_vmem(),
        compiler_params=pltpu.CompilerParams(vmem_limit_bytes=4_000_000),
        cost_estimate=pl.CostEstimate(flops=10 * local.size, bytes_accessed=4 * local.size, transcendentals=0),
        name="merge",
    )(local, other)


def exchange(local, edges, points, x):
    mine = merge_cores(local)
    top, bottom = exchange_rows(edges)
    norm = combine_statistics(lax.all_to_all(mine, CHIPS, 0, 0), points, x)
    return norm, (top, bottom, *exchange_columns(edges, top, bottom))


def per_device(features, band_points, survival_flags, first_kernel_weight, second_kernel_weight):
    channels = features.shape[3]
    flags = survival_flags.T
    first_weight = first_kernel_weight.reshape(3, 3 * channels, channels)
    second_weight = second_kernel_weight.reshape(3, 3 * channels, channels)
    local, *edges = local_statistics(features, band_points)
    norm, halos = exchange(local, edges, band_points, features)
    first, local, *edges = convolve(
        features, halos, first_weight, norm, band_points, flags, FIRST_DILATION, 0, True
    )
    norm, halos = exchange(local, edges, band_points, first)
    (section,) = convolve(
        first, halos, second_weight, norm, band_points, flags, SECOND_DILATION, 1, False
    )
    return section


def solution(mesh):
    grid = Mesh(mesh.devices.reshape(2, 2, 4, 2, 4), (LAT + LON))
    spec = P(None, LAT, LON, None)
    return jax.shard_map(
        per_device, mesh=grid, in_specs=(spec, P(), P(), P(), P()), out_specs=spec, check_vma=False
    )
```

```python
import functools

import jax
import jax.numpy as jnp
from jax import lax
from jax.experimental import pallas as pl
from jax.experimental.pallas import tpu as pltpu
from jax.sharding import Mesh, PartitionSpec as P

GROUPS = 32
FIRST_DILATION = 2
SECOND_DILATION = 4
EPS = 1e-05
KEEP_RATE = 0.8

LAT = ("zh", "core")
LON = ("y", "zl", "x")
CHIPS = ("zh", "y", "zl", "x")
LANES = 128
VMEM_LIMIT = 52_000_000
CHUNK = 8


def exact_dot(a, selection):
    high = a.astype(jnp.bfloat16)
    rest = a - high.astype(jnp.float32)
    middle = rest.astype(jnp.bfloat16)
    low = (rest - middle.astype(jnp.float32)).astype(jnp.bfloat16)
    m = a.shape[0]
    parts = jnp.concatenate([high.astype(jnp.float32), middle.astype(jnp.float32), low.astype(jnp.float32)], axis=0)
    terms = jnp.dot(parts.astype(jnp.bfloat16), selection, preferred_element_type=jnp.float32)
    return terms[:m] + terms[m : 2 * m] + terms[2 * m :]


def selection_matrix(shape, channel_dim, channels):
    size = channels // GROUPS
    channel = lax.broadcasted_iota(jnp.int32, shape, channel_dim)
    lane = lax.broadcasted_iota(jnp.int32, shape, 1 - channel_dim)
    return jnp.where(channel // size == lane % GROUPS, 1.0, 0.0).astype(jnp.bfloat16)


def slot_lanes(samples):
    row = lax.broadcasted_iota(jnp.int32, (samples, LANES), 0)
    lane = lax.broadcasted_iota(jnp.int32, (samples, LANES), 1)
    return lane // GROUPS == row % (LANES // GROUPS)


def store_group_stats(sums_ref, squares_ref, count, out_ref):
    samples, channels = sums_ref.shape
    slots = LANES // GROUPS
    size = channels // GROUPS
    own = slot_lanes(samples)
    fold = selection_matrix((channels, LANES), 0, channels)
    spread = selection_matrix((LANES, channels), 1, channels)
    per_channel = jnp.maximum(count, 1.0)
    sums = sums_ref[...]

    def packed(value):
        return jnp.where(own, value, 0.0).reshape(samples // slots, slots, LANES).sum(axis=1)

    group_sum = exact_dot(sums, fold)
    centre = exact_dot(jnp.where(own, group_sum, 0.0), spread) / (per_channel * size)
    offset = sums / per_channel - centre
    group_squares = exact_dot(squares_ref[...] + count * offset * offset, fold)
    out_ref[0] = packed(group_sum)
    out_ref[1] = packed(group_squares)
    out_ref[2] = jnp.full(out_ref.shape[1:], count * size, jnp.float32)


def row_statistics(rows, limits, count, sums_ref, squares_ref, b):
    some = 16
    cols, channels = rows(0, None).shape
    column = lax.broadcasted_iota(jnp.int32, (cols, channels), 0)
    few = sum(jnp.minimum(limit, some) for limit in limits).astype(jnp.float32)
    total = jnp.zeros((some, channels), jnp.float32)
    for h in range(len(limits)):
        total = total + jnp.where(column[:some] < limits[h], rows(h, some), 0.0)
    pivot = total.sum(axis=0, keepdims=True) / jnp.maximum(few, 1.0)
    first = jnp.zeros((cols, channels), jnp.float32)
    second = jnp.zeros((cols, channels), jnp.float32)
    for h in range(len(limits)):
        value = jnp.where(column < limits[h], rows(h, None) - pivot, 0.0)
        first = first + value
        second = second + value * value
    moved = first.sum(axis=0, keepdims=True)
    squares = second.sum(axis=0, keepdims=True) - moved * moved / jnp.maximum(count, 1.0)
    sums_ref[pl.ds(b, 1)] = moved + count * pivot
    squares_ref[pl.ds(b, 1)] = jnp.maximum(squares, 0.0)


def tile_position():
    lat = lax.axis_index("zh") * lax.axis_size("core") + lax.axis_index("core")
    lon = (lax.axis_index("y") * lax.axis_size("zl") + lax.axis_index("zl")) * lax.axis_size("x")
    return lat, lon + lax.axis_index("x")


def row_points(points_ref, lat, rows, e):
    row = lat * rows + e
    if 0 <= e < rows:
        return points_ref[row]
    total = points_ref.shape[0]
    inside = (row >= 0) & (row < total)
    return jnp.where(inside, points_ref[jnp.clip(row, 0, total - 1)], 0)


def live_limits(points_ref, rows, cols):
    lat, lon = tile_position()
    return [jnp.clip(points_ref[lat * rows + h] - lon * cols, 0, cols) for h in range(rows)]


def live_count(limits):
    return functools.reduce(lambda a, c: a + c, limits).astype(jnp.float32)


def in_vmem():
    return pl.BlockSpec(memory_space=pltpu.VMEM)


def fetch(x_hbm_ref, x_ref, sems, b):
    return pltpu.make_async_copy(x_hbm_ref.at[b], x_ref.at[b], sems.at[b])


def pack_edges(x_ref, b, d, edges, k):
    _, rows, cols, _ = x_ref.shape
    first_row_ref, last_row_ref, first_col_ref, last_col_ref = edges
    first_row_ref[k] = x_ref[b, :d]
    last_row_ref[k] = x_ref[b, rows - d :]
    for h in range(rows):
        first_col_ref[k, h * d : (h + 1) * d] = x_ref[b, h, :d]
        last_col_ref[k, h * d : (h + 1) * d] = x_ref[b, h, cols - d :]


def edge_shapes(x, d):
    samples, rows, width, channels = x.shape
    shapes = [(samples, d, width, channels)] * 2 + [(samples, rows * d, channels)] * 2
    return [jax.ShapeDtypeStruct(shape, x.dtype) for shape in shapes]


def edge_specs(x, d, block):
    return [
        pl.BlockSpec((block, *e.shape[1:]), lambda g, *_, n=len(e.shape): (g,) + (0,) * (n - 1))
        for e in edge_shapes(x, d)
    ]


def stats_kernel(points_ref, x_hbm_ref, out_ref, *refs):
    *edges, x_ref, sems, sums_ref, squares_ref = refs
    g = pl.program_id(0)

    @pl.when(g == 0)
    def _():
        for b in range(x_ref.shape[0]):
            fetch(x_hbm_ref, x_ref, sems, b).start()

    fetch(x_hbm_ref, x_ref, sems, g).wait()
    _, rows, cols, _ = x_ref.shape
    limits = live_limits(points_ref, rows, cols)
    count = live_count(limits)
    row_statistics(
        lambda h, n: x_ref[g, h, :n].astype(jnp.float32), limits, count, sums_ref, squares_ref, g
    )
    pack_edges(x_ref, g, FIRST_DILATION, edges, 0)

    @pl.when(g == pl.num_programs(0) - 1)
    def _():
        store_group_stats(sums_ref, squares_ref, count, out_ref)


def local_statistics(x, points):
    samples, rows, width, channels = x.shape
    shape = (3, samples * GROUPS // LANES, LANES)
    return pl.pallas_call(
        stats_kernel,
        out_shape=[jax.ShapeDtypeStruct(shape, jnp.float32), *edge_shapes(x, FIRST_DILATION)],
        grid_spec=pltpu.PrefetchScalarGridSpec(
            num_scalar_prefetch=1,
            grid=(samples,),
            in_specs=[pl.BlockSpec(memory_space=pltpu.HBM)],
            out_specs=[
                pl.BlockSpec(shape, lambda g, *_: (0, 0, 0)),
                *edge_specs(x, FIRST_DILATION, 1),
            ],
            scratch_shapes=[
                pltpu.VMEM(x.shape, x.dtype),
                pltpu.SemaphoreType.DMA((samples,)),
                pltpu.VMEM((samples, channels), jnp.float32),
                pltpu.VMEM((samples, channels), jnp.float32),
            ],
        ),
        compiler_params=pltpu.CompilerParams(
            dimension_semantics=("arbitrary",), vmem_limit_bytes=58_000_000
        ),
        cost_estimate=pl.CostEstimate(
            flops=8 * x.size, bytes_accessed=2 * x.size, transcendentals=0
        ),
        name="stats",
    )(points, x)


def chip_counts(points, chips, rows, cols, size):
    total = points.shape[1]
    lons = chips // lax.axis_size("zh")
    chip = lax.broadcasted_iota(jnp.int32, (chips, total), 0)
    row = lax.broadcasted_iota(jnp.int32, (chips, total), 1)
    live = jnp.clip(points - (chip % lons) * cols, 0, cols)
    mine = row // (rows * lax.axis_size("core")) == chip // lons
    return jnp.where(mine, live, 0).astype(jnp.float32).sum(axis=1, keepdims=True) * size


def combine_kernel(rows, cols, parts_ref, points_ref, norm_ref):
    _, samples, channels = norm_ref.shape
    slots = LANES // GROUPS
    chips = parts_ref.shape[0]
    counts = chip_counts(points_ref[...], chips, rows, cols, channels // GROUPS)[:, None, :]
    sums = parts_ref[:, 0]
    squares = parts_ref[:, 1]
    count = counts.sum(axis=0)
    mean = sums.sum(axis=0) / count
    offset = sums / jnp.maximum(counts, 1.0) - mean[None]
    var = (squares + counts * offset * offset).sum(axis=0) / count
    half = 0.5 * lax.rsqrt(var + EPS)
    own = slot_lanes(samples)
    spread = selection_matrix((LANES, channels), 1, channels)

    def unpacked(value):
        rows = jnp.broadcast_to(value[:, None], (samples // slots, slots, LANES)).reshape(samples, LANES)
        return jnp.where(own, rows, 0.0)

    both = exact_dot(jnp.concatenate([unpacked(mean), unpacked(half)], axis=0), spread)
    norm_ref[0] = both[:samples]
    norm_ref[1] = both[samples:]


def combine_statistics(parts, points, x, flops):
    samples, rows, cols, channels = x.shape
    return pl.pallas_call(
        functools.partial(combine_kernel, rows, cols),
        out_shape=jax.ShapeDtypeStruct((2, samples, channels), jnp.float32),
        in_specs=[in_vmem(), in_vmem()],
        out_specs=in_vmem(),
        compiler_params=pltpu.CompilerParams(vmem_limit_bytes=4_000_000),
        cost_estimate=pl.CostEstimate(flops=flops, bytes_accessed=parts.size * 4, transcendentals=0),
        name="norm",
    )(parts, points[None])


def conv_kernel(dilation, chunk, which, with_stats, points_ref, flags_ref, norm_ref, *refs):
    d = dilation
    x_hbm_ref, top_ref, bottom_ref, left_ref, right_ref, w_ref, out_hbm_ref, *rest = refs
    if with_stats:
        stats_ref, *edges = rest[:5]
        x_ref, sems, out_ref, out_sems, even_ref, odd_ref, sums_ref, squares_ref, kept_ref = rest[5:]
    else:
        x_ref, sems, out_ref, out_sems, even_ref, odd_ref = rest
    g = pl.program_id(0)
    samples = norm_ref.shape[1]
    _, rows, cols, channels = x_ref.shape
    lat, lon = tile_position()
    lon_total = lax.axis_size(LON) * cols
    origin = lon * cols
    column = lax.broadcasted_iota(jnp.int32, (cols, channels), 0)
    edge = lax.broadcasted_iota(jnp.int32, (d, channels), 0)
    points = [row_points(points_ref, lat, rows, e - d) for e in range(rows + 2 * d)]
    limits = [jnp.clip(points[d + h] - origin, 0, cols) for h in range(rows)]
    before_origin = (origin + lon_total - d) % lon_total
    after_origin = (origin + cols) % lon_total

    def activate_rows(b, act_ref, lo, hi):
        mean = norm_ref[0, pl.ds(b, 1)]
        half = norm_ref[1, pl.ds(b, 1)]

        def activated(value):
            t = (value.astype(jnp.float32) - mean) * half
            return t + t * jnp.tanh(t)

        left = activated(left_ref[b, lo * d : hi * d])
        right = activated(right_ref[b, lo * d : hi * d])
        for e in range(lo, hi):
            if e < d:
                row = top_ref[b, e]
            elif e < rows + d:
                row = x_ref[b, e - d]
            else:
                row = bottom_ref[b, e - rows - d]
            at = slice((e - lo) * d, (e - lo + 1) * d)
            mid = jnp.where(column < points[e] - origin, activated(row), 0.0).astype(jnp.bfloat16)
            lhs = jnp.where(edge < points[e] - before_origin, left[at], 0.0).astype(jnp.bfloat16)
            rhs = jnp.where(edge < points[e] - after_origin, right[at], 0.0).astype(jnp.bfloat16)
            act_ref[e, d:, 0:channels] = mid[: cols - d]
            act_ref[e, :d, 0:channels] = lhs
            act_ref[e, :, channels : 2 * channels] = mid
            act_ref[e, : cols - d, 2 * channels :] = mid[d:]
            act_ref[e, cols - d :, 2 * channels :] = rhs

    def convolve_rows(k, scale, act_ref, start):
        acc = None
        for tap in range(3):
            lo = start + tap * d
            taken = act_ref[lo : lo + chunk].reshape(chunk * cols, 3 * channels)
            term = jnp.dot(taken, w_ref[tap], preferred_element_type=jnp.float32)
            acc = term if acc is None else acc + term
        base = x_ref[2 * g + k, start : start + chunk].astype(jnp.float32)
        result = (base + scale * acc.reshape(chunk, cols, channels)).astype(jnp.bfloat16)
        out_ref[2 * g + k, start : start + chunk] = result
        if with_stats and k == 1:
            kept_ref[start : start + chunk] = result

    def phase(k, act_ref, follow, next_ref):
        scale = flags_ref[which, 2 * g + k].astype(jnp.float32) * (1.0 / KEEP_RATE)
        steps = rows // chunk
        each = (rows + 2 * d) // steps
        for step in range(steps):
            last = rows + 2 * d if step == steps - 1 else (step + 1) * each
            activate_rows(follow, next_ref, step * each, last)
            convolve_rows(k, scale, act_ref, step * chunk)
        store(2 * g + k).start()
        if with_stats:
            pack_edges(out_ref, 2 * g + k, SECOND_DILATION, edges, k)

    def store(b):
        return pltpu.make_async_copy(out_ref.at[b], out_hbm_ref.at[b], out_sems.at[b])

    @pl.when(g == 0)
    def _():
        for b in range(samples):
            fetch(x_hbm_ref, x_ref, sems, b).start()
        fetch(x_hbm_ref, x_ref, sems, 0).wait()
        activate_rows(0, even_ref, 0, rows + 2 * d)
        if with_stats:
            kept_ref[...] = jnp.zeros_like(kept_ref)

    @pl.when(g < samples // 2 - 1)
    def _():
        fetch(x_hbm_ref, x_ref, sems, 2 * g + 2).wait()

    fetch(x_hbm_ref, x_ref, sems, 2 * g + 1).wait()
    count = live_count(limits)
    phase(0, even_ref, 2 * g + 1, odd_ref)
    if with_stats:
        row_statistics(
            lambda h, n: kept_ref[h, :n].astype(jnp.float32), limits, count, sums_ref, squares_ref, jnp.maximum(2 * g - 1, 0)
        )
    phase(1, odd_ref, jnp.minimum(2 * g + 2, samples - 1), even_ref)
    if with_stats:
        row_statistics(
            lambda h, n: out_ref[2 * g, h, :n].astype(jnp.float32), limits, count, sums_ref, squares_ref, 2 * g
        )

        @pl.when(g == pl.num_programs(0) - 1)
        def _():
            row_statistics(
                lambda h, n: out_ref[2 * g + 1, h, :n].astype(jnp.float32), limits, count, sums_ref, squares_ref, samples - 1
            )
            store_group_stats(sums_ref, squares_ref, count, stats_ref)

    @pl.when(g == pl.num_programs(0) - 1)
    def _():
        for b in range(samples):
            store(b).wait()


def convolve(x, halos, weight, norm, points, flags, dilation, which, with_stats):
    samples, rows, width, channels = x.shape
    d = dilation
    def whole(shape):
        return pl.BlockSpec(shape, lambda g, *_: (0,) * len(shape))

    out_shape = [jax.ShapeDtypeStruct(x.shape, jnp.bfloat16)]
    out_specs = [pl.BlockSpec(memory_space=pltpu.HBM)]
    act = pltpu.VMEM((rows + 2 * d, width, 3 * channels), jnp.bfloat16)
    scratch = [pltpu.VMEM(x.shape, x.dtype), pltpu.SemaphoreType.DMA((samples,))] * 2
    scratch += [act, act]
    if with_stats:
        shape = (3, samples * GROUPS // LANES, LANES)
        out_shape += [jax.ShapeDtypeStruct(shape, jnp.float32), *edge_shapes(x, SECOND_DILATION)]
        out_specs += [whole(shape), *edge_specs(x, SECOND_DILATION, 2)]
        scratch += [pltpu.VMEM((samples, channels), jnp.float32)] * 2
        scratch += [pltpu.VMEM((rows, width, channels), jnp.bfloat16)]
    return pl.pallas_call(
        functools.partial(conv_kernel, d, CHUNK, which, with_stats),
        out_shape=out_shape,
        grid_spec=pltpu.PrefetchScalarGridSpec(
            num_scalar_prefetch=2,
            grid=(samples // 2,),
            in_specs=[
                in_vmem(),
                pl.BlockSpec(memory_space=pltpu.HBM),
                *[in_vmem()] * len(halos),
                in_vmem(),
            ],
            out_specs=out_specs,
            scratch_shapes=scratch,
        ),
        compiler_params=pltpu.CompilerParams(
            dimension_semantics=("arbitrary",), vmem_limit_bytes=VMEM_LIMIT
        ),
        cost_estimate=pl.CostEstimate(
            flops=2 * x.size * 9 * channels, bytes_accessed=5 * x.size, transcendentals=2 * x.size
        ),
        name="conv%d" % d,
    )(points, flags, norm, x, *halos, weight)


def exchange_rows(edges):
    lat = lax.axis_size(LAT)
    top = lax.ppermute(edges[1], LAT, [(i, i + 1) for i in range(lat - 1)])
    bottom = lax.ppermute(edges[0], LAT, [(i + 1, i) for i in range(lat - 1)])
    return top, bottom


def exchange_columns(edges, top, bottom):
    samples, d, width, channels = top.shape
    lon = lax.axis_size(LON)

    def packed(cols, lo, hi):
        above = top[:, :, lo:hi].reshape(samples, d * d, channels)
        below = bottom[:, :, lo:hi].reshape(samples, d * d, channels)
        return jnp.concatenate([above, cols, below], axis=1)

    left = lax.ppermute(packed(edges[3], width - d, width), LON, [(i, (i + 1) % lon) for i in range(lon)])
    right = lax.ppermute(packed(edges[2], 0, d), LON, [((i + 1) % lon, i) for i in range(lon)])
    return left, right


def merge_cores(local):
    other = lax.ppermute(local, "core", [(0, 1), (1, 0)])
    own_count, other_count = local[2], other[2]
    both = jnp.maximum(own_count + other_count, 1.0)
    gap = local[0] / jnp.maximum(own_count, 1.0) - other[0] / jnp.maximum(other_count, 1.0)
    squares = local[1] + other[1] + gap * gap * (own_count * other_count / both)
    merged = jnp.stack([local[0] + other[0], squares])
    return jnp.broadcast_to(merged[None], (lax.axis_size(CHIPS), *merged.shape))


def exchange_first(local, edges, points, x):
    mine = merge_cores(local)
    top, bottom = exchange_rows(edges)
    norm = combine_statistics(lax.all_to_all(mine, CHIPS, 0, 0), points, x, 10**10)
    return norm, (top, bottom, *exchange_columns(edges, top, bottom))


def hold_kernel(points_ref, mine_ref, out_ref):
    out_ref[...] = points_ref[...]


def hold(points, mine):
    return pl.pallas_call(
        hold_kernel,
        out_shape=jax.ShapeDtypeStruct((1, points.shape[0]), points.dtype),
        in_specs=[in_vmem(), pl.BlockSpec(memory_space=pltpu.HBM)],
        out_specs=in_vmem(),
        compiler_params=pltpu.CompilerParams(vmem_limit_bytes=4_000_000),
        cost_estimate=pl.CostEstimate(flops=10**8, bytes_accessed=4 * points.size, transcendentals=0),
        name="hold",
    )(points[None], mine)[0]


def exchange_second(local, edges, points, x):
    mine = merge_cores(local)
    mine, top, bottom = lax.optimization_barrier((mine, *exchange_rows(edges)))
    columns = exchange_columns(edges, top, bottom)
    norm = combine_statistics(lax.all_to_all(mine, CHIPS, 0, 0), points, x, 10**9)
    return norm, (top, bottom, *columns), hold(points, mine)


def per_device(features, band_points, survival_flags, first_kernel_weight, second_kernel_weight):
    channels = features.shape[3]
    flags = survival_flags.T
    first_weight = first_kernel_weight.reshape(3, 3 * channels, channels)
    second_weight = second_kernel_weight.reshape(3, 3 * channels, channels)
    local, *edges = local_statistics(features, band_points)
    norm, halos = exchange_first(local, edges, band_points, features)
    first, local, *edges = convolve(
        features, halos, first_weight, norm, band_points, flags, FIRST_DILATION, 0, True
    )
    norm, halos, points = exchange_second(local, edges, band_points, first)
    (section,) = convolve(
        first, halos, second_weight, norm, points, flags, SECOND_DILATION, 1, False
    )
    return section


def solution(mesh):
    grid = Mesh(mesh.devices.reshape(2, 2, 4, 2, 4), (LAT + LON))
    spec = P(None, LAT, LON, None)
    return jax.shard_map(
        per_device, mesh=grid, in_specs=(spec, P(), P(), P(), P()), out_specs=spec, check_vma=False
    )
```

```python
import functools

import jax
import jax.numpy as jnp
from jax import lax
from jax.experimental import pallas as pl
from jax.experimental.pallas import tpu as pltpu
from jax.sharding import Mesh, PartitionSpec as P

GROUPS = 32
FIRST_DILATION = 2
SECOND_DILATION = 4
EPS = 1e-05
KEEP_RATE = 0.8

LAT = ("zh", "core")
LON = ("y", "zl", "x")
CHIPS = ("zh", "y", "zl", "x")
LANES = 128
VMEM_LIMIT = 52_000_000
CHUNK = 8
NORM_FLOPS = 10 * 10**9


def exact_dot(a, selection):
    high = a.astype(jnp.bfloat16)
    rest = a - high.astype(jnp.float32)
    middle = rest.astype(jnp.bfloat16)
    low = (rest - middle.astype(jnp.float32)).astype(jnp.bfloat16)
    m = a.shape[0]
    parts = jnp.concatenate([high.astype(jnp.float32), middle.astype(jnp.float32), low.astype(jnp.float32)], axis=0)
    terms = jnp.dot(parts.astype(jnp.bfloat16), selection, preferred_element_type=jnp.float32)
    return terms[:m] + terms[m : 2 * m] + terms[2 * m :]


def selection_matrix(shape, channel_dim, channels):
    size = channels // GROUPS
    channel = lax.broadcasted_iota(jnp.int32, shape, channel_dim)
    lane = lax.broadcasted_iota(jnp.int32, shape, 1 - channel_dim)
    return jnp.where(channel // size == lane % GROUPS, 1.0, 0.0).astype(jnp.bfloat16)


def slot_lanes(samples):
    row = lax.broadcasted_iota(jnp.int32, (samples, LANES), 0)
    lane = lax.broadcasted_iota(jnp.int32, (samples, LANES), 1)
    return lane // GROUPS == row % (LANES // GROUPS)


def store_group_stats(sums_ref, squares_ref, count, out_ref):
    samples, channels = sums_ref.shape
    slots = LANES // GROUPS
    size = channels // GROUPS
    own = slot_lanes(samples)
    fold = selection_matrix((channels, LANES), 0, channels)
    spread = selection_matrix((LANES, channels), 1, channels)
    per_channel = jnp.maximum(count, 1.0)
    sums = sums_ref[...]

    def packed(value):
        return jnp.where(own, value, 0.0).reshape(samples // slots, slots, LANES).sum(axis=1)

    group_sum = exact_dot(sums, fold)
    centre = exact_dot(jnp.where(own, group_sum, 0.0), spread) / (per_channel * size)
    offset = sums / per_channel - centre
    group_squares = exact_dot(squares_ref[...] + count * offset * offset, fold)
    out_ref[0] = packed(group_sum)
    out_ref[1] = packed(group_squares)
    out_ref[2] = jnp.full(out_ref.shape[1:], count * size, jnp.float32)


def row_statistics(rows, limits, count, sums_ref, squares_ref, b):
    some = 16
    cols, channels = rows(0, None).shape
    column = lax.broadcasted_iota(jnp.int32, (cols, channels), 0)
    few = sum(jnp.minimum(limit, some) for limit in limits).astype(jnp.float32)
    total = jnp.zeros((some, channels), jnp.float32)
    for h in range(len(limits)):
        total = total + jnp.where(column[:some] < limits[h], rows(h, some), 0.0)
    pivot = total.sum(axis=0, keepdims=True) / jnp.maximum(few, 1.0)
    first = jnp.zeros((cols, channels), jnp.float32)
    second = jnp.zeros((cols, channels), jnp.float32)
    for h in range(len(limits)):
        value = jnp.where(column < limits[h], rows(h, None) - pivot, 0.0)
        first = first + value
        second = second + value * value
    moved = first.sum(axis=0, keepdims=True)
    squares = second.sum(axis=0, keepdims=True) - moved * moved / jnp.maximum(count, 1.0)
    sums_ref[pl.ds(b, 1)] = moved + count * pivot
    squares_ref[pl.ds(b, 1)] = jnp.maximum(squares, 0.0)


def tile_position():
    lat = lax.axis_index("zh") * lax.axis_size("core") + lax.axis_index("core")
    lon = (lax.axis_index("y") * lax.axis_size("zl") + lax.axis_index("zl")) * lax.axis_size("x")
    return lat, lon + lax.axis_index("x")


def row_points(points_ref, lat, rows, e):
    row = lat * rows + e
    if 0 <= e < rows:
        return points_ref[row]
    total = points_ref.shape[0]
    inside = (row >= 0) & (row < total)
    return jnp.where(inside, points_ref[jnp.clip(row, 0, total - 1)], 0)


def live_limits(points_ref, rows, cols):
    lat, lon = tile_position()
    return [jnp.clip(points_ref[lat * rows + h] - lon * cols, 0, cols) for h in range(rows)]


def live_count(limits):
    return functools.reduce(lambda a, c: a + c, limits).astype(jnp.float32)


def in_vmem():
    return pl.BlockSpec(memory_space=pltpu.VMEM)


def fetch(x_hbm_ref, x_ref, sems, b):
    return pltpu.make_async_copy(x_hbm_ref.at[b], x_ref.at[b], sems.at[b])


def pack_edges(x_ref, b, d, edges, k):
    _, rows, cols, _ = x_ref.shape
    first_row_ref, last_row_ref, first_col_ref, last_col_ref = edges
    first_row_ref[k] = x_ref[b, :d]
    last_row_ref[k] = x_ref[b, rows - d :]
    for h in range(rows):
        first_col_ref[k, h * d : (h + 1) * d] = x_ref[b, h, :d]
        last_col_ref[k, h * d : (h + 1) * d] = x_ref[b, h, cols - d :]


def edge_shapes(x, d):
    samples, rows, width, channels = x.shape
    shapes = [(samples, d, width, channels)] * 2 + [(samples, rows * d, channels)] * 2
    return [jax.ShapeDtypeStruct(shape, x.dtype) for shape in shapes]


def edge_specs(x, d, block):
    return [
        pl.BlockSpec((block, *e.shape[1:]), lambda g, *_, n=len(e.shape): (g,) + (0,) * (n - 1))
        for e in edge_shapes(x, d)
    ]


def stats_kernel(points_ref, x_hbm_ref, out_ref, *refs):
    *edges, x_ref, sems, sums_ref, squares_ref = refs
    g = pl.program_id(0)

    @pl.when(g == 0)
    def _():
        for b in range(x_ref.shape[0]):
            fetch(x_hbm_ref, x_ref, sems, b).start()

    fetch(x_hbm_ref, x_ref, sems, g).wait()
    _, rows, cols, _ = x_ref.shape
    limits = live_limits(points_ref, rows, cols)
    count = live_count(limits)
    row_statistics(
        lambda h, n: x_ref[g, h, :n].astype(jnp.float32), limits, count, sums_ref, squares_ref, g
    )
    pack_edges(x_ref, g, FIRST_DILATION, edges, 0)

    @pl.when(g == pl.num_programs(0) - 1)
    def _():
        store_group_stats(sums_ref, squares_ref, count, out_ref)


def local_statistics(x, points):
    samples, rows, width, channels = x.shape
    shape = (3, samples * GROUPS // LANES, LANES)
    return pl.pallas_call(
        stats_kernel,
        out_shape=[jax.ShapeDtypeStruct(shape, jnp.float32), *edge_shapes(x, FIRST_DILATION)],
        grid_spec=pltpu.PrefetchScalarGridSpec(
            num_scalar_prefetch=1,
            grid=(samples,),
            in_specs=[pl.BlockSpec(memory_space=pltpu.HBM)],
            out_specs=[
                pl.BlockSpec(shape, lambda g, *_: (0, 0, 0)),
                *edge_specs(x, FIRST_DILATION, 1),
            ],
            scratch_shapes=[
                pltpu.VMEM(x.shape, x.dtype),
                pltpu.SemaphoreType.DMA((samples,)),
                pltpu.VMEM((samples, channels), jnp.float32),
                pltpu.VMEM((samples, channels), jnp.float32),
            ],
        ),
        compiler_params=pltpu.CompilerParams(
            dimension_semantics=("arbitrary",), vmem_limit_bytes=58_000_000
        ),
        cost_estimate=pl.CostEstimate(
            flops=8 * x.size, bytes_accessed=2 * x.size, transcendentals=0
        ),
        name="stats",
    )(points, x)


def chip_counts(points, chips, rows, cols, size):
    total = points.shape[1]
    lons = chips // lax.axis_size("zh")
    chip = lax.broadcasted_iota(jnp.int32, (chips, total), 0)
    row = lax.broadcasted_iota(jnp.int32, (chips, total), 1)
    live = jnp.clip(points - (chip % lons) * cols, 0, cols)
    mine = row // (rows * lax.axis_size("core")) == chip // lons
    return jnp.where(mine, live, 0).astype(jnp.float32).sum(axis=1, keepdims=True) * size


def combine_kernel(rows, cols, parts_ref, points_ref, norm_ref):
    _, samples, channels = norm_ref.shape
    slots = LANES // GROUPS
    chips = parts_ref.shape[0]
    counts = chip_counts(points_ref[...], chips, rows, cols, channels // GROUPS)[:, None, :]
    sums = parts_ref[:, 0]
    squares = parts_ref[:, 1]
    count = counts.sum(axis=0)
    mean = sums.sum(axis=0) / count
    offset = sums / jnp.maximum(counts, 1.0) - mean[None]
    var = (squares + counts * offset * offset).sum(axis=0) / count
    half = 0.5 * lax.rsqrt(var + EPS)
    own = slot_lanes(samples)
    spread = selection_matrix((LANES, channels), 1, channels)

    def unpacked(value):
        rows = jnp.broadcast_to(value[:, None], (samples // slots, slots, LANES)).reshape(samples, LANES)
        return jnp.where(own, rows, 0.0)

    both = exact_dot(jnp.concatenate([unpacked(mean), unpacked(half)], axis=0), spread)
    norm_ref[0] = both[:samples]
    norm_ref[1] = both[samples:]


def combine_statistics(parts, points, x):
    samples, rows, cols, channels = x.shape
    return pl.pallas_call(
        functools.partial(combine_kernel, rows, cols),
        out_shape=jax.ShapeDtypeStruct((2, samples, channels), jnp.float32),
        in_specs=[in_vmem(), in_vmem()],
        out_specs=in_vmem(),
        compiler_params=pltpu.CompilerParams(vmem_limit_bytes=4_000_000),
        cost_estimate=pl.CostEstimate(flops=NORM_FLOPS, bytes_accessed=parts.size * 4, transcendentals=0),
        name="norm",
    )(parts, points[None])


def conv_kernel(dilation, chunk, which, with_stats, points_ref, flags_ref, norm_ref, *refs):
    d = dilation
    x_hbm_ref, top_ref, bottom_ref, left_ref, right_ref, w_ref, out_hbm_ref, *rest = refs
    if with_stats:
        stats_ref, *edges = rest[:5]
        x_ref, sems, out_ref, out_sems, even_ref, odd_ref, sums_ref, squares_ref, kept_ref = rest[5:]
    else:
        x_ref, sems, out_ref, out_sems, even_ref, odd_ref = rest
    g = pl.program_id(0)
    samples = norm_ref.shape[1]
    _, rows, cols, channels = x_ref.shape
    lat, lon = tile_position()
    lon_total = lax.axis_size(LON) * cols
    origin = lon * cols
    column = lax.broadcasted_iota(jnp.int32, (cols, channels), 0)
    edge = lax.broadcasted_iota(jnp.int32, (d, channels), 0)
    points = [row_points(points_ref, lat, rows, e - d) for e in range(rows + 2 * d)]
    limits = [jnp.clip(points[d + h] - origin, 0, cols) for h in range(rows)]
    before_origin = (origin + lon_total - d) % lon_total
    after_origin = (origin + cols) % lon_total

    def activate_rows(b, act_ref, lo, hi):
        mean = norm_ref[0, pl.ds(b, 1)]
        half = norm_ref[1, pl.ds(b, 1)]

        def activated(value):
            t = (value.astype(jnp.float32) - mean) * half
            return t + t * jnp.tanh(t)

        left = activated(left_ref[b, lo * d : hi * d])
        right = activated(right_ref[b, lo * d : hi * d])
        for e in range(lo, hi):
            if e < d:
                row = top_ref[b, e]
            elif e < rows + d:
                row = x_ref[b, e - d]
            else:
                row = bottom_ref[b, e - rows - d]
            at = slice((e - lo) * d, (e - lo + 1) * d)
            mid = jnp.where(column < points[e] - origin, activated(row), 0.0).astype(jnp.bfloat16)
            lhs = jnp.where(edge < points[e] - before_origin, left[at], 0.0).astype(jnp.bfloat16)
            rhs = jnp.where(edge < points[e] - after_origin, right[at], 0.0).astype(jnp.bfloat16)
            act_ref[e, d:, 0:channels] = mid[: cols - d]
            act_ref[e, :d, 0:channels] = lhs
            act_ref[e, :, channels : 2 * channels] = mid
            act_ref[e, : cols - d, 2 * channels :] = mid[d:]
            act_ref[e, cols - d :, 2 * channels :] = rhs

    def convolve_rows(k, scale, act_ref, start):
        acc = None
        for tap in range(3):
            lo = start + tap * d
            taken = act_ref[lo : lo + chunk].reshape(chunk * cols, 3 * channels)
            term = jnp.dot(taken, w_ref[tap], preferred_element_type=jnp.float32)
            acc = term if acc is None else acc + term
        base = x_ref[2 * g + k, start : start + chunk].astype(jnp.float32)
        result = (base + scale * acc.reshape(chunk, cols, channels)).astype(jnp.bfloat16)
        out_ref[2 * g + k, start : start + chunk] = result
        if with_stats and k == 1:
            kept_ref[start : start + chunk] = result

    def phase(k, act_ref, follow, next_ref):
        scale = flags_ref[which, 2 * g + k].astype(jnp.float32) * (1.0 / KEEP_RATE)
        steps = rows // chunk
        each = (rows + 2 * d) // steps
        for step in range(steps):
            last = rows + 2 * d if step == steps - 1 else (step + 1) * each
            activate_rows(follow, next_ref, step * each, last)
            convolve_rows(k, scale, act_ref, step * chunk)
        store(2 * g + k).start()
        if with_stats:
            pack_edges(out_ref, 2 * g + k, SECOND_DILATION, edges, k)

    def store(b):
        return pltpu.make_async_copy(out_ref.at[b], out_hbm_ref.at[b], out_sems.at[b])

    @pl.when(g == 0)
    def _():
        for b in range(samples):
            fetch(x_hbm_ref, x_ref, sems, b).start()
        fetch(x_hbm_ref, x_ref, sems, 0).wait()
        activate_rows(0, even_ref, 0, rows + 2 * d)
        if with_stats:
            kept_ref[...] = jnp.zeros_like(kept_ref)

    @pl.when(g < samples // 2 - 1)
    def _():
        fetch(x_hbm_ref, x_ref, sems, 2 * g + 2).wait()

    fetch(x_hbm_ref, x_ref, sems, 2 * g + 1).wait()
    count = live_count(limits)
    phase(0, even_ref, 2 * g + 1, odd_ref)
    if with_stats:
        row_statistics(
            lambda h, n: kept_ref[h, :n].astype(jnp.float32), limits, count, sums_ref, squares_ref, jnp.maximum(2 * g - 1, 0)
        )
    phase(1, odd_ref, jnp.minimum(2 * g + 2, samples - 1), even_ref)
    if with_stats:
        row_statistics(
            lambda h, n: out_ref[2 * g, h, :n].astype(jnp.float32), limits, count, sums_ref, squares_ref, 2 * g
        )

        @pl.when(g == pl.num_programs(0) - 1)
        def _():
            row_statistics(
                lambda h, n: out_ref[2 * g + 1, h, :n].astype(jnp.float32), limits, count, sums_ref, squares_ref, samples - 1
            )
            store_group_stats(sums_ref, squares_ref, count, stats_ref)

    @pl.when(g == pl.num_programs(0) - 1)
    def _():
        for b in range(samples):
            store(b).wait()


def convolve(x, halos, weight, norm, points, flags, dilation, which, with_stats):
    samples, rows, width, channels = x.shape
    d = dilation
    def whole(shape):
        return pl.BlockSpec(shape, lambda g, *_: (0,) * len(shape))

    out_shape = [jax.ShapeDtypeStruct(x.shape, jnp.bfloat16)]
    out_specs = [pl.BlockSpec(memory_space=pltpu.HBM)]
    act = pltpu.VMEM((rows + 2 * d, width, 3 * channels), jnp.bfloat16)
    scratch = [pltpu.VMEM(x.shape, x.dtype), pltpu.SemaphoreType.DMA((samples,))] * 2
    scratch += [act, act]
    if with_stats:
        shape = (3, samples * GROUPS // LANES, LANES)
        out_shape += [jax.ShapeDtypeStruct(shape, jnp.float32), *edge_shapes(x, SECOND_DILATION)]
        out_specs += [whole(shape), *edge_specs(x, SECOND_DILATION, 2)]
        scratch += [pltpu.VMEM((samples, channels), jnp.float32)] * 2
        scratch += [pltpu.VMEM((rows, width, channels), jnp.bfloat16)]
    return pl.pallas_call(
        functools.partial(conv_kernel, d, CHUNK, which, with_stats),
        out_shape=out_shape,
        grid_spec=pltpu.PrefetchScalarGridSpec(
            num_scalar_prefetch=2,
            grid=(samples // 2,),
            in_specs=[
                in_vmem(),
                pl.BlockSpec(memory_space=pltpu.HBM),
                *[in_vmem()] * len(halos),
                in_vmem(),
            ],
            out_specs=out_specs,
            scratch_shapes=scratch,
        ),
        compiler_params=pltpu.CompilerParams(
            dimension_semantics=("arbitrary",), vmem_limit_bytes=VMEM_LIMIT
        ),
        cost_estimate=pl.CostEstimate(
            flops=2 * x.size * 9 * channels, bytes_accessed=5 * x.size, transcendentals=2 * x.size
        ),
        name="conv%d" % d,
    )(points, flags, norm, x, *halos, weight)


def exchange_rows(edges):
    lat = lax.axis_size(LAT)
    top = lax.ppermute(edges[1], LAT, [(i, i + 1) for i in range(lat - 1)])
    bottom = lax.ppermute(edges[0], LAT, [(i + 1, i) for i in range(lat - 1)])
    return top, bottom


def exchange_columns(edges, top, bottom):
    samples, d, width, channels = top.shape
    lon = lax.axis_size(LON)

    def packed(cols, lo, hi):
        above = top[:, :, lo:hi].reshape(samples, d * d, channels)
        below = bottom[:, :, lo:hi].reshape(samples, d * d, channels)
        return jnp.concatenate([above, cols, below], axis=1)

    left = lax.ppermute(packed(edges[3], width - d, width), LON, [(i, (i + 1) % lon) for i in range(lon)])
    right = lax.ppermute(packed(edges[2], 0, d), LON, [((i + 1) % lon, i) for i in range(lon)])
    return left, right


def merge_cores(local, edges):
    other = lax.ppermute(local, "core", [(0, 1), (1, 0)])
    other, *edges = lax.optimization_barrier((other, *edges))
    own_count, other_count = local[2], other[2]
    both = jnp.maximum(own_count + other_count, 1.0)
    gap = local[0] / jnp.maximum(own_count, 1.0) - other[0] / jnp.maximum(other_count, 1.0)
    squares = local[1] + other[1] + gap * gap * (own_count * other_count / both)
    merged = jnp.stack([local[0] + other[0], squares])
    return jnp.broadcast_to(merged[None], (lax.axis_size(CHIPS), *merged.shape)), edges


def exchange(local, edges, points, x):
    mine, edges = merge_cores(local, edges)
    top, bottom = exchange_rows(edges)
    norm = combine_statistics(lax.all_to_all(mine, CHIPS, 0, 0), points, x)
    return norm, (top, bottom, *exchange_columns(edges, top, bottom))


def per_device(features, band_points, survival_flags, first_kernel_weight, second_kernel_weight):
    channels = features.shape[3]
    flags = survival_flags.T
    first_weight = first_kernel_weight.reshape(3, 3 * channels, channels)
    second_weight = second_kernel_weight.reshape(3, 3 * channels, channels)
    local, *edges = local_statistics(features, band_points)
    norm, halos = exchange(local, edges, band_points, features)
    first, local, *edges = convolve(
        features, halos, first_weight, norm, band_points, flags, FIRST_DILATION, 0, True
    )
    norm, halos = exchange(local, edges, band_points, first)
    (section,) = convolve(
        first, halos, second_weight, norm, band_points, flags, SECOND_DILATION, 1, False
    )
    return section


def solution(mesh):
    grid = Mesh(mesh.devices.reshape(2, 2, 4, 2, 4), (LAT + LON))
    spec = P(None, LAT, LON, None)
    return jax.shard_map(
        per_device, mesh=grid, in_specs=(spec, P(), P(), P(), P()), out_specs=spec, check_vma=False
    )
```
